32 devices in a mesh: dp: 4 (over z), ctx: 4 (over y, x), tensor: 2 (over core).
Axes of the slice: x: 2, y: 2, z: 4, core: 2. Of those that a mesh axis runs over, the one named last changes fastest.
Arguments:
- tokens: bfloat16 [12, 1024, 768], P('dp', 'ctx'), may hold values from -6 to 6
- segment_ids: int32 [12, 1024], P('dp', 'ctx'), may hold values from 0 to 3, never falling along the last dimension, each value on 1 to 512 neighbouring positions
- w_qkv: bfloat16 [3, 768, 768], P(None, None, 'tensor'), may hold values from -0.21875 to 0.21875
- w_out: bfloat16 [768, 768], P('tensor'), may hold values from -3 to 3
- w_up: bfloat16 [3072, 768], P('tensor'), may hold values from -0.21875 to 0.21875
- w_down: bfloat16 [3072, 768], P('tensor'), may hold values from -0.109375 to 0.109375
- norm_gain: float32 [2, 768], replicated, may hold values from 0.1 to 1.9
- norm_bias: float32 [2, 768], replicated, may hold values from -1.5 to 1.5
- grad_out: bfloat16 [12, 1024, 768], P('dp', 'ctx'), may hold values from -6 to 6
Outputs:
- out: bfloat16 [12, 1024, 768], P('dp', 'ctx')
- grad_tokens: float32 [12, 1024, 768], P('dp', 'ctx')
- grad_qkv: float32 [3, 768, 768], P(None, 'ctx', 'tensor')
- grad_w_out: float32 [768, 768], P('tensor', 'ctx')
- grad_up: float32 [3072, 768], P('tensor', 'ctx')
- grad_down: float32 [3072, 768], P('tensor', 'ctx')
- grad_gain: float32 [2, 768], P(None, 'ctx')
- grad_bias: float32 [2, 768], P(None, 'ctx')
The draws below stay inside these ranges and needn't reach their ends.
Inputs may be any that keep to these rules, and one draw needn't show every extreme that they name: `segment_ids`: documents are contiguous runs of equal ids that never fall along a sequence; each id names 1 to 512 tokens and one document has exactly 512.
All inputs are finite; a program needn't handle non-finite values.
Results may differ from the reference program's by a relative error of at most 0.02.
Values may be sent and summed in bfloat16 or wider, within the bound.
No kernel may reach another device: no remote copies, remote signals or barrier semaphores. Data moves between devices by JAX's collectives and lax.ppermute only.
A program may use at most 320 MiB of HBM per device.

```python
import math
import jax
import jax.numpy as jnp
import numpy as np
from jax import lax

D = 768
HEADS = 12
HEAD_DIM = 64
FF = 3072
LEN = 1024
SEQUENCES = 12


def level_of(key, shape, split, low, largest):
    def one(dim, parts):
        heights = jax.random.uniform(jax.random.fold_in(jax.random.fold_in(key, 6), dim), (parts,), jnp.float32, low / len(split), largest / len(split))
        return jnp.repeat(jnp.exp(heights), shape[dim] // parts).reshape((-1,) + (1,) * (len(shape) - dim - 1))

    level = one(*split[0])
    for cut in split[1:]:
        level = level * one(*cut)
    return level


def profile(number_of, total, limit, slope):
    loads = [(1 << 20) // math.isqrt(standing ** slope) + 1 for standing in range(2, number_of + 1)]
    surplus, given = total - limit - (number_of - 1), [1] * (number_of - 1)
    while surplus > 0:
        free = [i for i in range(number_of - 1) if given[i] < limit]
        mass, remaining = sum([loads[i] for i in free]), surplus
        for i in free:
            extra = min(limit - given[i], max(1, remaining * loads[i] // mass), surplus)
            given[i] = given[i] + extra
            surplus = surplus - extra
    return np.array([limit] + given)


def uneven_parts(key, count, total, reach, lean):
    if count == 2:
        one = jax.random.randint(key, (), max(1, total - reach), min(reach, total - 1) + 1)
        return jnp.stack([one, total - one])
    sizes = jnp.asarray(profile(count, total, reach, lean), jnp.int32)
    twos = (count - 1) // 2
    donor, receiver = sizes[1:1 + 2 * twos:2], sizes[2:2 + 2 * twos:2]
    room = jnp.minimum(donor - 1, reach - receiver)
    passed = jax.random.randint(jax.random.fold_in(key, 1), (twos,), 0, 1 << 20) % (room + 1)
    sizes = sizes.at[1:1 + 2 * twos:2].set(donor - passed).at[2:2 + 2 * twos:2].set(receiver + passed)
    return sizes[jax.random.permutation(jax.random.fold_in(key, 2), count)]


def gaussian(key, shape, scale, bound, shards=(), kind=jnp.bfloat16):
    gain = level_of(key, shape, shards, -0.22, 0.18) if shards else 1.0
    values = jax.random.normal(key, shape, jnp.float32) * scale * gain
    return jnp.minimum(jnp.maximum(values, -bound), bound).astype(kind)


def setup_inputs(seed: int = 0) -> dict:
    streams_of = jax.random.split(jax.random.key(seed), 10)
    tokens = gaussian(streams_of[0], (SEQUENCES, LEN, D), 1.0, 6.0, ((0, 4), (1, 4)))
    segment_ids = jax.vmap(lambda own: jnp.searchsorted(jnp.cumsum(uneven_parts(own, max(4, LEN // 256), LEN, LEN // 2, 2)), jnp.arange(LEN), side="right"))(jax.random.split(streams_of[1], SEQUENCES)).reshape((SEQUENCES, LEN)).astype(jnp.int32)
    w_qkv = gaussian(streams_of[2], (3, D, D), D ** -0.5, 0.21875, ((2, 2),))
    w_out = gaussian(streams_of[3], (D, D), (max(4, D // 192)) ** -0.5, 3.0, ((0, 2),))
    w_up = gaussian(streams_of[4], (FF, D), D ** -0.5, 0.21875, ((0, 2),))
    w_down = gaussian(streams_of[5], (FF, D), FF ** -0.5, 0.109375, ((0, 2),))
    norm_gain = jnp.clip(1.0 + 0.18 * jax.random.normal(streams_of[6], (2, D), jnp.float32), 0.1, 1.9)
    norm_bias = gaussian(streams_of[7], (2, D), 0.3, 1.5, (), jnp.float32)
    grad_out = gaussian(streams_of[8], (SEQUENCES, LEN, D), 1.0, 6.0, ((0, 4), (1, 4)))
    return {"tokens": tokens, "segment_ids": segment_ids, "w_qkv": w_qkv, "w_out": w_out, "w_up": w_up, "w_down": w_down, "norm_gain": norm_gain, "norm_bias": norm_bias, "grad_out": grad_out}


precise = lax.Precision.HIGHEST

@jax.custom_vjp
def low(v):
    return lax.optimization_barrier(v.astype(jnp.bfloat16)).astype(jnp.float32)

@jax.custom_vjp
def low_back(v):
    return v

def low_keep(v):
    return (low(v), None)

def low_pass(kept, grad):
    return (grad,)

def back_keep(v):
    return (v, None)

def back_low(kept, grad):
    return (low(grad),)
low.defvjp(low_keep, low_pass)
low_back.defvjp(back_keep, back_low)

def matmul(left, right):
    return jnp.dot(left, right, precision=precise, preferred_element_type=jnp.float32)

def layer_norm(residual, norm_gain, norm_shift):
    center = residual - lax.optimization_barrier(jnp.mean(residual, axis=-1, keepdims=True))
    spread = lax.optimization_barrier(jnp.mean(center * center, axis=-1, keepdims=True))
    return center * lax.rsqrt(spread + 1e-06) * norm_gain + norm_shift

def attend_block(queries, seg_query, key_heads, value_heads, seg_ids):
    scores = jnp.einsum('qhd,khd->hqk', queries, key_heads, precision=precise) * 0.125
    scores = low_back(scores)
    allowed = seg_query[:, None] == seg_ids[None, :]
    scores = jnp.where(allowed[None], scores, -1e+30)
    weights = low(jax.nn.softmax(scores, axis=-1))
    return jnp.einsum('hqk,khd->qhd', weights, value_heads, precision=precise)

def sequence_layer(inputs, seg_ids, w_qkv, w_out, w_up, w_down, norm_gain, norm_shift):
    length = inputs.shape[0]
    projected = jnp.einsum('tf,jfd->jtd', inputs, w_qkv, precision=precise)
    projected = low_back(low(projected))
    queries = projected[0].reshape(length, HEADS, HEAD_DIM)
    key_heads = projected[1].reshape(length, HEADS, HEAD_DIM)
    value_heads = projected[2].reshape(length, HEADS, HEAD_DIM)
    row_block = min(length, 512)
    block_count = length // row_block

    def run_block(step_index):
        offset = (step_index * row_block).astype(jnp.int32)
        query_rows = lax.dynamic_slice_in_dim(queries, offset, row_block, 0)
        seg_rows = lax.dynamic_slice_in_dim(seg_ids, offset, row_block, 0)
        return attend_block(query_rows, seg_rows, key_heads, value_heads, seg_ids)
    mixed_heads = lax.map(jax.checkpoint(run_block), jnp.arange(block_count, dtype=jnp.int32))
    mixed_heads = low_back(low(mixed_heads.reshape(length, D)))
    attention = low_back(matmul(mixed_heads, w_out))
    resid_one = inputs + attention
    normed_one = layer_norm(resid_one, norm_gain[0], norm_shift[0])
    upward = low_back(matmul(low(normed_one), w_up.T))
    active = low(jax.nn.gelu(upward, approximate=False))
    ffn_out = low_back(matmul(active, w_down))
    return layer_norm(normed_one + ffn_out, norm_gain[1], norm_shift[1])

def reference(tokens, segment_ids, w_qkv, w_out, w_up, w_down, norm_gain, norm_bias, grad_out):
    params = (w_qkv.astype(jnp.float32), w_out.astype(jnp.float32), w_up.astype(jnp.float32), w_down.astype(jnp.float32), norm_gain.astype(jnp.float32), norm_bias.astype(jnp.float32))

    def step(totals, seq_item):
        inputs, seg_ids, cotangent = seq_item

        def forward(tok_rows, *weights):
            return sequence_layer(tok_rows, seg_ids, *weights)
        result, pullback = jax.vjp(forward, inputs.astype(jnp.float32), *params)
        gradients = pullback(cotangent.astype(jnp.float32))
        totals = tuple((left + right for left, right in zip(totals, gradients[1:])))
        return (totals, (result.astype(jnp.bfloat16), gradients[0]))
    zero_sums = tuple((jnp.zeros_like(weight) for weight in params))
    totals, (outputs, grad_tokens) = lax.scan(step, zero_sums, (tokens, segment_ids, grad_out))
    return (outputs, grad_tokens, totals[0], totals[1], totals[2], totals[3], totals[4], totals[5])
```

```python
import functools
import jax
import jax.numpy as jnp
from jax import lax
from jax.experimental import pallas as pl
from jax.experimental.pallas import tpu as pltpu
from jax.sharding import PartitionSpec as P

HEAD_DIM = 64
LANES = 128
STAT_ROWS = 16
BIG = 2.0**30
VMEM_BYTES = 60 * 1024 * 1024
low, full = jnp.bfloat16, jnp.float32


def dot_nn(left, right):
    return lax.dot_general(left, right, (((1,), (0,)), ((), ())), preferred_element_type=full)


def dot_nt(left, right):
    return lax.dot_general(left, right, (((1,), (1,)), ((), ())), preferred_element_type=full)


def dot_tn(left, right):
    return lax.dot_general(left, right, (((0,), (0,)), ((), ())), preferred_element_type=full)


def two_parts(values):
    high = values.astype(low)
    return high, (values - high.astype(full)).astype(low)


def one_hot_rows(seg_row):
    count = seg_row.shape[1]
    ids = lax.broadcasted_iota(jnp.int32, (LANES, count), 0).astype(full)
    return jnp.where(ids == seg_row, 1.0, 0.0).T


def head_mask(rows):
    return lax.broadcasted_iota(jnp.int32, (rows, LANES), 1) < HEAD_DIM


def for_pieces(count, body):
    if count == 1:
        body(0)
    else:
        lax.fori_loop(0, count, lambda index, carry: (body(index), carry)[1], 0)


def attend_kernel(counts, heads, *refs):
    groups = len(counts)
    own_a, own_b, tok_a, tok_b = refs[:4]
    kv_refs = refs[4 : 4 + groups]
    seg_refs = refs[4 + groups : 4 + 2 * groups]
    mixed_keep, mixed_send, lse_out, q_aug, top, total, acc = refs[4 + 2 * groups :]
    half = mixed_keep.shape[1]
    pairs = heads // 2
    seg_a = tok_a[0, 0:1, :LANES].astype(full)
    seg_b = tok_b[0, 0:1, :LANES].astype(full)
    hot_a, hot_b = one_hot_rows(seg_a), one_hot_rows(seg_b)
    hot_own = jnp.concatenate([hot_a, hot_b], axis=0)
    penalty = ((hot_own - 1.0) * BIG).astype(low)
    seg_low = jnp.minimum(jnp.min(seg_a), jnp.min(seg_b))
    seg_high = jnp.maximum(jnp.max(seg_a), jnp.max(seg_b))
    left = head_mask(2 * half)
    for pair in range(pairs):
        lanes = slice(pair * LANES, (pair + 1) * LANES)
        q_pair = jnp.concatenate([own_a[0, 0, :half, lanes], own_b[0, 0, :half, lanes]], axis=0)
        zero = jnp.zeros_like(q_pair)
        q_aug[2 * pair] = jnp.concatenate([jnp.where(left, q_pair, zero), penalty], axis=1)
        q_aug[2 * pair + 1] = jnp.concatenate([jnp.where(left, zero, q_pair), penalty], axis=1)

    def tile(keys_of, values_of, hot, first):
        hot = hot.astype(low)
        for pair in range(pairs):
            lanes = slice(pair * LANES, (pair + 1) * LANES)
            k_aug = jnp.concatenate([keys_of(lanes), hot], axis=1)
            v_turned = values_of(lanes).T
            for side in range(2):
                head = 2 * pair + side
                rows = slice(head * HEAD_DIM, (head + 1) * HEAD_DIM)
                scores = dot_nt(k_aug, q_aug[head])
                peak = jnp.max(scores, axis=0, keepdims=True)
                if not first:
                    before = top[head : head + 1, :]
                    peak = jnp.maximum(before, peak)
                weights = jnp.exp(scores - peak)
                add = jnp.sum(weights, axis=0, keepdims=True)
                mix = dot_nn(v_turned[side * HEAD_DIM : (side + 1) * HEAD_DIM], weights.astype(low))
                if not first:
                    shrink = jnp.exp(before - peak)
                    add = add + total[head : head + 1, :] * shrink
                    mix = mix + acc[rows, :] * shrink
                top[head : head + 1, :] = peak
                total[head : head + 1, :] = add
                acc[rows, :] = mix

    tile(
        lambda lanes: jnp.concatenate([own_a[1, 0, :half, lanes], own_b[1, 0, :half, lanes]], axis=0),
        lambda lanes: jnp.concatenate([own_a[2, 0, :half, lanes], own_b[2, 0, :half, lanes]], axis=0),
        hot_own,
        True,
    )
    for group in range(groups):
        kv_ref, seg_ref = kv_refs[group], seg_refs[group]

        def piece(index, kv_ref=kv_ref, seg_ref=seg_ref):
            seg = seg_ref[0, index, 0:1, :LANES].astype(full)

            @pl.when((jnp.min(seg) <= seg_high) & (jnp.max(seg) >= seg_low))
            def _():
                tile(
                    lambda lanes: kv_ref[0, 0, index, :half, lanes],
                    lambda lanes: kv_ref[1, 0, index, :half, lanes],
                    one_hot_rows(seg),
                    False,
                )

        for_pieces(counts[group], piece)
    lse = top[0:heads, :] + jnp.log(total[0:heads, :])
    lse_out[0, 0:heads, :] = lse
    row_of = lax.broadcasted_iota(jnp.int32, (STAT_ROWS, half), 0)
    scale = 1.0 / total[0:heads, :]
    for pair in range(pairs):
        lanes = slice(pair * LANES, (pair + 1) * LANES)
        heads_of = [
            acc[(2 * pair + side) * HEAD_DIM : (2 * pair + side + 1) * HEAD_DIM, :]
            * scale[2 * pair + side : 2 * pair + side + 1, :]
            for side in range(2)
        ]
        mixed = jnp.concatenate(heads_of, axis=0).T.astype(low)
        mixed_keep[0, :, lanes] = mixed[:half]
        mixed_send[0, :half, lanes] = mixed[half:]
    for column in range(pairs):
        stat = jnp.zeros((STAT_ROWS, half), full)
        for which in range(2):
            row = lse[which * pairs + column : which * pairs + column + 1, half:]
            for kind, part in enumerate(two_parts(row)):
                stat = jnp.where(row_of == kind + 2 * which, part.astype(full), stat)
        mixed_send[0, half:, column * LANES : (column + 1) * LANES] = stat.astype(low)


def own_block(own_ref, half, lanes, other_ref, kind):
    return jnp.concatenate([own_ref[kind, 0, :half, lanes], other_ref[kind, 0, :half, lanes]], axis=0)


def stat_row(ref, index, kind, other, head, half):
    row = kind * 2 + 4 * other
    tile = slice(head * LANES, (head + 1) * LANES)
    block = ref[index] if index is not None else ref
    return (
        ref[index + (slice(half + row, half + row + 1), tile)].astype(full)
        + ref[index + (slice(half + row + 1, half + row + 2), tile)].astype(full)
    )


def query_grad_kernel(counts, heads, turn_ref, *refs):
    groups = len(counts)
    own_a, own_b, tok_a, tok_b, grad_a, grad_b, w_out = refs[:7]
    kv_refs = refs[7 : 7 + groups]
    seg_refs = refs[7 + groups : 7 + 2 * groups]
    dq_out, dk_out, dv_out, q_aug, d_mix, acc = refs[7 + 2 * groups :]
    half = own_a.shape[2] - STAT_ROWS
    pairs = heads // 2
    turn = turn_ref[0]
    seg_a = tok_a[0, 0:1, :LANES].astype(full)
    seg_b = tok_b[0, 0:1, :LANES].astype(full)
    hot_own = jnp.concatenate([one_hot_rows(seg_a), one_hot_rows(seg_b)], axis=0)
    penalty = ((hot_own - 1.0) * BIG).astype(low)
    hot_own = hot_own.astype(low)
    seg_low = jnp.minimum(jnp.min(seg_a), jnp.min(seg_b))
    seg_high = jnp.maximum(jnp.max(seg_a), jnp.max(seg_b))
    left = head_mask(2 * half)
    d_attn = jnp.concatenate([grad_a[0, :half, :], grad_b[0, :half, :]], axis=0)
    d_mixed = dot_nt(d_attn, w_out[...]).astype(low)
    lse_rows, delta_rows = [], []
    for head in range(heads):
        pair, side = head // 2, head % 2
        lanes = slice(pair * LANES, (pair + 1) * LANES)
        keep = left if side == 0 else jnp.logical_not(left)
        q_pair = own_block(own_a, half, lanes, own_b, 0)
        q_aug[head] = jnp.concatenate(
            [jnp.where(keep, q_pair, jnp.zeros_like(q_pair)), penalty], axis=1
        )
        d_pair = d_mixed[:, lanes]
        d_mix[head] = jnp.where(keep, d_pair, jnp.zeros_like(d_pair))
        lse_rows.append(
            jnp.concatenate(
                [stat_row(grad_a, (0,), 0, 0, head, half), stat_row(grad_b, (0,), 0, 1, head, half)],
                axis=1,
            )
        )
        delta_rows.append(
            jnp.concatenate(
                [stat_row(grad_a, (0,), 1, 0, head, half), stat_row(grad_b, (0,), 1, 1, head, half)],
                axis=1,
            )
        )

    def weights_of(keys, hot, values, head):
        scores = dot_nt(jnp.concatenate([keys, hot], axis=1), q_aug[head])
        weights = jnp.exp(scores - lse_rows[head])
        d_weights = dot_nt(values, d_mix[head])
        return weights, (weights * (d_weights - delta_rows[head])).astype(low)

    half_a = pl.ds(pl.multiple_of(turn * half, half), half)
    half_b = pl.ds(pl.multiple_of((1 - turn) * half, half), half)
    for pair in range(pairs):
        lanes = slice(pair * LANES, (pair + 1) * LANES)
        keys, values = own_block(own_a, half, lanes, own_b, 1), own_block(own_a, half, lanes, own_b, 2)
        k_turned = keys.T
        dk = jnp.zeros((2 * half, LANES), full)
        dv = jnp.zeros((2 * half, LANES), full)
        for side in range(2):
            head = 2 * pair + side
            weights, d_scores = weights_of(keys, hot_own, values, head)
            acc[head * HEAD_DIM : (head + 1) * HEAD_DIM, :] = dot_nn(
                k_turned[side * HEAD_DIM : (side + 1) * HEAD_DIM], d_scores
            )
            dv = dv + dot_nn(weights.astype(low), d_mix[head])
            dk = dk + dot_nn(d_scores, q_aug[head, :, :LANES])
        dk_out[0, :, lanes] = dk
        dv_out[0, :, lanes] = dv
    for group in range(groups):
        kv_ref, seg_ref = kv_refs[group], seg_refs[group]

        def piece(index, kv_ref=kv_ref, seg_ref=seg_ref):
            seg = seg_ref[0, index, 0:1, :LANES].astype(full)

            @pl.when((jnp.min(seg) <= seg_high) & (jnp.max(seg) >= seg_low))
            def _():
                hot = one_hot_rows(seg).astype(low)
                for pair in range(pairs):
                    lanes = slice(pair * LANES, (pair + 1) * LANES)
                    keys, values = kv_ref[0, 0, index, :half, lanes], kv_ref[1, 0, index, :half, lanes]
                    k_turned = keys.T
                    for side in range(2):
                        head = 2 * pair + side
                        rows = slice(head * HEAD_DIM, (head + 1) * HEAD_DIM)
                        _, d_scores = weights_of(keys, hot, values, head)
                        acc[rows, :] += dot_nn(
                            k_turned[side * HEAD_DIM : (side + 1) * HEAD_DIM], d_scores
                        )

        for_pieces(counts[group], piece)
    for pair in range(pairs):
        lanes = slice(pair * LANES, (pair + 1) * LANES)
        dq = (acc[pair * LANES : (pair + 1) * LANES, :] * 0.125).T.astype(low)
        dq_out[0, half_a, lanes] = dq[:half]
        dq_out[0, half_b, lanes] = dq[half:]


def key_grad_kernel(counts, sides, heads, turn_ref, *refs):
    groups = len(counts)
    own_a, own_b, tok_a, tok_b, dk_in, dv_in, w_out = refs[:7]
    q_refs = refs[7 : 7 + groups]
    seg_refs = refs[7 + groups : 7 + 2 * groups]
    grad_refs = refs[7 + 2 * groups : 7 + 3 * groups]
    dk_out, dv_out, k_aug, values, dk_acc, dv_acc = refs[7 + 3 * groups :]
    half = own_a.shape[2] - STAT_ROWS
    pairs = heads // 2
    turn = turn_ref[0]
    seg_a = tok_a[0, 0:1, :LANES].astype(full)
    seg_b = tok_b[0, 0:1, :LANES].astype(full)
    hot_own = jnp.concatenate([one_hot_rows(seg_a), one_hot_rows(seg_b)], axis=0).astype(low)
    seg_low = jnp.minimum(jnp.min(seg_a), jnp.min(seg_b))
    seg_high = jnp.maximum(jnp.max(seg_a), jnp.max(seg_b))
    left = head_mask(half)
    for pair in range(pairs):
        lanes = slice(pair * LANES, (pair + 1) * LANES)
        k_aug[pair] = jnp.concatenate([own_block(own_a, half, lanes, own_b, 1), hot_own], axis=1)
        values[pair] = own_block(own_a, half, lanes, own_b, 2)
    dk_acc[...] = dk_in[0]
    dv_acc[...] = dv_in[0]
    for group in range(groups):
        q_ref, seg_ref, grad_ref, other = q_refs[group], seg_refs[group], grad_refs[group], sides[group]

        def piece(index, q_ref=q_ref, seg_ref=seg_ref, grad_ref=grad_ref, other=other):
            seg = seg_ref[0, index, 0:1, :LANES].astype(full)

            @pl.when((jnp.min(seg) <= seg_high) & (jnp.max(seg) >= seg_low))
            def _():
                penalty = ((one_hot_rows(seg) - 1.0) * BIG).astype(low)
                d_mixed = dot_nt(grad_ref[0, index, :half, :], w_out[...]).astype(low)
                for pair in range(pairs):
                    lanes = slice(pair * LANES, (pair + 1) * LANES)
                    q_pair, d_pair = q_ref[0, index, :half, lanes], d_mixed[:, lanes]
                    zero = jnp.zeros_like(q_pair)
                    dk, dv = dk_acc[:, lanes], dv_acc[:, lanes]
                    for side in range(2):
                        head = 2 * pair + side
                        keep = left if side == 0 else jnp.logical_not(left)
                        q_mask = jnp.where(keep, q_pair, zero)
                        d_mask = jnp.where(keep, d_pair, zero)
                        lse = stat_row(grad_ref, (0, index), 0, other, head, half)
                        delta = stat_row(grad_ref, (0, index), 1, other, head, half)
                        scores = dot_nt(k_aug[pair], jnp.concatenate([q_mask, penalty], axis=1))
                        weights = jnp.exp(scores - lse)
                        d_weights = dot_nt(values[pair], d_mask)
                        d_scores = (weights * (d_weights - delta)).astype(low)
                        dv = dv + dot_nn(weights.astype(low), d_mask)
                        dk = dk + dot_nn(d_scores, q_mask)
                    dk_acc[:, lanes] = dk
                    dv_acc[:, lanes] = dv

        for_pieces(counts[group], piece)
    half_a = pl.ds(pl.multiple_of(turn * half, half), half)
    half_b = pl.ds(pl.multiple_of((1 - turn) * half, half), half)
    dk_out[0, half_a, :] = dk_acc[:half, :].astype(low)
    dk_out[0, half_b, :] = dk_acc[half:, :].astype(low)
    dv_out[0, half_a, :] = dv_acc[:half, :].astype(low)
    dv_out[0, half_b, :] = dv_acc[half:, :].astype(low)


def norm_of(residual):
    center = residual - jnp.mean(residual, axis=-1, keepdims=True)
    inverse = lax.rsqrt(jnp.mean(center * center, axis=-1, keepdims=True) + 1e-06)
    return center * inverse, inverse


def norm_back(d_normal, normal, inverse):
    return inverse * (
        d_normal
        - jnp.mean(d_normal, axis=-1, keepdims=True)
        - normal * jnp.mean(d_normal * normal, axis=-1, keepdims=True)
    )


def middle_kernel(
    chunk,
    turn_ref,
    tok,
    mixed_keep,
    mixed_recv,
    lse_keep,
    w_out_own,
    w_out_oth,
    w_up_own,
    w_up_oth,
    w_down_own,
    w_down_oth,
    gain,
    shift,
    grad_out,
    out,
    d_resid,
    payload,
    active_own,
    active_oth,
    d_up_own,
    d_up_oth,
    d_ffn_out,
    normed_out,
    small,
    slope,
):
    seqs, half, width = out.shape
    rows = seqs * half
    heads = mixed_keep.shape[2] // HEAD_DIM
    keep = mixed_keep[...].reshape(rows, -1)
    recv = mixed_recv[:, :half, :].reshape(rows, -1)
    attn = dot_nn(keep, w_out_own[...]) + dot_nn(recv, w_out_oth[...])
    resid_one = tok[:, :half, :].reshape(rows, width).astype(full) + attn
    normal_one, inverse_one = norm_of(resid_one)
    gain_one, gain_two = gain[0:1, :], gain[1:2, :]
    normed = normal_one * gain_one + shift[0:1, :]
    normed_low = normed.astype(low)
    normed_out[...] = normed_low
    units = w_up_own.shape[0]
    sides = ((w_up_own, w_down_own, active_own, d_up_own), (w_up_oth, w_down_oth, active_oth, d_up_oth))
    ffn = jnp.zeros((rows, width), full)
    for which, (w_up, w_down, active_ref, _) in enumerate(sides):
        for start in range(0, units, chunk):
            part = slice(start, start + chunk)
            upward = dot_nt(normed_low, w_up[part, :])
            spread = 0.5 * (1.0 + lax.erf(upward * 0.7071067811865476))
            active = (upward * spread).astype(low)
            slope[:, which * units + start : which * units + start + chunk] = (
                spread + upward * (jnp.exp(upward * upward * -0.5) * 0.3989422804014327)
            )
            active_ref[:, part] = active
            ffn = ffn + dot_nn(active, w_down[part, :])
    normal_two, inverse_two = norm_of(normed + ffn)
    out[...] = (normal_two * gain_two + shift[1:2, :]).astype(low).reshape(seqs, half, width)
    grad = grad_out[...].reshape(rows, width).astype(full)
    small[1:2, :] = jnp.sum(grad * normal_two, axis=0, keepdims=True)
    small[3:4, :] = jnp.sum(grad, axis=0, keepdims=True)
    d_resid_two = norm_back(grad * gain_two, normal_two, inverse_two)
    d_ffn = d_resid_two.astype(low)
    d_ffn_out[...] = d_ffn
    d_normed = d_resid_two
    for which, (w_up, w_down, _, d_up_ref) in enumerate(sides):
        for start in range(0, units, chunk):
            part = slice(start, start + chunk)
            d_active = dot_nt(d_ffn, w_down[part, :])
            d_up = (d_active * slope[:, which * units + start : which * units + start + chunk]).astype(low)
            d_up_ref[:, part] = d_up
            d_normed = d_normed + dot_nn(d_up, w_up[part, :])
    small[0:1, :] = jnp.sum(d_normed * normal_one, axis=0, keepdims=True)
    small[2:3, :] = jnp.sum(d_normed, axis=0, keepdims=True)
    small[4:8, :] = jnp.zeros((4, width), full)
    d_resid_one = norm_back(d_normed * gain_one, normal_one, inverse_one)
    d_resid[...] = d_resid_one.reshape(seqs, half, width)
    d_attn = d_resid_one.astype(low)
    payload[:, :half, :] = d_attn.reshape(seqs, half, width)
    column_of = lax.broadcasted_iota(jnp.int32, (8, heads * HEAD_DIM), 1) // HEAD_DIM
    chosen = jnp.where(column_of == lax.broadcasted_iota(jnp.int32, (8, heads * HEAD_DIM), 0), 1.0, 0.0)
    deltas = []
    for mixed, w_out in ((keep, w_out_own), (recv, w_out_oth)):
        d_mixed = dot_nt(d_attn, w_out[...]).astype(low).astype(full)
        deltas.append(
            lax.dot_general(
                chosen,
                d_mixed * mixed.astype(full),
                (((1,), (1,)), ((), ())),
                precision=lax.Precision.HIGHEST,
                preferred_element_type=full,
            )
        )
    row_of = lax.broadcasted_iota(jnp.int32, (STAT_ROWS, half), 0)
    pairs = heads // 2
    for seq in range(seqs):
        for head in range(heads):
            lse_high, lse_low = two_parts(lse_keep[seq, head : head + 1, :half])
            tile = slice((head % pairs) * LANES, (head % pairs + 1) * LANES)
            row = half + 2 * (head // pairs)
            parts = [lse_high.astype(full), lse_low.astype(full)]
            for which in range(2):
                piece = deltas[which][head : head + 1, seq * half : (seq + 1) * half]
                if which == 1:
                    parts.append(mixed_recv[seq, row : row + 1, tile].astype(full))
                    parts.append(mixed_recv[seq, row + 1 : row + 2, tile].astype(full))
                parts.extend(part.astype(full) for part in two_parts(piece))
            stat = jnp.zeros((STAT_ROWS, half), full)
            for index, part in enumerate(parts):
                stat = jnp.where(row_of == index, part, stat)
            payload[seq, half:, head * LANES : (head + 1) * LANES] = stat.astype(low)


def slot_order(count):
    if count == 1:
        return [0]
    inner = slot_order(count // 2)
    return [2 * slot + 1 for slot in inner] + [2 * slot for slot in inner]


def reversed_bits(value, bits):
    return sum(((value >> bit) & 1) << (bits - 1 - bit) for bit in range(bits))


def whole(shape):
    return pl.BlockSpec(shape, lambda *_: (0,) * len(shape))


def kernel_params():
    return pltpu.CompilerParams(vmem_limit_bytes=VMEM_BYTES, dimension_semantics=("arbitrary",))


def on_device(
    ctx_size,
    dp_size,
    tokens,
    segment_ids,
    w_qkv,
    w_out,
    w_up,
    w_down,
    norm_gain,
    norm_bias,
    grad_out,
):
    seqs, span, width = tokens.shape
    half = span // 2
    local_width = w_out.shape[0]
    heads = local_width // HEAD_DIM
    units = w_up.shape[0]
    rows = seqs * half
    long_half = half + STAT_ROWS
    ctx_bits = ctx_size.bit_length() - 1
    turn = lax.axis_index("tensor")
    place = lax.axis_index("ctx")
    row_place = lax.axis_index("dp")
    turn_array = turn.reshape(1)

    def swap(value):
        return lax.ppermute(value, "tensor", [(0, 1), (1, 0)])

    def hop(value, stage):
        moves = []
        for spot in range(ctx_size):
            for core in range(2):
                bit = stage if core == 0 else ctx_bits - 1 - stage
                moves.append((spot * 2 + core, (spot ^ (1 << bit)) * 2 + core))
        return lax.ppermute(value, ("ctx", "tensor"), moves)

    def gather(own):
        own = own[:, None]
        groups = []
        if ctx_bits >= 1:
            groups.append(hop(own, 0))
        if ctx_bits >= 2:
            groups.append(hop(own, 1))
            groups.append(hop(groups[0], 1))
        for stage in range(2, ctx_bits):
            groups.append(hop(jnp.concatenate([own] + groups, axis=1), stage))
        return groups + [swap(group) for group in groups]

    def half_of(value, which):
        return lax.dynamic_slice_in_dim(value, which * half, half, 1)

    def with_ids(which):
        ids = half_of(segment_ids, which).astype(low)
        row = jnp.pad(ids[:, None, :], ((0, 0), (0, STAT_ROWS - 1), (0, width - half)))
        return jnp.concatenate([half_of(tokens, which), row], axis=1)

    tok_a, tok_b = with_ids(turn), with_ids(1 - turn)
    tok_groups = gather(tok_a)
    counts = [group.shape[1] for group in tok_groups]
    sides = [0] * (len(counts) // 2) + [1] * (len(counts) // 2)
    w_out_oth, w_up_oth, w_down_oth = swap(w_out), swap(w_up), swap(w_down)

    scale = jnp.array([0.125, 1.0, 1.0], full).reshape(3, 1, 1, 1)

    def project_own(value):
        product = jnp.einsum("srf,jfd->jsrd", value, w_qkv, preferred_element_type=full)
        return (product * scale).astype(low)

    def project_kv(value):
        return jnp.einsum("sgrf,jfd->jsgrd", value, w_qkv[1:], preferred_element_type=full).astype(low)

    def project_q(value):
        product = jnp.einsum("sgrf,fd->sgrd", value, w_qkv[0], preferred_element_type=full)
        return (product * 0.125).astype(low)

    own_a, own_b = project_own(tok_a), project_own(tok_b)
    kv_groups = [project_kv(group) for group in tok_groups]

    own_spec = pl.BlockSpec((3, 1, long_half, local_width), lambda s, *_: (0, s, 0, 0))
    tok_spec = pl.BlockSpec((1, STAT_ROWS, width), lambda s, *_: (s, half // STAT_ROWS, 0))
    kv_specs = [
        pl.BlockSpec((2, 1, count, long_half, local_width), lambda s, *_: (0, s, 0, 0, 0)) for count in counts
    ]
    seg_specs = [
        pl.BlockSpec((1, count, STAT_ROWS, width), lambda s, *_: (s, 0, half // STAT_ROWS, 0)) for count in counts
    ]

    def seq_spec(shape):
        return pl.BlockSpec((1,) + shape, lambda s, *_: (s,) + (0,) * len(shape))

    mixed_keep, mixed_send, lse = pl.pallas_call(
        functools.partial(attend_kernel, counts, heads),
        grid=(seqs,),
        in_specs=[own_spec, own_spec, tok_spec, tok_spec] + kv_specs + seg_specs,
        out_specs=[seq_spec((half, local_width)), seq_spec((long_half, local_width)), seq_spec((8, span))],
        out_shape=[
            jax.ShapeDtypeStruct((seqs, half, local_width), low),
            jax.ShapeDtypeStruct((seqs, long_half, local_width), low),
            jax.ShapeDtypeStruct((seqs, 8, span), full),
        ],
        scratch_shapes=[
            pltpu.VMEM((heads, span, 2 * LANES), low),
            pltpu.VMEM((8, span), full),
            pltpu.VMEM((8, span), full),
            pltpu.VMEM((local_width, span), full),
        ],
        compiler_params=kernel_params(),
        name="attend",
    )(own_a, own_b, tok_a, tok_b, *kv_groups, *tok_groups)
    mixed_recv = swap(mixed_send)

    middle_in = [
        tok_a,
        mixed_keep,
        mixed_recv,
        lse,
        w_out,
        w_out_oth,
        w_up,
        w_up_oth,
        w_down,
        w_down_oth,
        norm_gain,
        norm_bias,
    ]
    middle_shapes = [
        ((seqs, half, width), low),
        ((seqs, half, width), full),
        ((seqs, long_half, width), low),
        ((rows, units), low),
        ((rows, units), low),
        ((rows, units), low),
        ((rows, units), low),
        ((rows, width), low),
        ((rows, width), low),
        ((8, width), full),
    ]
    (
        out_half,
        d_resid,
        payload,
        active_own,
        active_oth,
        d_up_own,
        d_up_oth,
        d_ffn,
        normed_low,
        small,
    ) = pl.pallas_call(
        functools.partial(middle_kernel, min(512, units)),
        grid_spec=pltpu.PrefetchScalarGridSpec(
            num_scalar_prefetch=1,
            grid=(1,),
            in_specs=[whole(value.shape) for value in middle_in]
            + [pl.BlockSpec((seqs, half, width), lambda s, turn_ref: (0, turn_ref[0], 0))],
            out_specs=[whole(shape) for shape, _ in middle_shapes],
            scratch_shapes=[pltpu.VMEM((rows, 2 * units), full)],
        ),
        out_shape=[jax.ShapeDtypeStruct(shape, kind) for shape, kind in middle_shapes],
        compiler_params=kernel_params(),
        name="middle",
    )(turn_array, *middle_in, grad_out)

    grad_groups = gather(payload)
    payload_b = swap(payload)

    sum_shape = jax.ShapeDtypeStruct((seqs, span, local_width), full)
    row_shape = jax.ShapeDtypeStruct((seqs, span, local_width), low)
    grad_spec = seq_spec((long_half, width))
    span_spec = seq_spec((span, local_width))
    d_query, dk_sum, dv_sum = pl.pallas_call(
        functools.partial(query_grad_kernel, counts, heads),
        grid_spec=pltpu.PrefetchScalarGridSpec(
            num_scalar_prefetch=1,
            grid=(seqs,),
            in_specs=[own_spec, own_spec, tok_spec, tok_spec, grad_spec, grad_spec, whole(w_out.shape)]
            + kv_specs
            + seg_specs,
            out_specs=[span_spec] * 3,
            scratch_shapes=[
                pltpu.VMEM((heads, span, 2 * LANES), low),
                pltpu.VMEM((heads, span, LANES), low),
                pltpu.VMEM((local_width, span), full),
            ],
        ),
        out_shape=[row_shape, sum_shape, sum_shape],
        compiler_params=kernel_params(),
        name="query_grad",
    )(turn_array, own_a, own_b, tok_a, tok_b, payload, payload_b, w_out, *kv_groups, *tok_groups)

    q_groups = [project_q(group) for group in tok_groups]
    q_specs = [seq_spec((count, long_half, local_width)) for count in counts]
    grad_specs = [seq_spec((count, long_half, width)) for count in counts]
    d_key, d_value = pl.pallas_call(
        functools.partial(key_grad_kernel, counts, sides, heads),
        grid_spec=pltpu.PrefetchScalarGridSpec(
            num_scalar_prefetch=1,
            grid=(seqs,),
            in_specs=[own_spec, own_spec, tok_spec, tok_spec, span_spec, span_spec, whole(w_out.shape)]
            + q_specs
            + seg_specs
            + grad_specs,
            out_specs=[span_spec] * 2,
            scratch_shapes=[
                pltpu.VMEM((heads // 2, span, 2 * LANES), low),
                pltpu.VMEM((heads // 2, span, LANES), low),
                pltpu.VMEM((span, local_width), full),
                pltpu.VMEM((span, local_width), full),
            ],
        ),
        out_shape=[row_shape, row_shape],
        compiler_params=kernel_params(),
        name="key_grad",
    )(turn_array, own_a, own_b, tok_a, tok_b, dk_sum, dv_sum, w_out, *q_groups, *tok_groups, *grad_groups)

    d_proj = [value.reshape(seqs * span, local_width) for value in (d_query, d_key, d_value)]
    d_input = sum(dot_nt(value, w_qkv[j]) for j, value in enumerate(d_proj)).astype(low)
    d_input = (d_input.astype(full) + swap(d_input).astype(full)).reshape(seqs, span, width)

    def both_halves(own):
        other = swap(own)
        return jnp.where(
            turn == 0, jnp.concatenate([own, other], axis=1), jnp.concatenate([other, own], axis=1)
        )

    outputs = both_halves(out_half)
    grad_tokens = d_input + both_halves(d_resid)

    flat_tokens = tokens.reshape(seqs * span, width)
    order = jnp.array(slot_order(ctx_size), jnp.int32)
    mirrored = jnp.array([reversed_bits(slot, ctx_bits) for slot in slot_order(ctx_size)], jnp.int32)
    owners = place ^ jnp.where(turn == 0, order, mirrored)

    def by_owner(value):
        return value.reshape(ctx_size, value.shape[0] // ctx_size, -1)[owners]

    def reduce_blocks(blocks):
        blocks = blocks.astype(low)
        for stage in range(ctx_bits):
            count = blocks.shape[0] // 2
            got = hop(blocks[:count], stage)
            blocks = (blocks[count:].astype(full) + got.astype(full)).astype(low)
        block = blocks[0]
        split = block.shape[0] // 2
        parity = row_place & 1

        def part(which):
            return lax.dynamic_slice_in_dim(block, which * split, split, 0)

        near = [(spot, spot ^ 1) for spot in range(dp_size)]
        mine = (part(parity).astype(full) + lax.ppermute(part(1 - parity), "dp", near).astype(full)).astype(low)
        for bit in range(1, dp_size.bit_length() - 1):
            far = [(spot, spot ^ (1 << bit)) for spot in range(dp_size)]
            mine = (mine.astype(full) + lax.ppermute(mine, "dp", far).astype(full)).astype(low)
        other = lax.ppermute(mine, "dp", near)
        return jnp.where(
            parity == 0, jnp.concatenate([mine, other], axis=0), jnp.concatenate([other, mine], axis=0)
        ).astype(full)

    d_ffn_b, normed_b = swap(d_ffn), swap(normed_low)
    active_b, d_up_b = swap(active_oth), swap(d_up_oth)
    down_total = reduce_blocks(by_owner(dot_tn(d_ffn, active_own) + dot_tn(d_ffn_b, active_b)))
    up_total = reduce_blocks(by_owner(dot_tn(normed_low, d_up_own) + dot_tn(normed_b, d_up_b)))
    d_attn_a = payload[:, :half].reshape(rows, width)
    d_attn_b = payload_b[:, :half].reshape(rows, width)
    out_grad = dot_tn(d_attn_a, mixed_keep.reshape(rows, local_width)) + dot_tn(
        d_attn_b, mixed_send[:, :half].reshape(rows, local_width)
    )
    quarter = width // ctx_size
    pad_rows = 16
    small_rows = (small[:4] + swap(small)[:4]).reshape(4, ctx_size, quarter).transpose(1, 0, 2)[owners]
    small_rows = jnp.pad(small_rows, ((0, 0), (0, pad_rows - 4), (0, local_width - quarter)))
    out_total = reduce_blocks(jnp.concatenate([by_owner(out_grad), small_rows], axis=1))
    qkv_grad = jnp.concatenate([dot_tn(flat_tokens, value) for value in d_proj], axis=1)
    qkv_total = reduce_blocks(by_owner(qkv_grad))

    grad_qkv = qkv_total.reshape(quarter, 3, local_width).transpose(1, 0, 2)
    small_total = out_total[quarter : quarter + 4, :quarter]
    return (
        outputs,
        grad_tokens,
        grad_qkv,
        out_total[:quarter].T,
        up_total.T,
        down_total.T,
        small_total[0:2],
        small_total[2:4],
    )


def solution(mesh):
    return jax.shard_map(
        functools.partial(on_device, mesh.shape["ctx"], mesh.shape["dp"]),
        mesh=mesh,
        in_specs=(
            P("dp", "ctx", None),
            P("dp", "ctx"),
            P(None, None, "tensor"),
            P("tensor", None),
            P("tensor", None),
            P("tensor", None),
            P(),
            P(),
            P("dp", "ctx", None),
        ),
        out_specs=(
            P("dp", "ctx", None),
            P("dp", "ctx", None),
            P(None, "ctx", "tensor"),
            P("tensor", "ctx"),
            P("tensor", "ctx"),
            P("tensor", "ctx"),
            P(None, "ctx"),
            P(None, "ctx"),
        ),
        check_vma=False,
    )
```

```python
import functools
import jax
import jax.numpy as jnp
from jax import lax
from jax.experimental import pallas as pl
from jax.experimental.pallas import tpu as pltpu
from jax.sharding import PartitionSpec as P

HEAD_DIM = 64
LANES = 128
STAT_ROWS = 16
BIG = 2.0**30
low, full = jnp.bfloat16, jnp.float32


def dot_nn(left, right):
    return lax.dot_general(left, right, (((1,), (0,)), ((), ())), preferred_element_type=full)


def dot_nt(left, right):
    return lax.dot_general(left, right, (((1,), (1,)), ((), ())), preferred_element_type=full)


def dot_tn(left, right):
    return lax.dot_general(left, right, (((0,), (0,)), ((), ())), preferred_element_type=full)


def two_parts(values):
    high = values.astype(low)
    return high, (values - high.astype(full)).astype(low)


def project_kernel(w_qkv, part_a, part_b, out):
    seqs, half = part_a.shape[0], part_a.shape[2] - STAT_ROWS
    local = w_qkv.shape[2]
    rows = jnp.concatenate(
        [part[seq, 0, :half, :] for seq in range(seqs) for part in (part_a, part_b)], axis=0
    )
    for kind in range(3):
        product = dot_nn(rows, w_qkv[kind])
        if kind == 0:
            product = product * 0.125
        out[:, 0, :, kind * local : (kind + 1) * local] = product.astype(low).reshape(seqs, 2 * half, local)
    ids = lax.broadcasted_iota(jnp.int32, (LANES, half), 0).astype(full)
    for seq in range(seqs):
        for which, part in enumerate((part_a, part_b)):
            row = part[seq, 0, half : half + 1, :half].astype(full)
            out[seq, 0, which * half : (which + 1) * half, 3 * local :] = (
                jnp.where(ids == row, 1.0, 0.0).T.astype(low)
            )


class Lanes:
    def __init__(self, heads):
        self.local = heads * HEAD_DIM

    def of(self, kind, pair):
        start = kind * self.local + pair * LANES
        return slice(start, start + LANES)

    @property
    def hot(self):
        return slice(3 * self.local, 3 * self.local + LANES)


def split_heads(value):
    left = lax.broadcasted_iota(jnp.int32, value.shape, 1) < HEAD_DIM
    zero = jnp.zeros_like(value)
    return jnp.where(left, value, zero), jnp.where(left, zero, value)


def present(hot):
    return jnp.max(hot.astype(full), axis=0, keepdims=True)


def over_units(counts, unit_refs, lanes, own_ids, body):
    flags = [
        jnp.max(own_ids * present(ref[0, 0, :, lanes.hot])) > 0.0 if count == 1 else None
        for count, ref in zip(counts, unit_refs)
    ]
    for number, (count, ref) in enumerate(zip(counts, unit_refs)):
        if count == 1:
            pl.when(flags[number])(functools.partial(body, number, 0))
        else:

            def step(index, carry, number=number, ref=ref):
                shared = jnp.max(own_ids * present(ref[0, index, :, lanes.hot])) > 0.0
                pl.when(shared)(functools.partial(body, number, index))
                return carry

            lax.fori_loop(0, count, step, 0)


def attend_kernel(counts, heads, begin, finish, *refs):
    lanes, pairs, units = Lanes(heads), heads // 2, len(counts)
    own, unit_refs = refs[0], refs[1 : 1 + units]
    refs = refs[1 + units :]
    if not begin:
        acc_in, stat_in = refs[:2]
        refs = refs[2:]
    if finish:
        mixed_keep, mixed_send, lse_out = refs[:3]
        refs = refs[3:]
    else:
        acc_out, stat_out = refs[:2]
        refs = refs[2:]
    q_aug, scores, weights, stat, acc = refs
    span = own.shape[2]
    half = span // 2
    hot_own = own[0, 0, :, lanes.hot]
    penalty = ((hot_own.astype(full) - 1.0) * BIG).astype(low)
    for pair in range(pairs):
        for side, masked in enumerate(split_heads(own[0, 0, :, lanes.of(0, pair)])):
            q_aug[2 * pair + side] = jnp.concatenate([masked, penalty], axis=1)
    if not begin:
        acc[...] = acc_in[0]
        stat[...] = stat_in[0]

    def block(ref, index, first):
        hot = ref[0, index, :, lanes.hot]
        peaks = []
        for pair in range(pairs):
            k_aug = jnp.concatenate([ref[0, index, :, lanes.of(1, pair)], hot], axis=1)
            for side in range(2):
                head = 2 * pair + side
                product = dot_nt(k_aug, q_aug[head])
                scores[head] = product
                peak = jnp.max(product, axis=0, keepdims=True)
                peaks.append(peak if first else jnp.maximum(peak, stat[head : head + 1, :]))
        sums = []
        for head in range(heads):
            weight = jnp.exp(scores[head] - peaks[head])
            sums.append(jnp.sum(weight, axis=0, keepdims=True))
            weights[head] = weight.astype(low)
        for pair in range(pairs):
            turned = ref[0, index, :, lanes.of(2, pair)].T
            for side in range(2):
                head = 2 * pair + side
                rows = slice(head * HEAD_DIM, (head + 1) * HEAD_DIM)
                mix = dot_nn(turned[side * HEAD_DIM : (side + 1) * HEAD_DIM], weights[head])
                total = sums[head]
                if not first:
                    shrink = jnp.exp(stat[head : head + 1, :] - peaks[head])
                    total = total + stat[8 + head : 9 + head, :] * shrink
                    mix = mix + acc[rows, :] * shrink
                acc[rows, :] = mix
                stat[head : head + 1, :] = peaks[head]
                stat[8 + head : 9 + head, :] = total

    if begin:
        block(own, 0, True)
    over_units(
        counts, unit_refs, lanes, present(hot_own), lambda number, index: block(unit_refs[number], index, False)
    )
    if not finish:
        acc_out[0] = acc[...]
        stat_out[0] = stat[...]
        return
    totals = stat[8 : 8 + heads, :]
    lse = stat[0:heads, :] + jnp.log(totals)
    lse_out[0, 0:heads, :] = lse
    lse_out[0, heads:8, :] = jnp.zeros((8 - heads, span), full)
    scale = 1.0 / totals
    for pair in range(pairs):
        chosen = slice(pair * LANES, (pair + 1) * LANES)
        mixed = jnp.concatenate(
            [
                acc[head * HEAD_DIM : (head + 1) * HEAD_DIM, :] * scale[head : head + 1, :]
                for head in (2 * pair, 2 * pair + 1)
            ],
            axis=0,
        ).T.astype(low)
        mixed_keep[0, :, chosen] = mixed[:half]
        mixed_send[0, :half, chosen] = mixed[half:]
    row_of = lax.broadcasted_iota(jnp.int32, (STAT_ROWS, half), 0)
    for column in range(pairs):
        tile = jnp.zeros((STAT_ROWS, half), full)
        for which in range(2):
            row = lse[which * pairs + column : which * pairs + column + 1, half:]
            for kind, part in enumerate(two_parts(row)):
                tile = jnp.where(row_of == kind + 2 * which, part.astype(full), tile)
        mixed_send[0, half:, column * LANES : (column + 1) * LANES] = tile.astype(low)


def stat_row(grad_a, grad_b, at, kind, head, half):
    tile = slice(head * LANES, (head + 1) * LANES)
    parts = []
    for other, ref in enumerate((grad_a, grad_b)):
        row = half + 2 * kind + 4 * other
        parts.append(
            ref[at + (slice(row, row + 1), tile)].astype(full)
            + ref[at + (slice(row + 1, row + 2), tile)].astype(full)
        )
    return jnp.concatenate(parts, axis=1)


def query_grad_kernel(counts, heads, *refs):
    lanes, pairs, units = Lanes(heads), heads // 2, len(counts)
    own, grad_a, grad_b, w_out = refs[:4]
    unit_refs = refs[4 : 4 + units]
    dq_out, dk_out, dv_out, q_aug, d_mix, rows_of, scores, weights, d_scores, acc = refs[4 + units :]
    span = own.shape[2]
    half = span // 2
    hot_own = own[0, 0, :, lanes.hot]
    penalty = ((hot_own.astype(full) - 1.0) * BIG).astype(low)
    d_attn = jnp.concatenate([grad_a[0, :half, :], grad_b[0, :half, :]], axis=0)
    d_mixed = dot_nt(d_attn, w_out[...]).astype(low)
    for pair in range(pairs):
        q_parts = split_heads(own[0, 0, :, lanes.of(0, pair)])
        d_parts = split_heads(d_mixed[:, pair * LANES : (pair + 1) * LANES])
        for side in range(2):
            head = 2 * pair + side
            q_aug[head] = jnp.concatenate([q_parts[side], penalty], axis=1)
            d_mix[head] = d_parts[side]
            rows_of[head : head + 1, :] = stat_row(grad_a, grad_b, (0,), 0, head, half)
            rows_of[8 + head : 9 + head, :] = stat_row(grad_a, grad_b, (0,), 1, head, half)

    def block(ref, index, first):
        hot = ref[0, index, :, lanes.hot]
        for pair in range(pairs):
            k_aug = jnp.concatenate([ref[0, index, :, lanes.of(1, pair)], hot], axis=1)
            for side in range(2):
                head = 2 * pair + side
                scores[head] = dot_nt(k_aug, q_aug[head])
        for pair in range(pairs):
            values = ref[0, index, :, lanes.of(2, pair)]
            for side in range(2):
                head = 2 * pair + side
                weight = jnp.exp(scores[head] - rows_of[head : head + 1, :])
                d_weight = dot_nt(values, d_mix[head])
                d_scores[head] = (weight * (d_weight - rows_of[8 + head : 9 + head, :])).astype(low)
                if first:
                    weights[head] = weight.astype(low)
        for pair in range(pairs):
            turned = ref[0, index, :, lanes.of(1, pair)].T
            for side in range(2):
                head = 2 * pair + side
                rows = slice(head * HEAD_DIM, (head + 1) * HEAD_DIM)
                product = dot_nn(turned[side * HEAD_DIM : (side + 1) * HEAD_DIM], d_scores[head])
                acc[rows, :] = product if first else acc[rows, :] + product
            if first:
                chosen = slice(pair * LANES, (pair + 1) * LANES)
                one, two = 2 * pair, 2 * pair + 1
                dv_out[0, :, chosen] = dot_nn(weights[one], d_mix[one]) + dot_nn(weights[two], d_mix[two])
                dk_out[0, :, chosen] = dot_nn(d_scores[one], q_aug[one, :, :LANES]) + dot_nn(
                    d_scores[two], q_aug[two, :, :LANES]
                )

    block(own, 0, True)
    over_units(
        counts, unit_refs, lanes, present(hot_own), lambda number, index: block(unit_refs[number], index, False)
    )
    for pair in range(pairs):
        chosen = slice(pair * LANES, (pair + 1) * LANES)
        dq_out[0, :, chosen] = (acc[chosen, :] * 0.125).T.astype(low)


def key_grad_kernel(counts, heads, turn_ref, *refs):
    lanes, pairs, units = Lanes(heads), heads // 2, len(counts)
    own, dq_in, dk_in, dv_in, w_out, w_qkv = refs[:6]
    unit_refs = refs[6 : 6 + units]
    a_refs = refs[6 + units : 6 + 2 * units]
    b_refs = refs[6 + 2 * units : 6 + 3 * units]
    d_kv, d_input, k_aug, q_mask, d_mix, scores, weights, d_scores, dk_acc, dv_acc = refs[6 + 3 * units :]
    span = own.shape[2]
    half = span // 2
    local = lanes.local
    turn = turn_ref[0]
    hot_own = own[0, 0, :, lanes.hot]
    for pair in range(pairs):
        k_aug[pair] = jnp.concatenate([own[0, 0, :, lanes.of(1, pair)], hot_own], axis=1)
    dk_acc[...] = dk_in[0]
    dv_acc[...] = dv_in[0]

    def block(number, index):
        ref, grad_a, grad_b = unit_refs[number], a_refs[number], b_refs[number]
        penalty = ((ref[0, index, :, lanes.hot].astype(full) - 1.0) * BIG).astype(low)
        d_attn = jnp.concatenate([grad_a[0, index, :half, :], grad_b[0, index, :half, :]], axis=0)
        d_mixed = dot_nt(d_attn, w_out[...]).astype(low)
        for pair in range(pairs):
            q_parts = split_heads(ref[0, index, :, lanes.of(0, pair)])
            d_parts = split_heads(d_mixed[:, pair * LANES : (pair + 1) * LANES])
            for side in range(2):
                head = 2 * pair + side
                q_mask[head] = q_parts[side]
                d_mix[head] = d_parts[side]
                scores[head] = dot_nt(k_aug[pair], jnp.concatenate([q_parts[side], penalty], axis=1))
        for pair in range(pairs):
            values = own[0, 0, :, lanes.of(2, pair)]
            for side in range(2):
                head = 2 * pair + side
                lse = stat_row(grad_a, grad_b, (0, index), 0, head, half)
                delta = stat_row(grad_a, grad_b, (0, index), 1, head, half)
                weight = jnp.exp(scores[head] - lse)
                d_weight = dot_nt(values, d_mix[head])
                d_scores[head] = (weight * (d_weight - delta)).astype(low)
                weights[head] = weight.astype(low)
        for pair in range(pairs):
            chosen = slice(pair * LANES, (pair + 1) * LANES)
            one, two = 2 * pair, 2 * pair + 1
            dv_acc[:, chosen] += dot_nn(weights[one], d_mix[one]) + dot_nn(weights[two], d_mix[two])
            dk_acc[:, chosen] += dot_nn(d_scores[one], q_mask[one]) + dot_nn(d_scores[two], q_mask[two])

    over_units(counts, unit_refs, lanes, present(hot_own), block)
    half_a = pl.ds(pl.multiple_of(turn * half, half), half)
    half_b = pl.ds(pl.multiple_of((1 - turn) * half, half), half)
    for kind, value in enumerate((dq_in[0], dk_acc[...].astype(low), dv_acc[...].astype(low))):
        chosen = slice(kind * local, (kind + 1) * local)
        product = dot_nt(value, w_qkv[kind])
        total = product if kind == 0 else total + product
        if kind > 0:
            d_kv[0, :, (kind - 1) * local : kind * local] = value
    total = total.astype(low)
    d_input[0, half_a, :] = total[:half]
    d_input[0, half_b, :] = total[half:]


def padded(block):
    return -(-block // 16) * 16


def put_slots(turned, slots, values, owners, block):
    start = 0
    for value in values:
        turned[:, start : start + value.shape[0]] = value.astype(turned.dtype).T
        start += value.shape[0]
    room = padded(block)
    for slot in range(slots.shape[0] // room):
        source = pl.ds(pl.multiple_of(owners[slot] * block, 16 if block % 16 == 0 else 8), block)
        slots[slot * room : slot * room + block, :] = turned[source, :].astype(low)


def places_of(targets):
    return [(ref, index) for ref in targets for index in range(ref.shape[0])]


def put_blocks(product, targets, block, skip):
    for slot, (ref, index) in enumerate(places_of(targets)):
        start = slot * padded(block)
        ref[index, skip : skip + block, :] = product[start : start + block].astype(low)


def pair_grad_kernel(owners, left_a, left_b, right_a, right_b, *refs):
    targets, (turned, slots) = refs[:-2], refs[-2:]
    block = targets[0].shape[1]

    @pl.when(pl.program_id(0) == 0)
    def _():
        put_slots(turned, slots, (left_a[...], left_b[...]), owners, block)

    right = jnp.concatenate([right_a[...], right_b[...]], axis=0)
    put_blocks(dot_nn(slots[...], right), targets, block, 0)


def half_rows(part, half):
    return part[:, :half, :].reshape(part.shape[0] * half, -1)


def both_rows(value, half):
    return jnp.concatenate([half_rows(value[:, :half], half), half_rows(value[:, half:], half)], axis=0)


def query_out_grad_kernel(owners, tok_a, tok_b, d_query, d_attn_a, d_attn_b, mixed_a, mixed_b, small, *refs):
    targets, (turned, slots, turned_second, slots_second) = refs[:-4], refs[-4:]
    span, local = d_query.shape[1:]
    half = span // 2
    block = targets[0].shape[1] - STAT_ROWS
    put_slots(turned, slots, [half_rows(part, half) for part in (tok_a, tok_b)], owners, block)
    first = dot_nn(slots[...], both_rows(d_query, half)).astype(low)
    put_slots(turned_second, slots_second, [half_rows(part, half) for part in (d_attn_a, d_attn_b)], owners, block)
    mixed = jnp.concatenate([half_rows(part, half) for part in (mixed_a, mixed_b)], axis=0)
    second = dot_nn(slots_second[...], mixed).astype(low)
    for slot, (ref, index) in enumerate(places_of(targets)):
        start = slot * padded(block)
        for which, product in enumerate((first, second)):
            columns = slice(which * local, (which + 1) * local)
            ref[index, STAT_ROWS:, columns] = product[start : start + block]
        ref[index, :STAT_ROWS, :local] = jnp.zeros((STAT_ROWS, local), low)
        ref[index, :STAT_ROWS, local:] = small[owners[slot]].astype(low)


def key_value_grad_kernel(owners, tok_a, tok_b, d_kv, *refs):
    targets, (turned, slots) = refs[:-2], refs[-2:]
    half = d_kv.shape[1] // 2
    block = targets[0].shape[1]
    put_slots(turned, slots, [half_rows(part, half) for part in (tok_a, tok_b)], owners, block)
    put_blocks(dot_nn(slots[...], both_rows(d_kv, half)), targets, block, 0)


def norm_of(residual):
    center = residual - jnp.mean(residual, axis=-1, keepdims=True)
    inverse = lax.rsqrt(jnp.mean(center * center, axis=-1, keepdims=True) + 1e-06)
    return center * inverse, inverse


def norm_back(d_normal, normal, inverse):
    return inverse * (
        d_normal
        - jnp.mean(d_normal, axis=-1, keepdims=True)
        - normal * jnp.mean(d_normal * normal, axis=-1, keepdims=True)
    )


def middle_kernel(
    chunk,
    turn_ref,
    tok,
    mixed_keep,
    mixed_recv,
    lse_keep,
    w_out_own,
    w_out_oth,
    w_up_own,
    w_up_oth,
    w_down_own,
    w_down_oth,
    gain,
    shift,
    grad_out,
    out,
    d_resid,
    payload,
    active_own,
    active_oth,
    d_up_own,
    d_up_oth,
    d_ffn_out,
    normed_out,
    small,
    slope,
):
    seqs, half, width = out.shape
    rows = seqs * half
    heads = mixed_keep.shape[2] // HEAD_DIM
    keep = mixed_keep[...].reshape(rows, -1)
    recv = mixed_recv[:, :half, :].reshape(rows, -1)
    attn = dot_nn(keep, w_out_own[...]) + dot_nn(recv, w_out_oth[...])
    resid_one = tok[:, :half, :].reshape(rows, width).astype(full) + attn
    normal_one, inverse_one = norm_of(resid_one)
    gain_one, gain_two = gain[0:1, :], gain[1:2, :]
    normed = normal_one * gain_one + shift[0:1, :]
    normed_low = normed.astype(low)
    normed_out[...] = normed_low
    units = w_up_own.shape[0]
    sides = ((w_up_own, w_down_own, active_own, d_up_own), (w_up_oth, w_down_oth, active_oth, d_up_oth))
    ffn = jnp.zeros((rows, width), full)
    for which, (w_up, w_down, active_ref, _) in enumerate(sides):
        for start in range(0, units, chunk):
            part = slice(start, start + chunk)
            upward = dot_nt(normed_low, w_up[part, :])
            spread = 0.5 * (1.0 + lax.erf(upward * 0.7071067811865476))
            active = (upward * spread).astype(low)
            slope[:, which * units + start : which * units + start + chunk] = (
                spread + upward * (jnp.exp(upward * upward * -0.5) * 0.3989422804014327)
            )
            active_ref[:, part] = active
            ffn = ffn + dot_nn(active, w_down[part, :])
    normal_two, inverse_two = norm_of(normed + ffn)
    out[...] = (normal_two * gain_two + shift[1:2, :]).astype(low).reshape(seqs, half, width)
    grad = grad_out[...].reshape(rows, width).astype(full)
    small[1:2, :] = jnp.sum(grad * normal_two, axis=0, keepdims=True)
    small[3:4, :] = jnp.sum(grad, axis=0, keepdims=True)
    d_resid_two = norm_back(grad * gain_two, normal_two, inverse_two)
    d_ffn = d_resid_two.astype(low)
    d_ffn_out[...] = d_ffn
    d_normed = d_resid_two
    for which, (w_up, w_down, _, d_up_ref) in enumerate(sides):
        for start in range(0, units, chunk):
            part = slice(start, start + chunk)
            d_active = dot_nt(d_ffn, w_down[part, :])
            d_up = (d_active * slope[:, which * units + start : which * units + start + chunk]).astype(low)
            d_up_ref[:, part] = d_up
            d_normed = d_normed + dot_nn(d_up, w_up[part, :])
    small[0:1, :] = jnp.sum(d_normed * normal_one, axis=0, keepdims=True)
    small[2:3, :] = jnp.sum(d_normed, axis=0, keepdims=True)
    small[4:8, :] = jnp.zeros((4, width), full)
    d_resid_one = norm_back(d_normed * gain_one, normal_one, inverse_one)
    d_resid[...] = d_resid_one.reshape(seqs, half, width)
    d_attn = d_resid_one.astype(low)
    payload[:, :half, :] = d_attn.reshape(seqs, half, width)
    column_of = lax.broadcasted_iota(jnp.int32, (8, heads * HEAD_DIM), 1) // HEAD_DIM
    chosen = jnp.where(column_of == lax.broadcasted_iota(jnp.int32, (8, heads * HEAD_DIM), 0), 1.0, 0.0)
    deltas = []
    for mixed, w_out in ((keep, w_out_own), (recv, w_out_oth)):
        d_mixed = dot_nt(d_attn, w_out[...]).astype(low).astype(full)
        deltas.append(
            lax.dot_general(
                chosen,
                d_mixed * mixed.astype(full),
                (((1,), (1,)), ((), ())),
                precision=lax.Precision.HIGHEST,
                preferred_element_type=full,
            )
        )
    row_of = lax.broadcasted_iota(jnp.int32, (STAT_ROWS, half), 0)
    pairs = heads // 2
    for seq in range(seqs):
        for head in range(heads):
            lse_high, lse_low = two_parts(lse_keep[seq, head : head + 1, :half])
            tile = slice((head % pairs) * LANES, (head % pairs + 1) * LANES)
            row = half + 2 * (head // pairs)
            parts = [lse_high.astype(full), lse_low.astype(full)]
            for which in range(2):
                piece = deltas[which][head : head + 1, seq * half : (seq + 1) * half]
                if which == 1:
                    parts.append(mixed_recv[seq, row : row + 1, tile].astype(full))
                    parts.append(mixed_recv[seq, row + 1 : row + 2, tile].astype(full))
                parts.extend(part.astype(full) for part in two_parts(piece))
            stat = jnp.zeros((STAT_ROWS, half), full)
            for index, part in enumerate(parts):
                stat = jnp.where(row_of == index, part, stat)
            payload[seq, half:, head * LANES : (head + 1) * LANES] = stat.astype(low)


def slot_order(count):
    if count == 1:
        return [0]
    inner = slot_order(count // 2)
    return [2 * slot + 1 for slot in inner] + [2 * slot for slot in inner]


def reversed_bits(value, bits):
    return sum(((value >> bit) & 1) << (bits - 1 - bit) for bit in range(bits))


def far(value):
    return pltpu.with_memory_space_constraint(value, pltpu.HBM)


def whole(shape):
    return pl.BlockSpec(shape, lambda *_: (0,) * len(shape), pipeline_mode=pl.Buffered(1))


def kernel_params(megabytes):
    return pltpu.CompilerParams(vmem_limit_bytes=megabytes << 20, dimension_semantics=("arbitrary",))


def on_device(
    ctx_size,
    dp_size,
    tokens,
    segment_ids,
    w_qkv,
    w_out,
    w_up,
    w_down,
    norm_gain,
    norm_bias,
    grad_out,
):
    seqs, span, width = tokens.shape
    half = span // 2
    local_width = w_out.shape[0]
    heads = local_width // HEAD_DIM
    units_local = w_up.shape[0]
    rows = seqs * half
    long_half = half + STAT_ROWS
    ctx_bits = ctx_size.bit_length() - 1
    turn = lax.axis_index("tensor")
    place = lax.axis_index("ctx")
    row_place = lax.axis_index("dp")
    turn_array = turn.reshape(1)

    def room(megabytes):
        return kernel_params(megabytes if ctx_size <= 4 else 60)

    def swap(value):
        return lax.ppermute(value, "tensor", [(0, 1), (1, 0)])

    def hop(value, stage):
        moves = []
        for spot in range(ctx_size):
            for core in range(2):
                bit = stage if core == 0 else ctx_bits - 1 - stage
                moves.append((spot * 2 + core, (spot ^ (1 << bit)) * 2 + core))
        return lax.ppermute(value, ("ctx", "tensor"), moves)

    def tie(*values):
        return lax.optimization_barrier(values)

    def gather_near(own):
        own = own[:, None]
        return [hop(own, stage) for stage in range(min(ctx_bits, 2))]

    def gather_far(own, near_groups):
        groups = list(near_groups)
        if ctx_bits >= 2:
            groups.append(hop(groups[0], 1))
        for stage in range(2, ctx_bits):
            groups.append(hop(jnp.concatenate([own[:, None]] + groups, axis=1), stage))
        return groups

    def half_of(value, which):
        return lax.dynamic_slice_in_dim(value, which * half, half, 1)

    def with_ids(which):
        ids = half_of(segment_ids, which).astype(low)
        row = jnp.pad(ids[:, None, :], ((0, 0), (0, STAT_ROWS - 1), (0, width - half)))
        return jnp.concatenate([half_of(tokens, which), row], axis=1)

    def units_of(groups):
        direct, swapped = groups[: len(groups) // 2], groups[len(groups) // 2 :]
        if ctx_size == 4:
            return [(direct[0], swapped[1]), (direct[1], swapped[0]), (direct[2], swapped[2])]
        mirror = [reversed_bits(slot, ctx_bits) - 1 for slot in range(1, ctx_size)]
        first, second = jnp.concatenate(direct, axis=1), jnp.concatenate(swapped, axis=1)
        return [(first, jnp.stack([second[:, slot] for slot in mirror], axis=1))]

    block_width = 3 * local_width + LANES
    part_spec = pl.BlockSpec((seqs, 1, long_half, width), lambda g: (0, g, 0, 0))

    def project(part_a, part_b):
        count = part_a.shape[1]
        return pl.pallas_call(
            project_kernel,
            grid=(count,),
            in_specs=[whole(w_qkv.shape), part_spec, part_spec],
            out_specs=pl.BlockSpec((seqs, 1, span, block_width), lambda g: (0, g, 0, 0)),
            out_shape=jax.ShapeDtypeStruct((seqs, count, span, block_width), low),
            compiler_params=room(16),
            name="project",
        )(w_qkv, part_a, part_b)

    tok_a, tok_b = with_ids(turn), with_ids(1 - turn)
    tok_near = gather_near(tok_a)
    w_out_oth, w_up_oth, w_down_oth = swap(w_out), swap(w_up), swap(w_down)
    own = project(tok_a[:, None], tok_b[:, None])

    def seq_spec(shape):
        return pl.BlockSpec((1,) + shape, lambda s, *_: (s,) + (0,) * len(shape))

    def unit_specs(chosen):
        return [
            pl.BlockSpec(
                (1,) + value.shape[1:],
                lambda s, *_: (s, 0, 0, 0),
                pipeline_mode=pl.Buffered(2 if value.shape[1] == 1 else 1),
            )
            for value in chosen
        ]

    head_square = pltpu.VMEM((heads, span, span), full)
    head_square_low = pltpu.VMEM((heads, span, span), low)
    q_scratch = pltpu.VMEM((heads, span, 2 * LANES), low)
    head_rows = pltpu.VMEM((heads, span, LANES), low)

    def attend(chosen, state, finish):
        begin = state is None
        state_shapes = [((local_width, span), full), ((16, span), full)]
        shapes = (
            [((half, local_width), low), ((long_half, local_width), low), ((8, span), full)]
            if finish
            else state_shapes
        )
        state = [] if begin else list(state)
        return pl.pallas_call(
            functools.partial(attend_kernel, [value.shape[1] for value in chosen], heads, begin, finish),
            grid=(seqs,),
            in_specs=unit_specs([own] + chosen) + [seq_spec(value.shape[1:]) for value in state],
            out_specs=[seq_spec(shape) for shape, _ in shapes],
            out_shape=[
                (pltpu.HBM if finish else jax.ShapeDtypeStruct)((seqs,) + shape, kind) for shape, kind in shapes
            ],
            scratch_shapes=[
                q_scratch,
                head_square,
                head_square_low,
                pltpu.VMEM((16, span), full),
                pltpu.VMEM((local_width, span), full),
            ],
            compiler_params=room(14),
            name="attend",
        )(own, *chosen, *state)

    state = attend([], None, False)
    *tok_near, first_state = tie(*tok_near, state[0])
    state = (first_state, state[1])
    tok_groups = gather_far(tok_a, tok_near)
    if ctx_size == 4:
        swapped = [swap(group) for group in tok_groups[:2]]
        near_units = [project(tok_groups[0], swapped[1]), project(tok_groups[1], swapped[0])]
        state = attend(near_units, state, False)
        last, first_state = tie(tok_groups[2], state[0])
        far_units = [project(last, swap(last))]
        units = near_units + far_units
        mixed_keep, mixed_send, lse = attend(far_units, (first_state, state[1]), True)
    else:
        units = [project(*pair) for pair in units_of(tok_groups + [swap(group) for group in tok_groups])]
        mixed_keep, mixed_send, lse = attend(units, state, True)
    mixed_recv = swap(mixed_send)

    middle_in = [
        tok_a,
        mixed_keep,
        mixed_recv,
        lse,
        w_out,
        w_out_oth,
        w_up,
        w_up_oth,
        w_down,
        w_down_oth,
        norm_gain,
        norm_bias,
    ]
    middle_shapes = [
        ((seqs, half, width), low),
        ((seqs, half, width), full),
        ((seqs, long_half, width), low),
        ((rows, units_local), low),
        ((rows, units_local), low),
        ((rows, units_local), low),
        ((rows, units_local), low),
        ((rows, width), low),
        ((rows, width), low),
        ((8, width), full),
    ]
    (
        out_half,
        d_resid,
        payload,
        active_own,
        active_oth,
        d_up_own,
        d_up_oth,
        d_ffn,
        normed_low,
        small,
    ) = pl.pallas_call(
        functools.partial(middle_kernel, min(512, units_local)),
        grid_spec=pltpu.PrefetchScalarGridSpec(
            num_scalar_prefetch=1,
            grid=(1,),
            in_specs=[whole(value.shape) for value in middle_in]
            + [pl.BlockSpec((seqs, half, width), lambda s, turn_ref: (0, turn_ref[0], 0))],
            out_specs=[whole(shape) for shape, _ in middle_shapes],
            scratch_shapes=[pltpu.VMEM((rows, 2 * units_local), full)],
        ),
        out_shape=[
            (jax.ShapeDtypeStruct if number == 2 else pltpu.HBM)(shape, kind)
            for number, (shape, kind) in enumerate(middle_shapes)
        ],
        compiler_params=room(36),
        name="middle",
    )(turn_array, *middle_in, grad_out)

    order = slot_order(ctx_size)
    mirrored = [reversed_bits(slot, ctx_bits) for slot in order]
    owners = place ^ jnp.where(turn == 0, jnp.array(order, jnp.int32), jnp.array(mirrored, jnp.int32))
    quarter = width // ctx_size
    stages = [ctx_size >> (stage + 1) for stage in range(ctx_bits)] + [1]
    turned_kind = low if quarter % 16 == 0 else full
    chunk = min(512, units_local)

    def slot_scratch(count):
        return [pltpu.VMEM((width, count), turned_kind), pltpu.VMEM((ctx_size * padded(quarter), count), low)]

    def pair_grad(left_a, left_b, right_a, right_b, name):
        right_spec = pl.BlockSpec((rows, chunk), lambda n, *_: (0, n))
        return pl.pallas_call(
            pair_grad_kernel,
            grid_spec=pltpu.PrefetchScalarGridSpec(
                num_scalar_prefetch=1,
                grid=(units_local // chunk,),
                in_specs=[whole(left_a.shape), whole(left_b.shape), right_spec, right_spec],
                out_specs=[pl.BlockSpec((count, quarter, chunk), lambda n, *_: (0, 0, n)) for count in stages],
                scratch_shapes=slot_scratch(2 * rows),
            ),
            out_shape=[pltpu.HBM((count, quarter, units_local), low) for count in stages],
            compiler_params=room(16),
            name=name,
        )(owners, left_a, left_b, right_a, right_b)

    parity = row_place & 1

    def add_up(values):
        return sum(value.astype(full) for value in values)

    def send_stage(parts, gots, stage):
        count, start = parts[stage].shape[0], 0
        values = [parts[stage]]
        for got in gots:
            start = got.shape[0] - sum(part.shape[0] for part in parts[stage:])
            values.append(got[start : start + count])
        return add_up(values).astype(low)

    def own_half(parts, gots, which):
        values = [parts[-1]] + gots
        split = parts[-1].shape[1] // 2
        return add_up(
            [
                lax.dynamic_slice(value, (value.shape[0] - 1, which * split, 0), (1, split, value.shape[2]))
                for value in values
            ]
        )[0]

    class Blocks:
        def __init__(self, parts):
            self.parts, self.gots, self.stage, self.sent = list(parts), [], 0, None
            self.dp_stage, self.got = 0, None

        @property
        def arrived(self):
            return self.gots[-1] if self.dp_stage == 0 else self.got

        @arrived.setter
        def arrived(self, value):
            if self.dp_stage == 0:
                self.gots[-1] = value
            else:
                self.got = value

        def ready(self):
            if self.stage < ctx_bits:
                self.sent = send_stage(self.parts, self.gots, self.stage) if self.stage else self.parts[0]
            elif self.dp_stage == 0:
                self.sent = own_half(self.parts, self.gots, 1 - parity).astype(low)
            else:
                mine = own_half(self.parts, self.gots, parity) if self.dp_stage == 1 else self.sent.astype(full)
                self.sent = (mine + self.got.astype(full)).astype(low)

        def send(self):
            if self.stage < ctx_bits:
                self.gots.append(hop(self.sent, self.stage))
                self.stage += 1
                return
            last = self.dp_stage == dp_size.bit_length() - 1
            bit = 0 if last else self.dp_stage
            moves = [(spot, spot ^ (1 << bit)) for spot in range(dp_size)]
            self.got = lax.ppermute(self.sent, "dp", moves)
            self.dp_stage += 1

        def advance(self):
            self.ready()
            self.send()

        def total(self):
            while self.dp_stage < dp_size.bit_length():
                self.advance()
            mine, other = self.sent, self.got
            return jnp.where(
                parity == 0, jnp.concatenate([mine, other], axis=0), jnp.concatenate([other, mine], axis=0)
            ).astype(full)

    grad_near = gather_near(payload)
    payload_b = swap(payload)
    d_ffn_b, active_b = swap(d_ffn), swap(active_oth)
    normed_b, d_up_b = swap(normed_low), swap(d_up_oth)
    down = Blocks(pair_grad(d_ffn, d_ffn_b, active_own, active_b, "grad_down"))
    down.advance()
    up = Blocks(pair_grad(normed_low, normed_b, d_up_own, d_up_b, "grad_up"))
    *grad_near, up.parts[0], own_back = tie(*grad_near, up.parts[0], own)
    up.advance()
    grad_far = gather_far(payload, grad_near)
    grad_groups = grad_far + [swap(group) for group in grad_far]

    sum_shape = pltpu.HBM((seqs, span, local_width), full)
    row_shape = pltpu.HBM((seqs, span, local_width), low)
    grad_spec = seq_spec((long_half, width))
    span_spec = seq_spec((span, local_width))
    counts = [value.shape[1] for value in units]
    d_query, dk_sum, dv_sum = pl.pallas_call(
        functools.partial(query_grad_kernel, counts, heads),
        grid=(seqs,),
        in_specs=unit_specs([own]) + [grad_spec, grad_spec, whole(w_out.shape)] + unit_specs(units),
        out_specs=[span_spec] * 3,
        out_shape=[row_shape, sum_shape, sum_shape],
        scratch_shapes=[
            q_scratch,
            head_rows,
            pltpu.VMEM((16, span), full),
            head_square,
            head_square_low,
            head_square_low,
            pltpu.VMEM((local_width, span), full),
        ],
        compiler_params=room(20),
        name="query_grad",
    )(own_back, payload, payload_b, far(w_out), *units)

    def sequence_grad(kernel, values, lefts, extra, columns, name):
        return Blocks(
            pl.pallas_call(
                kernel,
                grid_spec=pltpu.PrefetchScalarGridSpec(
                    num_scalar_prefetch=1,
                    grid=(1,),
                    in_specs=[whole(value.shape) for value in values],
                    out_specs=[whole((count, extra + quarter, columns)) for count in stages],
                    scratch_shapes=slot_scratch(seqs * span) * lefts,
                ),
                out_shape=[pltpu.HBM((count, extra + quarter, columns), low) for count in stages],
                compiler_params=room(20),
                name=name,
            )(owners, *values)
        )

    small_rows = (small[:4] + swap(small)[:4]).reshape(4, ctx_size, quarter).transpose(1, 0, 2)
    small_rows = jnp.pad(small_rows, ((0, 0), (0, STAT_ROWS - 4), (0, local_width - quarter)))
    d_query, down.arrived = tie(d_query, down.arrived)
    down.advance()
    query_out = sequence_grad(
        query_out_grad_kernel,
        (tok_a, tok_b, d_query, payload, payload_b, mixed_keep, mixed_send, small_rows),
        2,
        STAT_ROWS,
        2 * local_width,
        "query_out_grad",
    )
    query_out.parts[0], d_query = tie(query_out.parts[0], d_query)
    query_out.advance()
    grad_units = units_of(grad_groups)
    grad_a, grad_b = [pair[0] for pair in grad_units], [pair[1] for pair in grad_units]
    d_kv, d_input = pl.pallas_call(
        functools.partial(key_grad_kernel, counts, heads),
        grid_spec=pltpu.PrefetchScalarGridSpec(
            num_scalar_prefetch=1,
            grid=(seqs,),
            in_specs=unit_specs([own])
            + [span_spec] * 3
            + [whole(w_out.shape), whole(w_qkv.shape)]
            + unit_specs(units + grad_a + grad_b),
            out_specs=[seq_spec((span, 2 * local_width)), seq_spec((span, width))],
            scratch_shapes=[
                pltpu.VMEM((heads // 2, span, 2 * LANES), low),
                head_rows,
                head_rows,
                head_square,
                head_square_low,
                head_square_low,
                pltpu.VMEM((span, local_width), full),
                pltpu.VMEM((span, local_width), full),
            ],
        ),
        out_shape=[
            jax.ShapeDtypeStruct((seqs, span, 2 * local_width), low),
            jax.ShapeDtypeStruct((seqs, span, width), low),
        ],
        compiler_params=room(26),
        name="key_grad",
    )(turn_array, own, *map(far, (d_query, dk_sum, dv_sum, w_out, w_qkv)), *units, *grad_a, *grad_b)

    d_kv, down.arrived, up.arrived = tie(d_kv, down.arrived, up.arrived)
    down.advance()
    up.advance()
    key_value = sequence_grad(key_value_grad_kernel, (tok_a, tok_b, d_kv), 1, 0, 2 * local_width, "key_value_grad")
    key_value.parts[0], query_out.arrived = tie(key_value.parts[0], query_out.arrived)
    key_value.advance()
    query_out.advance()

    def both_halves(mine):
        other = swap(mine)
        return jnp.where(
            turn == 0, jnp.concatenate([mine, other], axis=1), jnp.concatenate([other, mine], axis=1)
        )

    outputs = both_halves(out_half)
    grad_tokens = d_input.astype(full) + swap(d_input).astype(full) + both_halves(d_resid)

    down_total, up_total = down.total(), up.total()
    query_out_total, key_value_total = query_out.total(), key_value.total()
    small_total = query_out_total[:4, local_width : local_width + quarter]
    query_out_total = query_out_total[STAT_ROWS:]
    return (
        outputs,
        grad_tokens,
        jnp.stack(
            [query_out_total[:, :local_width], key_value_total[:, :local_width], key_value_total[:, local_width:]]
        ),
        query_out_total[:, local_width:].T,
        up_total.T,
        down_total.T,
        small_total[0:2],
        small_total[2:4],
    )


def solution(mesh):
    return jax.shard_map(
        functools.partial(on_device, mesh.shape["ctx"], mesh.shape["dp"]),
        mesh=mesh,
        in_specs=(
            P("dp", "ctx", None),
            P("dp", "ctx"),
            P(None, None, "tensor"),
            P("tensor", None),
            P("tensor", None),
            P("tensor", None),
            P(),
            P(),
            P("dp", "ctx", None),
        ),
        out_specs=(
            P("dp", "ctx", None),
            P("dp", "ctx", None),
            P(None, "ctx", "tensor"),
            P("tensor", "ctx"),
            P("tensor", "ctx"),
            P("tensor", "ctx"),
            P(None, "ctx"),
            P(None, "ctx"),
        ),
        check_vma=False,
    )
```

```python
import functools
import jax
import jax.numpy as jnp
from jax import lax
from jax.experimental import pallas as pl
from jax.experimental.pallas import tpu as pltpu
from jax.sharding import PartitionSpec as P

HEAD_DIM = 64
LANES = 128
STAT_ROWS = 16
BIG = 2.0**30
low, full = jnp.bfloat16, jnp.float32


def dot_nn(left, right):
    return lax.dot_general(left, right, (((1,), (0,)), ((), ())), preferred_element_type=full)


def dot_nt(left, right):
    return lax.dot_general(left, right, (((1,), (1,)), ((), ())), preferred_element_type=full)


def dot_tn(left, right):
    return lax.dot_general(left, right, (((0,), (0,)), ((), ())), preferred_element_type=full)


def two_parts(values):
    high = values.astype(low)
    return high, (values - high.astype(full)).astype(low)


def project_kernel(w_qkv, part_a, part_b, out):
    seqs, half = part_a.shape[0], part_a.shape[2] - STAT_ROWS
    local = w_qkv.shape[2]
    rows = jnp.concatenate(
        [part[seq, 0, :half, :] for seq in range(seqs) for part in (part_a, part_b)], axis=0
    )
    for kind in range(3):
        product = dot_nn(rows, w_qkv[kind])
        if kind == 0:
            product = product * 0.125
        out[:, 0, :, kind * local : (kind + 1) * local] = product.astype(low).reshape(seqs, 2 * half, local)
    ids = lax.broadcasted_iota(jnp.int32, (LANES, half), 0).astype(full)
    for seq in range(seqs):
        for which, part in enumerate((part_a, part_b)):
            row = part[seq, 0, half : half + 1, :half].astype(full)
            out[seq, 0, which * half : (which + 1) * half, 3 * local :] = (
                jnp.where(ids == row, 1.0, 0.0).T.astype(low)
            )


class Lanes:
    def __init__(self, heads):
        self.local = heads * HEAD_DIM

    def of(self, kind, pair):
        start = kind * self.local + pair * LANES
        return slice(start, start + LANES)

    @property
    def hot(self):
        return slice(3 * self.local, 3 * self.local + LANES)


def split_heads(value):
    left = lax.broadcasted_iota(jnp.int32, value.shape, 1) < HEAD_DIM
    zero = jnp.zeros_like(value)
    return jnp.where(left, value, zero), jnp.where(left, zero, value)


def present(hot):
    return jnp.max(hot.astype(full), axis=0, keepdims=True)


def over_units(counts, unit_refs, lanes, own_ids, body):
    flags = [
        jnp.max(own_ids * present(ref[0, 0, :, lanes.hot])) > 0.0 if count == 1 else None
        for count, ref in zip(counts, unit_refs)
    ]
    for number, (count, ref) in enumerate(zip(counts, unit_refs)):
        if count == 1:
            pl.when(flags[number])(functools.partial(body, number, 0))
        else:

            def step(index, carry, number=number, ref=ref):
                shared = jnp.max(own_ids * present(ref[0, index, :, lanes.hot])) > 0.0
                pl.when(shared)(functools.partial(body, number, index))
                return carry

            lax.fori_loop(0, count, step, 0)


def attend_kernel(counts, heads, begin, finish, *refs):
    lanes, pairs, units = Lanes(heads), heads // 2, len(counts)
    own, unit_refs = refs[0], refs[1 : 1 + units]
    refs = refs[1 + units :]
    if not begin:
        acc_in, stat_in = refs[:2]
        refs = refs[2:]
    if finish:
        mixed_keep, mixed_send, lse_out = refs[:3]
        refs = refs[3:]
    else:
        acc_out, stat_out = refs[:2]
        refs = refs[2:]
    q_aug, scores, weights, stat, acc = refs
    span = own.shape[2]
    half = span // 2
    hot_own = own[0, 0, :, lanes.hot]
    penalty = ((hot_own.astype(full) - 1.0) * BIG).astype(low)
    for pair in range(pairs):
        for side, masked in enumerate(split_heads(own[0, 0, :, lanes.of(0, pair)])):
            q_aug[2 * pair + side] = jnp.concatenate([masked, penalty], axis=1)
    if not begin:
        acc[...] = acc_in[0]
        stat[...] = stat_in[0]

    def block(ref, index, first):
        hot = ref[0, index, :, lanes.hot]
        peaks = []
        for pair in range(pairs):
            k_aug = jnp.concatenate([ref[0, index, :, lanes.of(1, pair)], hot], axis=1)
            for side in range(2):
                head = 2 * pair + side
                product = dot_nt(k_aug, q_aug[head])
                scores[head] = product
                peak = jnp.max(product, axis=0, keepdims=True)
                peaks.append(peak if first else jnp.maximum(peak, stat[head : head + 1, :]))
        sums = []
        for head in range(heads):
            weight = jnp.exp(scores[head] - peaks[head])
            sums.append(jnp.sum(weight, axis=0, keepdims=True))
            weights[head] = weight.astype(low)
        for pair in range(pairs):
            turned = ref[0, index, :, lanes.of(2, pair)].T
            for side in range(2):
                head = 2 * pair + side
                rows = slice(head * HEAD_DIM, (head + 1) * HEAD_DIM)
                mix = dot_nn(turned[side * HEAD_DIM : (side + 1) * HEAD_DIM], weights[head])
                total = sums[head]
                if not first:
                    shrink = jnp.exp(stat[head : head + 1, :] - peaks[head])
                    total = total + stat[8 + head : 9 + head, :] * shrink
                    mix = mix + acc[rows, :] * shrink
                acc[rows, :] = mix
                stat[head : head + 1, :] = peaks[head]
                stat[8 + head : 9 + head, :] = total

    if begin:
        block(own, 0, True)
    over_units(
        counts, unit_refs, lanes, present(hot_own), lambda number, index: block(unit_refs[number], index, False)
    )
    if not finish:
        acc_out[0] = acc[...]
        stat_out[0] = stat[...]
        return
    totals = stat[8 : 8 + heads, :]
    lse = stat[0:heads, :] + jnp.log(totals)
    lse_out[0, 0:heads, :] = lse
    lse_out[0, heads:8, :] = jnp.zeros((8 - heads, span), full)
    scale = 1.0 / totals
    for pair in range(pairs):
        chosen = slice(pair * LANES, (pair + 1) * LANES)
        mixed = jnp.concatenate(
            [
                acc[head * HEAD_DIM : (head + 1) * HEAD_DIM, :] * scale[head : head + 1, :]
                for head in (2 * pair, 2 * pair + 1)
            ],
            axis=0,
        ).T.astype(low)
        mixed_keep[0, :, chosen] = mixed[:half]
        mixed_send[0, :half, chosen] = mixed[half:]
    row_of = lax.broadcasted_iota(jnp.int32, (STAT_ROWS, half), 0)
    for column in range(pairs):
        tile = jnp.zeros((STAT_ROWS, half), full)
        for which in range(2):
            row = lse[which * pairs + column : which * pairs + column + 1, half:]
            for kind, part in enumerate(two_parts(row)):
                tile = jnp.where(row_of == kind + 2 * which, part.astype(full), tile)
        mixed_send[0, half:, column * LANES : (column + 1) * LANES] = tile.astype(low)


def stat_row(grad_a, grad_b, at, kind, head, half):
    tile = slice(head * LANES, (head + 1) * LANES)
    parts = []
    for other, ref in enumerate((grad_a, grad_b)):
        row = half + 2 * kind + 4 * other
        parts.append(
            ref[at + (slice(row, row + 1), tile)].astype(full)
            + ref[at + (slice(row + 1, row + 2), tile)].astype(full)
        )
    return jnp.concatenate(parts, axis=1)


def query_grad_kernel(counts, heads, *refs):
    lanes, pairs, units = Lanes(heads), heads // 2, len(counts)
    own, grad_a, grad_b, w_out = refs[:4]
    unit_refs = refs[4 : 4 + units]
    dq_out, dk_out, dv_out, q_aug, d_mix, rows_of, scores, weights, d_scores, acc = refs[4 + units :]
    span = own.shape[2]
    half = span // 2
    hot_own = own[0, 0, :, lanes.hot]
    penalty = ((hot_own.astype(full) - 1.0) * BIG).astype(low)
    d_attn = jnp.concatenate([grad_a[0, :half, :], grad_b[0, :half, :]], axis=0)
    d_mixed = dot_nt(d_attn, w_out[...]).astype(low)
    for pair in range(pairs):
        q_parts = split_heads(own[0, 0, :, lanes.of(0, pair)])
        d_parts = split_heads(d_mixed[:, pair * LANES : (pair + 1) * LANES])
        for side in range(2):
            head = 2 * pair + side
            q_aug[head] = jnp.concatenate([q_parts[side], penalty], axis=1)
            d_mix[head] = d_parts[side]
            rows_of[head : head + 1, :] = stat_row(grad_a, grad_b, (0,), 0, head, half)
            rows_of[8 + head : 9 + head, :] = stat_row(grad_a, grad_b, (0,), 1, head, half)

    def block(ref, index, first):
        hot = ref[0, index, :, lanes.hot]
        for pair in range(pairs):
            k_aug = jnp.concatenate([ref[0, index, :, lanes.of(1, pair)], hot], axis=1)
            for side in range(2):
                head = 2 * pair + side
                scores[head] = dot_nt(k_aug, q_aug[head])
        for pair in range(pairs):
            values = ref[0, index, :, lanes.of(2, pair)]
            for side in range(2):
                head = 2 * pair + side
                weight = jnp.exp(scores[head] - rows_of[head : head + 1, :])
                d_weight = dot_nt(values, d_mix[head])
                d_scores[head] = (weight * (d_weight - rows_of[8 + head : 9 + head, :])).astype(low)
                if first:
                    weights[head] = weight.astype(low)
        for pair in range(pairs):
            turned = ref[0, index, :, lanes.of(1, pair)].T
            for side in range(2):
                head = 2 * pair + side
                rows = slice(head * HEAD_DIM, (head + 1) * HEAD_DIM)
                product = dot_nn(turned[side * HEAD_DIM : (side + 1) * HEAD_DIM], d_scores[head])
                acc[rows, :] = product if first else acc[rows, :] + product
            if first:
                chosen = slice(pair * LANES, (pair + 1) * LANES)
                one, two = 2 * pair, 2 * pair + 1
                dv_out[0, :, chosen] = dot_nn(weights[one], d_mix[one]) + dot_nn(weights[two], d_mix[two])
                dk_out[0, :, chosen] = dot_nn(d_scores[one], q_aug[one, :, :LANES]) + dot_nn(
                    d_scores[two], q_aug[two, :, :LANES]
                )

    block(own, 0, True)
    over_units(
        counts, unit_refs, lanes, present(hot_own), lambda number, index: block(unit_refs[number], index, False)
    )
    for pair in range(pairs):
        chosen = slice(pair * LANES, (pair + 1) * LANES)
        dq_out[0, :, chosen] = (acc[chosen, :] * 0.125).T.astype(low)


def key_grad_kernel(counts, heads, turn_ref, *refs):
    lanes, pairs, units = Lanes(heads), heads // 2, len(counts)
    own, dq_in, dk_in, dv_in, w_out, w_qkv = refs[:6]
    unit_refs = refs[6 : 6 + units]
    a_refs = refs[6 + units : 6 + 2 * units]
    b_refs = refs[6 + 2 * units : 6 + 3 * units]
    d_kv, d_input, k_aug, q_mask, d_mix, scores, weights, d_scores, dk_acc, dv_acc = refs[6 + 3 * units :]
    span = own.shape[2]
    half = span // 2
    local = lanes.local
    turn = turn_ref[0]
    hot_own = own[0, 0, :, lanes.hot]
    for pair in range(pairs):
        k_aug[pair] = jnp.concatenate([own[0, 0, :, lanes.of(1, pair)], hot_own], axis=1)
    dk_acc[...] = dk_in[0]
    dv_acc[...] = dv_in[0]

    def block(number, index):
        ref, grad_a, grad_b = unit_refs[number], a_refs[number], b_refs[number]
        penalty = ((ref[0, index, :, lanes.hot].astype(full) - 1.0) * BIG).astype(low)
        d_attn = jnp.concatenate([grad_a[0, index, :half, :], grad_b[0, index, :half, :]], axis=0)
        d_mixed = dot_nt(d_attn, w_out[...]).astype(low)
        for pair in range(pairs):
            q_parts = split_heads(ref[0, index, :, lanes.of(0, pair)])
            d_parts = split_heads(d_mixed[:, pair * LANES : (pair + 1) * LANES])
            for side in range(2):
                head = 2 * pair + side
                q_mask[head] = q_parts[side]
                d_mix[head] = d_parts[side]
                scores[head] = dot_nt(k_aug[pair], jnp.concatenate([q_parts[side], penalty], axis=1))
        for pair in range(pairs):
            values = own[0, 0, :, lanes.of(2, pair)]
            for side in range(2):
                head = 2 * pair + side
                lse = stat_row(grad_a, grad_b, (0, index), 0, head, half)
                delta = stat_row(grad_a, grad_b, (0, index), 1, head, half)
                weight = jnp.exp(scores[head] - lse)
                d_weight = dot_nt(values, d_mix[head])
                d_scores[head] = (weight * (d_weight - delta)).astype(low)
                weights[head] = weight.astype(low)
        for pair in range(pairs):
            chosen = slice(pair * LANES, (pair + 1) * LANES)
            one, two = 2 * pair, 2 * pair + 1
            dv_acc[:, chosen] += dot_nn(weights[one], d_mix[one]) + dot_nn(weights[two], d_mix[two])
            dk_acc[:, chosen] += dot_nn(d_scores[one], q_mask[one]) + dot_nn(d_scores[two], q_mask[two])

    over_units(counts, unit_refs, lanes, present(hot_own), block)
    half_a = pl.ds(pl.multiple_of(turn * half, half), half)
    half_b = pl.ds(pl.multiple_of((1 - turn) * half, half), half)
    for kind, value in enumerate((dq_in[0], dk_acc[...].astype(low), dv_acc[...].astype(low))):
        chosen = slice(kind * local, (kind + 1) * local)
        product = dot_nt(value, w_qkv[kind])
        total = product if kind == 0 else total + product
        if kind > 0:
            d_kv[0, :, (kind - 1) * local : kind * local] = value
    total = total.astype(low)
    d_input[0, half_a, :] = total[:half]
    d_input[0, half_b, :] = total[half:]


def padded(block):
    return -(-block // 16) * 16


def put_slots(turned, slots, values, owners, block):
    start = 0
    for value in values:
        turned[:, start : start + value.shape[0]] = value.astype(turned.dtype).T
        start += value.shape[0]
    room = padded(block)
    for slot in range(slots.shape[0] // room):
        source = pl.ds(pl.multiple_of(owners[slot] * block, 16 if block % 16 == 0 else 8), block)
        slots[slot * room : slot * room + block, :] = turned[source, :].astype(low)


def places_of(targets):
    return [(ref, index) for ref in targets for index in range(ref.shape[0])]


def put_blocks(product, targets, block, skip):
    for slot, (ref, index) in enumerate(places_of(targets)):
        start = slot * padded(block)
        ref[index, skip : skip + block, :] = product[start : start + block].astype(low)


def pair_grad_kernel(owners, left_a, left_b, right_a, right_b, *refs):
    targets, (turned, slots) = refs[:-2], refs[-2:]
    block = targets[0].shape[1]

    @pl.when(pl.program_id(0) == 0)
    def _():
        put_slots(turned, slots, (left_a[...], left_b[...]), owners, block)

    right = jnp.concatenate([right_a[...], right_b[...]], axis=0)
    put_blocks(dot_nn(slots[...], right), targets, block, 0)


def half_rows(part, half):
    return part[:, :half, :].reshape(part.shape[0] * half, -1)


def both_rows(value, half):
    return jnp.concatenate([half_rows(value[:, :half], half), half_rows(value[:, half:], half)], axis=0)


def query_out_grad_kernel(owners, tok_a, tok_b, d_query, d_attn_a, d_attn_b, mixed_a, mixed_b, small, *refs):
    targets, (turned, slots, turned_second, slots_second) = refs[:-4], refs[-4:]
    span, local = d_query.shape[1:]
    half = span // 2
    block = targets[0].shape[1] - STAT_ROWS
    put_slots(turned, slots, [half_rows(part, half) for part in (tok_a, tok_b)], owners, block)
    first = dot_nn(slots[...], both_rows(d_query, half)).astype(low)
    put_slots(turned_second, slots_second, [half_rows(part, half) for part in (d_attn_a, d_attn_b)], owners, block)
    mixed = jnp.concatenate([half_rows(part, half) for part in (mixed_a, mixed_b)], axis=0)
    second = dot_nn(slots_second[...], mixed).astype(low)
    for slot, (ref, index) in enumerate(places_of(targets)):
        start = slot * padded(block)
        for which, product in enumerate((first, second)):
            columns = slice(which * local, (which + 1) * local)
            ref[index, STAT_ROWS:, columns] = product[start : start + block]
        ref[index, :STAT_ROWS, :local] = jnp.zeros((STAT_ROWS, local), low)
        ref[index, :STAT_ROWS, local:] = small[owners[slot]].astype(low)


def key_value_grad_kernel(owners, tok_a, tok_b, d_kv, *refs):
    targets, (turned, slots) = refs[:-2], refs[-2:]
    half = d_kv.shape[1] // 2
    block = targets[0].shape[1]
    put_slots(turned, slots, [half_rows(part, half) for part in (tok_a, tok_b)], owners, block)
    put_blocks(dot_nn(slots[...], both_rows(d_kv, half)), targets, block, 0)


def norm_of(residual):
    center = residual - jnp.mean(residual, axis=-1, keepdims=True)
    inverse = lax.rsqrt(jnp.mean(center * center, axis=-1, keepdims=True) + 1e-06)
    return center * inverse, inverse


def norm_back(d_normal, normal, inverse):
    return inverse * (
        d_normal
        - jnp.mean(d_normal, axis=-1, keepdims=True)
        - normal * jnp.mean(d_normal * normal, axis=-1, keepdims=True)
    )


def middle_kernel(
    chunk,
    turn_ref,
    tok,
    mixed_keep,
    mixed_recv,
    lse_keep,
    w_out_own,
    w_out_oth,
    w_up_own,
    w_up_oth,
    w_down_own,
    w_down_oth,
    gain,
    shift,
    grad_out,
    out,
    d_resid,
    payload,
    active_own,
    active_oth,
    d_up_own,
    d_up_oth,
    d_ffn_out,
    normed_out,
    small,
    slope,
):
    seqs, half, width = out.shape
    rows = seqs * half
    heads = mixed_keep.shape[2] // HEAD_DIM
    keep = mixed_keep[...].reshape(rows, -1)
    recv = mixed_recv[:, :half, :].reshape(rows, -1)
    attn = dot_nn(keep, w_out_own[...]) + dot_nn(recv, w_out_oth[...])
    resid_one = tok[:, :half, :].reshape(rows, width).astype(full) + attn
    normal_one, inverse_one = norm_of(resid_one)
    gain_one, gain_two = gain[0:1, :], gain[1:2, :]
    normed = normal_one * gain_one + shift[0:1, :]
    normed_low = normed.astype(low)
    normed_out[...] = normed_low
    units = w_up_own.shape[0]
    sides = ((w_up_own, w_down_own, active_own, d_up_own), (w_up_oth, w_down_oth, active_oth, d_up_oth))
    ffn = jnp.zeros((rows, width), full)
    for which, (w_up, w_down, active_ref, _) in enumerate(sides):
        for start in range(0, units, chunk):
            part = slice(start, start + chunk)
            upward = dot_nt(normed_low, w_up[part, :])
            spread = 0.5 * (1.0 + lax.erf(upward * 0.7071067811865476))
            active = (upward * spread).astype(low)
            slope[:, which * units + start : which * units + start + chunk] = (
                spread + upward * (jnp.exp(upward * upward * -0.5) * 0.3989422804014327)
            )
            active_ref[:, part] = active
            ffn = ffn + dot_nn(active, w_down[part, :])
    normal_two, inverse_two = norm_of(normed + ffn)
    out[...] = (normal_two * gain_two + shift[1:2, :]).astype(low).reshape(seqs, half, width)
    grad = grad_out[...].reshape(rows, width).astype(full)
    small[1:2, :] = jnp.sum(grad * normal_two, axis=0, keepdims=True)
    small[3:4, :] = jnp.sum(grad, axis=0, keepdims=True)
    d_resid_two = norm_back(grad * gain_two, normal_two, inverse_two)
    d_ffn = d_resid_two.astype(low)
    d_ffn_out[...] = d_ffn
    d_normed = d_resid_two
    for which, (w_up, w_down, _, d_up_ref) in enumerate(sides):
        for start in range(0, units, chunk):
            part = slice(start, start + chunk)
            d_active = dot_nt(d_ffn, w_down[part, :])
            d_up = (d_active * slope[:, which * units + start : which * units + start + chunk]).astype(low)
            d_up_ref[:, part] = d_up
            d_normed = d_normed + dot_nn(d_up, w_up[part, :])
    small[0:1, :] = jnp.sum(d_normed * normal_one, axis=0, keepdims=True)
    small[2:3, :] = jnp.sum(d_normed, axis=0, keepdims=True)
    small[4:8, :] = jnp.zeros((4, width), full)
    d_resid_one = norm_back(d_normed * gain_one, normal_one, inverse_one)
    d_resid[...] = d_resid_one.reshape(seqs, half, width)
    d_attn = d_resid_one.astype(low)
    payload[:, :half, :] = d_attn.reshape(seqs, half, width)
    column_of = lax.broadcasted_iota(jnp.int32, (8, heads * HEAD_DIM), 1) // HEAD_DIM
    chosen = jnp.where(column_of == lax.broadcasted_iota(jnp.int32, (8, heads * HEAD_DIM), 0), 1.0, 0.0)
    deltas = []
    for mixed, w_out in ((keep, w_out_own), (recv, w_out_oth)):
        d_mixed = dot_nt(d_attn, w_out[...]).astype(low).astype(full)
        deltas.append(
            lax.dot_general(
                chosen,
                d_mixed * mixed.astype(full),
                (((1,), (1,)), ((), ())),
                precision=lax.Precision.HIGHEST,
                preferred_element_type=full,
            )
        )
    row_of = lax.broadcasted_iota(jnp.int32, (STAT_ROWS, half), 0)
    pairs = heads // 2
    for seq in range(seqs):
        for head in range(heads):
            lse_high, lse_low = two_parts(lse_keep[seq, head : head + 1, :half])
            tile = slice((head % pairs) * LANES, (head % pairs + 1) * LANES)
            row = half + 2 * (head // pairs)
            parts = [lse_high.astype(full), lse_low.astype(full)]
            for which in range(2):
                piece = deltas[which][head : head + 1, seq * half : (seq + 1) * half]
                if which == 1:
                    parts.append(mixed_recv[seq, row : row + 1, tile].astype(full))
                    parts.append(mixed_recv[seq, row + 1 : row + 2, tile].astype(full))
                parts.extend(part.astype(full) for part in two_parts(piece))
            stat = jnp.zeros((STAT_ROWS, half), full)
            for index, part in enumerate(parts):
                stat = jnp.where(row_of == index, part, stat)
            payload[seq, half:, head * LANES : (head + 1) * LANES] = stat.astype(low)


def slot_order(count):
    if count == 1:
        return [0]
    inner = slot_order(count // 2)
    return [2 * slot + 1 for slot in inner] + [2 * slot for slot in inner]


def reversed_bits(value, bits):
    return sum(((value >> bit) & 1) << (bits - 1 - bit) for bit in range(bits))


def lasting(microseconds):
    return pl.CostEstimate(flops=int(microseconds * 1.15e+09), transcendentals=0, bytes_accessed=0)


def far(value):
    return pltpu.with_memory_space_constraint(value, pltpu.HBM)


def whole(shape):
    return pl.BlockSpec(shape, lambda *_: (0,) * len(shape), pipeline_mode=pl.Buffered(1))


def kernel_params(megabytes):
    return pltpu.CompilerParams(vmem_limit_bytes=megabytes << 20, dimension_semantics=("arbitrary",))


def on_device(
    ctx_size,
    dp_size,
    tokens,
    segment_ids,
    w_qkv,
    w_out,
    w_up,
    w_down,
    norm_gain,
    norm_bias,
    grad_out,
):
    seqs, span, width = tokens.shape
    half = span // 2
    local_width = w_out.shape[0]
    heads = local_width // HEAD_DIM
    units_local = w_up.shape[0]
    rows = seqs * half
    long_half = half + STAT_ROWS
    ctx_bits = ctx_size.bit_length() - 1
    turn = lax.axis_index("tensor")
    place = lax.axis_index("ctx")
    row_place = lax.axis_index("dp")
    turn_array = turn.reshape(1)

    def room(megabytes):
        return kernel_params(megabytes if ctx_size <= 4 else 60)

    def swap(value):
        return lax.ppermute(value, "tensor", [(0, 1), (1, 0)])

    def hop(value, stage):
        moves = []
        for spot in range(ctx_size):
            for core in range(2):
                bit = stage if core == 0 else ctx_bits - 1 - stage
                moves.append((spot * 2 + core, (spot ^ (1 << bit)) * 2 + core))
        return lax.ppermute(value, ("ctx", "tensor"), moves)

    def tie(*values):
        return lax.optimization_barrier(values)

    def gather_near(own):
        own = own[:, None]
        return [hop(own, stage) for stage in range(min(ctx_bits, 2))]

    def gather_far(own, near_groups):
        groups = list(near_groups)
        if ctx_bits >= 2:
            groups.append(hop(groups[0], 1))
        for stage in range(2, ctx_bits):
            groups.append(hop(jnp.concatenate([own[:, None]] + groups, axis=1), stage))
        return groups

    def half_of(value, which):
        return lax.dynamic_slice_in_dim(value, which * half, half, 1)

    def with_ids(which):
        ids = half_of(segment_ids, which).astype(low)
        row = jnp.pad(ids[:, None, :], ((0, 0), (0, STAT_ROWS - 1), (0, width - half)))
        return jnp.concatenate([half_of(tokens, which), row], axis=1)

    def units_of(groups):
        direct, swapped = groups[: len(groups) // 2], groups[len(groups) // 2 :]
        if ctx_size == 4:
            return [(direct[0], swapped[1]), (direct[1], swapped[0]), (direct[2], swapped[2])]
        mirror = [reversed_bits(slot, ctx_bits) - 1 for slot in range(1, ctx_size)]
        first, second = jnp.concatenate(direct, axis=1), jnp.concatenate(swapped, axis=1)
        return [(first, jnp.stack([second[:, slot] for slot in mirror], axis=1))]

    block_width = 3 * local_width + LANES
    part_spec = pl.BlockSpec((seqs, 1, long_half, width), lambda g: (0, g, 0, 0))

    def project(part_a, part_b):
        count = part_a.shape[1]
        return pl.pallas_call(
            project_kernel,
            grid=(count,),
            in_specs=[whole(w_qkv.shape), part_spec, part_spec],
            out_specs=pl.BlockSpec((seqs, 1, span, block_width), lambda g: (0, g, 0, 0)),
            out_shape=jax.ShapeDtypeStruct((seqs, count, span, block_width), low),
            compiler_params=room(16),
            cost_estimate=lasting(2),
            name="project",
        )(w_qkv, part_a, part_b)

    tok_a, tok_b = with_ids(turn), with_ids(1 - turn)
    tok_near = gather_near(tok_a)
    w_out_oth, w_up_oth, w_down_oth = swap(w_out), swap(w_up), swap(w_down)
    own = project(tok_a[:, None], tok_b[:, None])

    def seq_spec(shape):
        return pl.BlockSpec((1,) + shape, lambda s, *_: (s,) + (0,) * len(shape))

    def unit_specs(chosen):
        return [
            pl.BlockSpec(
                (1,) + value.shape[1:],
                lambda s, *_: (s, 0, 0, 0),
                pipeline_mode=pl.Buffered(2 if value.shape[1] == 1 else 1),
            )
            for value in chosen
        ]

    head_square = pltpu.VMEM((heads, span, span), full)
    head_square_low = pltpu.VMEM((heads, span, span), low)
    q_scratch = pltpu.VMEM((heads, span, 2 * LANES), low)
    head_rows = pltpu.VMEM((heads, span, LANES), low)

    def attend(chosen, state, finish):
        begin = state is None
        state_shapes = [((local_width, span), full), ((16, span), full)]
        shapes = (
            [((half, local_width), low), ((long_half, local_width), low), ((8, span), full)]
            if finish
            else state_shapes
        )
        state = [] if begin else list(state)
        return pl.pallas_call(
            functools.partial(attend_kernel, [value.shape[1] for value in chosen], heads, begin, finish),
            grid=(seqs,),
            in_specs=unit_specs([own] + chosen) + [seq_spec(value.shape[1:]) for value in state],
            out_specs=[seq_spec(shape) for shape, _ in shapes],
            out_shape=[
                (pltpu.HBM if finish else jax.ShapeDtypeStruct)((seqs,) + shape, kind) for shape, kind in shapes
            ],
            scratch_shapes=[
                q_scratch,
                head_square,
                head_square_low,
                pltpu.VMEM((16, span), full),
                pltpu.VMEM((local_width, span), full),
            ],
            compiler_params=room(14),
            cost_estimate=lasting(3),
            name="attend",
        )(own, *chosen, *state)

    state = attend([], None, False)
    *tok_near, first_state = tie(*tok_near, state[0])
    state = (first_state, state[1])
    tok_groups = gather_far(tok_a, tok_near)
    if ctx_size == 4:
        swapped = [swap(group) for group in tok_groups[:2]]
        near_units = [project(tok_groups[0], swapped[1]), project(tok_groups[1], swapped[0])]
        state = attend(near_units, state, False)
        last, first_state = tie(tok_groups[2], state[0])
        far_units = [project(last, swap(last))]
        units = near_units + far_units
        mixed_keep, mixed_send, lse = attend(far_units, (first_state, state[1]), True)
    else:
        units = [project(*pair) for pair in units_of(tok_groups + [swap(group) for group in tok_groups])]
        mixed_keep, mixed_send, lse = attend(units, state, True)
    mixed_recv = swap(mixed_send)

    middle_in = [
        tok_a,
        mixed_keep,
        mixed_recv,
        lse,
        w_out,
        w_out_oth,
        w_up,
        w_up_oth,
        w_down,
        w_down_oth,
        norm_gain,
        norm_bias,
    ]
    middle_shapes = [
        ((seqs, half, width), low),
        ((seqs, half, width), full),
        ((seqs, long_half, width), low),
        ((rows, units_local), low),
        ((rows, units_local), low),
        ((rows, units_local), low),
        ((rows, units_local), low),
        ((rows, width), low),
        ((rows, width), low),
        ((8, width), full),
    ]
    (
        out_half,
        d_resid,
        payload,
        active_own,
        active_oth,
        d_up_own,
        d_up_oth,
        d_ffn,
        normed_low,
        small,
    ) = pl.pallas_call(
        functools.partial(middle_kernel, min(512, units_local)),
        grid_spec=pltpu.PrefetchScalarGridSpec(
            num_scalar_prefetch=1,
            grid=(1,),
            in_specs=[whole(value.shape) for value in middle_in]
            + [pl.BlockSpec((seqs, half, width), lambda s, turn_ref: (0, turn_ref[0], 0))],
            out_specs=[whole(shape) for shape, _ in middle_shapes],
            scratch_shapes=[pltpu.VMEM((rows, 2 * units_local), full)],
        ),
        out_shape=[
            (jax.ShapeDtypeStruct if number == 2 else pltpu.HBM)(shape, kind)
            for number, (shape, kind) in enumerate(middle_shapes)
        ],
        compiler_params=room(36),
        cost_estimate=lasting(16),
        name="middle",
    )(turn_array, *middle_in, grad_out)

    order = slot_order(ctx_size)
    mirrored = [reversed_bits(slot, ctx_bits) for slot in order]
    owners = place ^ jnp.where(turn == 0, jnp.array(order, jnp.int32), jnp.array(mirrored, jnp.int32))
    quarter = width // ctx_size
    stages = [ctx_size >> (stage + 1) for stage in range(ctx_bits)] + [1]
    turned_kind = low if quarter % 16 == 0 else full
    chunk = min(512, units_local)

    def slot_scratch(count):
        return [pltpu.VMEM((width, count), turned_kind), pltpu.VMEM((ctx_size * padded(quarter), count), low)]

    def pair_grad(left_a, left_b, right_a, right_b, name):
        right_spec = pl.BlockSpec((rows, chunk), lambda n, *_: (0, n))
        return pl.pallas_call(
            pair_grad_kernel,
            grid_spec=pltpu.PrefetchScalarGridSpec(
                num_scalar_prefetch=1,
                grid=(units_local // chunk,),
                in_specs=[whole(left_a.shape), whole(left_b.shape), right_spec, right_spec],
                out_specs=[pl.BlockSpec((count, quarter, chunk), lambda n, *_: (0, 0, n)) for count in stages],
                scratch_shapes=slot_scratch(2 * rows),
            ),
            out_shape=[pltpu.HBM((count, quarter, units_local), low) for count in stages],
            compiler_params=room(16),
            cost_estimate=lasting(5.5),
            name=name,
        )(owners, *map(far, (left_a, left_b, right_a, right_b)))

    parity = row_place & 1

    def add_up(values):
        return sum(value.astype(full) for value in values)

    def send_stage(parts, gots, stage):
        count, start = parts[stage].shape[0], 0
        values = [parts[stage]]
        for got in gots:
            start = got.shape[0] - sum(part.shape[0] for part in parts[stage:])
            values.append(got[start : start + count])
        return add_up(values).astype(low)

    def own_half(parts, gots, which):
        values = [parts[-1]] + gots
        split = parts[-1].shape[1] // 2
        return add_up(
            [
                lax.dynamic_slice(value, (value.shape[0] - 1, which * split, 0), (1, split, value.shape[2]))
                for value in values
            ]
        )[0]

    class Blocks:
        def __init__(self, parts):
            self.parts, self.gots, self.stage, self.sent = list(parts), [], 0, None
            self.dp_stage, self.got = 0, None

        @property
        def arrived(self):
            return self.gots[-1] if self.dp_stage == 0 else self.got

        @arrived.setter
        def arrived(self, value):
            if self.dp_stage == 0:
                self.gots[-1] = value
            else:
                self.got = value

        def ready(self):
            if self.stage < ctx_bits:
                self.sent = send_stage(self.parts, self.gots, self.stage) if self.stage else self.parts[0]
            elif self.dp_stage == 0:
                self.sent = own_half(self.parts, self.gots, 1 - parity).astype(low)
            else:
                mine = own_half(self.parts, self.gots, parity) if self.dp_stage == 1 else self.sent.astype(full)
                self.sent = (mine + self.got.astype(full)).astype(low)

        def send(self):
            if self.stage < ctx_bits:
                self.gots.append(hop(self.sent, self.stage))
                self.stage += 1
                return
            last = self.dp_stage == dp_size.bit_length() - 1
            bit = 0 if last else self.dp_stage
            moves = [(spot, spot ^ (1 << bit)) for spot in range(dp_size)]
            self.got = lax.ppermute(self.sent, "dp", moves)
            self.dp_stage += 1

        def advance(self, *after):
            if self.gots:
                self.arrived = tie(self.arrived, *after)[0]
            elif after:
                self.parts[0] = tie(self.parts[0], *after)[0]
            self.ready()
            self.send()
            return self.sent

        def total(self):
            while self.dp_stage < dp_size.bit_length():
                self.advance()
            mine, other = self.sent, self.got
            return jnp.where(
                parity == 0, jnp.concatenate([mine, other], axis=0), jnp.concatenate([other, mine], axis=0)
            ).astype(full)

    grad_near = gather_near(payload)
    payload_b = swap(payload)
    d_ffn_b, active_b = swap(d_ffn), swap(active_oth)
    normed_b, d_up_b = swap(normed_low), swap(d_up_oth)
    down = Blocks(pair_grad(d_ffn, d_ffn_b, active_own, active_b, "grad_down"))
    latest = down.advance()
    normed_low, latest = tie(normed_low, latest)
    up = Blocks(pair_grad(normed_low, normed_b, d_up_own, d_up_b, "grad_up"))
    *grad_near, up.parts[0] = tie(*grad_near, up.parts[0])
    latest = up.advance()
    own_back, latest = tie(own, latest)
    grad_far = gather_far(payload, grad_near)
    grad_groups = grad_far + [swap(group) for group in grad_far]

    sum_shape = pltpu.HBM((seqs, span, local_width), full)
    row_shape = pltpu.HBM((seqs, span, local_width), low)
    grad_spec = seq_spec((long_half, width))
    span_spec = seq_spec((span, local_width))
    counts = [value.shape[1] for value in units]
    d_query, dk_sum, dv_sum = pl.pallas_call(
        functools.partial(query_grad_kernel, counts, heads),
        grid=(seqs,),
        in_specs=unit_specs([own]) + [grad_spec, grad_spec, whole(w_out.shape)] + unit_specs(units),
        out_specs=[span_spec] * 3,
        out_shape=[row_shape, sum_shape, sum_shape],
        scratch_shapes=[
            q_scratch,
            head_rows,
            pltpu.VMEM((16, span), full),
            head_square,
            head_square_low,
            head_square_low,
            pltpu.VMEM((local_width, span), full),
        ],
        compiler_params=room(20),
        cost_estimate=lasting(11),
        name="query_grad",
    )(own_back, payload, payload_b, far(w_out), *units)

    def sequence_grad(kernel, values, lefts, extra, columns, name):
        return Blocks(
            pl.pallas_call(
                kernel,
                grid_spec=pltpu.PrefetchScalarGridSpec(
                    num_scalar_prefetch=1,
                    grid=(1,),
                    in_specs=[whole(value.shape) for value in values],
                    out_specs=[whole((count, extra + quarter, columns)) for count in stages],
                    scratch_shapes=slot_scratch(seqs * span) * lefts,
                ),
                out_shape=[pltpu.HBM((count, extra + quarter, columns), low) for count in stages],
                compiler_params=room(20),
                cost_estimate=lasting(5.5),
                name=name,
            )(owners, *map(far, values))
        )

    small_rows = (small[:4] + swap(small)[:4]).reshape(4, ctx_size, quarter).transpose(1, 0, 2)
    small_rows = jnp.pad(small_rows, ((0, 0), (0, STAT_ROWS - 4), (0, local_width - quarter)))
    latest = down.advance(d_query)
    d_query, latest = tie(d_query, latest)
    query_out = sequence_grad(
        query_out_grad_kernel,
        (tok_a, tok_b, d_query, payload, payload_b, mixed_keep, mixed_send, small_rows),
        2,
        STAT_ROWS,
        2 * local_width,
        "query_out_grad",
    )
    latest = query_out.advance()
    latest = down.advance(latest)
    d_query, latest = tie(d_query, latest)
    grad_units = units_of(grad_groups)
    grad_a, grad_b = [pair[0] for pair in grad_units], [pair[1] for pair in grad_units]
    d_kv, d_input = pl.pallas_call(
        functools.partial(key_grad_kernel, counts, heads),
        grid_spec=pltpu.PrefetchScalarGridSpec(
            num_scalar_prefetch=1,
            grid=(seqs,),
            in_specs=unit_specs([own])
            + [span_spec] * 3
            + [whole(w_out.shape), whole(w_qkv.shape)]
            + unit_specs(units + grad_a + grad_b),
            out_specs=[seq_spec((span, 2 * local_width)), seq_spec((span, width))],
            scratch_shapes=[
                pltpu.VMEM((heads // 2, span, 2 * LANES), low),
                head_rows,
                head_rows,
                head_square,
                head_square_low,
                head_square_low,
                pltpu.VMEM((span, local_width), full),
                pltpu.VMEM((span, local_width), full),
            ],
        ),
        out_shape=[
            jax.ShapeDtypeStruct((seqs, span, 2 * local_width), low),
            jax.ShapeDtypeStruct((seqs, span, width), low),
        ],
        compiler_params=room(26),
        cost_estimate=lasting(12.5),
        name="key_grad",
    )(turn_array, own, *map(far, (d_query, dk_sum, dv_sum, w_out, w_qkv, *units)), *grad_a, *grad_b)

    latest = up.advance(d_kv)
    latest = down.advance(latest)
    latest = query_out.advance(latest)
    d_kv, latest = tie(d_kv, latest)
    key_value = sequence_grad(key_value_grad_kernel, (tok_a, tok_b, d_kv), 1, 0, 2 * local_width, "key_value_grad")
    latest = key_value.advance()
    out_half, d_resid, d_input, latest = tie(out_half, d_resid, d_input, latest)
    swapped = [swap(out_half), swap(d_resid), swap(d_input)]
    for blocks in (up, down, key_value, query_out):
        latest = blocks.advance(latest)

    def both_halves(mine, other):
        return jnp.where(
            turn == 0, jnp.concatenate([mine, other], axis=1), jnp.concatenate([other, mine], axis=1)
        )

    *swapped, latest = tie(*swapped, latest)
    outputs = both_halves(out_half, swapped[0])
    grad_tokens = d_input.astype(full) + swapped[2].astype(full) + both_halves(d_resid, swapped[1])
    outputs, grad_tokens, latest = tie(outputs, grad_tokens, latest)
    for blocks in (up, key_value, query_out, up, key_value, query_out, key_value):
        latest = blocks.advance(latest)
    down_total, up_total = down.total(), up.total()
    query_out_total, key_value_total = query_out.total(), key_value.total()
    small_total = query_out_total[:4, local_width : local_width + quarter]
    query_out_total = query_out_total[STAT_ROWS:]
    return (
        outputs,
        grad_tokens,
        jnp.stack(
            [query_out_total[:, :local_width], key_value_total[:, :local_width], key_value_total[:, local_width:]]
        ),
        query_out_total[:, local_width:].T,
        up_total.T,
        down_total.T,
        small_total[0:2],
        small_total[2:4],
    )


def solution(mesh):
    return jax.shard_map(
        functools.partial(on_device, mesh.shape["ctx"], mesh.shape["dp"]),
        mesh=mesh,
        in_specs=(
            P("dp", "ctx", None),
            P("dp", "ctx"),
            P(None, None, "tensor"),
            P("tensor", None),
            P("tensor", None),
            P("tensor", None),
            P(),
            P(),
            P("dp", "ctx", None),
        ),
        out_specs=(
            P("dp", "ctx", None),
            P("dp", "ctx", None),
            P(None, "ctx", "tensor"),
            P("tensor", "ctx"),
            P("tensor", "ctx"),
            P("tensor", "ctx"),
            P(None, "ctx"),
            P(None, "ctx"),
        ),
        check_vma=False,
    )
```

```python
import functools
import jax
import jax.numpy as jnp
from jax import lax
from jax.experimental import pallas as pl
from jax.experimental.pallas import tpu as pltpu
from jax.sharding import PartitionSpec as P

HEAD_DIM = 64
LANES = 128
STAT_ROWS = 16
BIG = 2.0**30
low, full = jnp.bfloat16, jnp.float32


def dot_nn(left, right):
    return lax.dot_general(left, right, (((1,), (0,)), ((), ())), preferred_element_type=full)


def dot_nt(left, right):
    return lax.dot_general(left, right, (((1,), (1,)), ((), ())), preferred_element_type=full)


def dot_tn(left, right):
    return lax.dot_general(left, right, (((0,), (0,)), ((), ())), preferred_element_type=full)


def two_parts(values):
    high = values.astype(low)
    return high, (values - high.astype(full)).astype(low)


def project_kernel(w_qkv, part_a, part_b, out):
    half = part_a.shape[2] - STAT_ROWS
    local = w_qkv.shape[2]
    rows = jnp.concatenate([part[0, 0, :half, :] for part in (part_a, part_b)], axis=0)
    for kind in range(3):
        product = dot_nn(rows, w_qkv[kind])
        if kind == 0:
            product = product * 0.125
        out[0, 0, :, kind * local : (kind + 1) * local] = product.astype(low)
    ids = lax.broadcasted_iota(jnp.int32, (LANES, half), 0).astype(full)
    for which, part in enumerate((part_a, part_b)):
        row = part[0, 0, half : half + 1, :half].astype(full)
        out[0, 0, which * half : (which + 1) * half, 3 * local :] = jnp.where(ids == row, 1.0, 0.0).T.astype(low)


class Lanes:
    def __init__(self, heads):
        self.local = heads * HEAD_DIM

    def of(self, kind, pair):
        start = kind * self.local + pair * LANES
        return slice(start, start + LANES)

    @property
    def hot(self):
        return slice(3 * self.local, 3 * self.local + LANES)


def split_heads(value):
    left = lax.broadcasted_iota(jnp.int32, value.shape, 1) < HEAD_DIM
    zero = jnp.zeros_like(value)
    return jnp.where(left, value, zero), jnp.where(left, zero, value)


def present(hot):
    return jnp.max(hot.astype(full), axis=0, keepdims=True)


def over_units(counts, unit_refs, lanes, own_ids, body):
    flags = [
        jnp.max(own_ids * present(ref[0, 0, :, lanes.hot])) > 0.0 if count == 1 else None
        for count, ref in zip(counts, unit_refs)
    ]
    for number, (count, ref) in enumerate(zip(counts, unit_refs)):
        if count == 1:
            pl.when(flags[number])(functools.partial(body, number, 0))
        else:

            def step(index, carry, number=number, ref=ref):
                shared = jnp.max(own_ids * present(ref[0, index, :, lanes.hot])) > 0.0
                pl.when(shared)(functools.partial(body, number, index))
                return carry

            lax.fori_loop(0, count, step, 0)


def attend_kernel(counts, heads, begin, finish, *refs):
    lanes, pairs, units = Lanes(heads), heads // 2, len(counts)
    own, unit_refs = refs[0], refs[1 : 1 + units]
    refs = refs[1 + units :]
    if not begin:
        acc_in, stat_in = refs[:2]
        refs = refs[2:]
    if finish:
        mixed_keep, mixed_send, lse_out = refs[:3]
        refs = refs[3:]
    else:
        acc_out, stat_out = refs[:2]
        refs = refs[2:]
    q_aug, scores, weights, stat, acc = refs
    span = own.shape[2]
    half = span // 2
    hot_own = own[0, 0, :, lanes.hot]
    penalty = ((hot_own.astype(full) - 1.0) * BIG).astype(low)
    for pair in range(pairs):
        for side, masked in enumerate(split_heads(own[0, 0, :, lanes.of(0, pair)])):
            q_aug[2 * pair + side] = jnp.concatenate([masked, penalty], axis=1)
    if not begin:
        acc[...] = acc_in[0]
        stat[...] = stat_in[0]

    def block(ref, index, first):
        hot = ref[0, index, :, lanes.hot]
        peaks = []
        for pair in range(pairs):
            k_aug = jnp.concatenate([ref[0, index, :, lanes.of(1, pair)], hot], axis=1)
            for side in range(2):
                head = 2 * pair + side
                product = dot_nt(k_aug, q_aug[head])
                scores[head] = product
                peak = jnp.max(product, axis=0, keepdims=True)
                peaks.append(peak if first else jnp.maximum(peak, stat[head : head + 1, :]))
        sums = []
        for head in range(heads):
            weight = jnp.exp(scores[head] - peaks[head])
            sums.append(jnp.sum(weight, axis=0, keepdims=True))
            weights[head] = weight.astype(low)
        for pair in range(pairs):
            turned = ref[0, index, :, lanes.of(2, pair)].T
            for side in range(2):
                head = 2 * pair + side
                rows = slice(head * HEAD_DIM, (head + 1) * HEAD_DIM)
                mix = dot_nn(turned[side * HEAD_DIM : (side + 1) * HEAD_DIM], weights[head])
                total = sums[head]
                if not first:
                    shrink = jnp.exp(stat[head : head + 1, :] - peaks[head])
                    total = total + stat[8 + head : 9 + head, :] * shrink
                    mix = mix + acc[rows, :] * shrink
                acc[rows, :] = mix
                stat[head : head + 1, :] = peaks[head]
                stat[8 + head : 9 + head, :] = total

    if begin:
        block(own, 0, True)
    over_units(
        counts, unit_refs, lanes, present(hot_own), lambda number, index: block(unit_refs[number], index, False)
    )
    if not finish:
        acc_out[0] = acc[...]
        stat_out[0] = stat[...]
        return
    totals = stat[8 : 8 + heads, :]
    lse = stat[0:heads, :] + jnp.log(totals)
    lse_out[0, 0:heads, :] = lse
    lse_out[0, heads:8, :] = jnp.zeros((8 - heads, span), full)
    scale = 1.0 / totals
    for pair in range(pairs):
        chosen = slice(pair * LANES, (pair + 1) * LANES)
        mixed = jnp.concatenate(
            [
                acc[head * HEAD_DIM : (head + 1) * HEAD_DIM, :] * scale[head : head + 1, :]
                for head in (2 * pair, 2 * pair + 1)
            ],
            axis=0,
        ).T.astype(low)
        mixed_keep[0, :, chosen] = mixed[:half]
        mixed_send[0, :half, chosen] = mixed[half:]
    row_of = lax.broadcasted_iota(jnp.int32, (STAT_ROWS, half), 0)
    for column in range(pairs):
        tile = jnp.zeros((STAT_ROWS, half), full)
        for which in range(2):
            row = lse[which * pairs + column : which * pairs + column + 1, half:]
            for kind, part in enumerate(two_parts(row)):
                tile = jnp.where(row_of == kind + 2 * which, part.astype(full), tile)
        mixed_send[0, half:, column * LANES : (column + 1) * LANES] = tile.astype(low)


def stat_row(grad_a, grad_b, at, kind, head, half):
    tile = slice(head * LANES, (head + 1) * LANES)
    parts = []
    for other, ref in enumerate((grad_a, grad_b)):
        row = half + 2 * kind + 4 * other
        parts.append(
            ref[at + (slice(row, row + 1), tile)].astype(full)
            + ref[at + (slice(row + 1, row + 2), tile)].astype(full)
        )
    return jnp.concatenate(parts, axis=1)


def query_grad_kernel(counts, heads, *refs):
    lanes, pairs, units = Lanes(heads), heads // 2, len(counts)
    own, grad_a, grad_b, w_out = refs[:4]
    unit_refs = refs[4 : 4 + units]
    dq_out, dk_out, dv_out, q_aug, d_mix, rows_of, scores, weights, d_scores, acc = refs[4 + units :]
    span = own.shape[2]
    half = span // 2
    hot_own = own[0, 0, :, lanes.hot]
    penalty = ((hot_own.astype(full) - 1.0) * BIG).astype(low)
    d_attn = jnp.concatenate([grad_a[0, :half, :], grad_b[0, :half, :]], axis=0)
    d_mixed = dot_nt(d_attn, w_out[...]).astype(low)
    for pair in range(pairs):
        q_parts = split_heads(own[0, 0, :, lanes.of(0, pair)])
        d_parts = split_heads(d_mixed[:, pair * LANES : (pair + 1) * LANES])
        for side in range(2):
            head = 2 * pair + side
            q_aug[head] = jnp.concatenate([q_parts[side], penalty], axis=1)
            d_mix[head] = d_parts[side]
            rows_of[head : head + 1, :] = stat_row(grad_a, grad_b, (0,), 0, head, half)
            rows_of[8 + head : 9 + head, :] = stat_row(grad_a, grad_b, (0,), 1, head, half)

    def block(ref, index, first):
        hot = ref[0, index, :, lanes.hot]
        for pair in range(pairs):
            k_aug = jnp.concatenate([ref[0, index, :, lanes.of(1, pair)], hot], axis=1)
            for side in range(2):
                head = 2 * pair + side
                scores[head] = dot_nt(k_aug, q_aug[head])
        for pair in range(pairs):
            values = ref[0, index, :, lanes.of(2, pair)]
            for side in range(2):
                head = 2 * pair + side
                weight = jnp.exp(scores[head] - rows_of[head : head + 1, :])
                d_weight = dot_nt(values, d_mix[head])
                d_scores[head] = (weight * (d_weight - rows_of[8 + head : 9 + head, :])).astype(low)
                if first:
                    weights[head] = weight.astype(low)
        for pair in range(pairs):
            turned = ref[0, index, :, lanes.of(1, pair)].T
            for side in range(2):
                head = 2 * pair + side
                rows = slice(head * HEAD_DIM, (head + 1) * HEAD_DIM)
                product = dot_nn(turned[side * HEAD_DIM : (side + 1) * HEAD_DIM], d_scores[head])
                acc[rows, :] = product if first else acc[rows, :] + product
            if first:
                chosen = slice(pair * LANES, (pair + 1) * LANES)
                one, two = 2 * pair, 2 * pair + 1
                dv_out[0, :, chosen] = dot_nn(weights[one], d_mix[one]) + dot_nn(weights[two], d_mix[two])
                dk_out[0, :, chosen] = dot_nn(d_scores[one], q_aug[one, :, :LANES]) + dot_nn(
                    d_scores[two], q_aug[two, :, :LANES]
                )

    block(own, 0, True)
    over_units(
        counts, unit_refs, lanes, present(hot_own), lambda number, index: block(unit_refs[number], index, False)
    )
    for pair in range(pairs):
        chosen = slice(pair * LANES, (pair + 1) * LANES)
        dq_out[0, :, chosen] = (acc[chosen, :] * 0.125).T.astype(low)


def key_grad_kernel(counts, heads, turn_ref, *refs):
    lanes, pairs, units = Lanes(heads), heads // 2, len(counts)
    own, dq_in, dk_in, dv_in, w_out, w_qkv = refs[:6]
    unit_refs = refs[6 : 6 + units]
    a_refs = refs[6 + units : 6 + 2 * units]
    b_refs = refs[6 + 2 * units : 6 + 3 * units]
    d_kv, d_input, k_aug, q_mask, d_mix, scores, weights, d_scores, dk_acc, dv_acc = refs[6 + 3 * units :]
    span = own.shape[2]
    half = span // 2
    local = lanes.local
    turn = turn_ref[0]
    hot_own = own[0, 0, :, lanes.hot]
    for pair in range(pairs):
        k_aug[pair] = jnp.concatenate([own[0, 0, :, lanes.of(1, pair)], hot_own], axis=1)
    dk_acc[...] = dk_in[0]
    dv_acc[...] = dv_in[0]

    def block(number, index):
        ref, grad_a, grad_b = unit_refs[number], a_refs[number], b_refs[number]
        penalty = ((ref[0, index, :, lanes.hot].astype(full) - 1.0) * BIG).astype(low)
        d_attn = jnp.concatenate([grad_a[0, index, :half, :], grad_b[0, index, :half, :]], axis=0)
        d_mixed = dot_nt(d_attn, w_out[...]).astype(low)
        for pair in range(pairs):
            q_parts = split_heads(ref[0, index, :, lanes.of(0, pair)])
            d_parts = split_heads(d_mixed[:, pair * LANES : (pair + 1) * LANES])
            for side in range(2):
                head = 2 * pair + side
                q_mask[head] = q_parts[side]
                d_mix[head] = d_parts[side]
                scores[head] = dot_nt(k_aug[pair], jnp.concatenate([q_parts[side], penalty], axis=1))
        for pair in range(pairs):
            values = own[0, 0, :, lanes.of(2, pair)]
            for side in range(2):
                head = 2 * pair + side
                lse = stat_row(grad_a, grad_b, (0, index), 0, head, half)
                delta = stat_row(grad_a, grad_b, (0, index), 1, head, half)
                weight = jnp.exp(scores[head] - lse)
                d_weight = dot_nt(values, d_mix[head])
                d_scores[head] = (weight * (d_weight - delta)).astype(low)
                weights[head] = weight.astype(low)
        for pair in range(pairs):
            chosen = slice(pair * LANES, (pair + 1) * LANES)
            one, two = 2 * pair, 2 * pair + 1
            dv_acc[:, chosen] += dot_nn(weights[one], d_mix[one]) + dot_nn(weights[two], d_mix[two])
            dk_acc[:, chosen] += dot_nn(d_scores[one], q_mask[one]) + dot_nn(d_scores[two], q_mask[two])

    over_units(counts, unit_refs, lanes, present(hot_own), block)
    half_a = pl.ds(pl.multiple_of(turn * half, half), half)
    half_b = pl.ds(pl.multiple_of((1 - turn) * half, half), half)
    for kind, value in enumerate((dq_in[0], dk_acc[...].astype(low), dv_acc[...].astype(low))):
        chosen = slice(kind * local, (kind + 1) * local)
        product = dot_nt(value, w_qkv[kind])
        total = product if kind == 0 else total + product
        if kind > 0:
            d_kv[0, :, (kind - 1) * local : kind * local] = value
    total = total.astype(low)
    d_input[0, half_a, :] = total[:half]
    d_input[0, half_b, :] = total[half:]


def padded(block):
    return -(-block // 16) * 16


def lane_part(ref, half=None):
    if half is None:
        return lambda lanes: ref[:, lanes]
    return lambda lanes: ref[:, :half, lanes].reshape(ref.shape[0] * half, LANES)


def put_slots(turned, slots, values, owners, block):
    def turn_lanes(step, carry):
        lanes = pl.ds(pl.multiple_of(step * LANES, LANES), LANES)
        start = 0
        for load in values:
            value = load(lanes)
            turned[lanes, start : start + value.shape[0]] = value.astype(turned.dtype).T
            start += value.shape[0]
        return carry

    lax.fori_loop(0, turned.shape[0] // LANES, turn_lanes, 0)
    room = padded(block)
    for slot in range(slots.shape[0] // room):
        source = pl.ds(pl.multiple_of(owners[slot] * block, 16 if block % 16 == 0 else 8), block)
        slots[slot * room : slot * room + block, :] = turned[source, :].astype(low)


def places_of(targets):
    return [(ref, index) for ref in targets for index in range(ref.shape[0])]


def put_blocks(product, targets, block, skip):
    for slot, (ref, index) in enumerate(places_of(targets)):
        start = slot * padded(block)
        ref[index, skip : skip + block, :] = product[start : start + block].astype(low)


def pair_grad_kernel(owners, left_a, left_b, right_a, right_b, *refs):
    targets, (turned, slots) = refs[:-2], refs[-2:]
    block = targets[0].shape[1]

    @pl.when(pl.program_id(0) == 0)
    def _():
        put_slots(turned, slots, [lane_part(part) for part in (left_a, left_b)], owners, block)

    right = jnp.concatenate([right_a[...], right_b[...]], axis=0)
    put_blocks(dot_nn(slots[...], right), targets, block, 0)


def half_rows(part, half):
    return part[:, :half, :].reshape(part.shape[0] * half, -1)


def both_rows(value, half):
    return jnp.concatenate([half_rows(value[:, :half], half), half_rows(value[:, half:], half)], axis=0)


def query_out_grad_kernel(owners, tok_a, tok_b, d_query, d_attn_a, d_attn_b, mixed_a, mixed_b, small, *refs):
    targets, (turned, slots, turned_second, slots_second) = refs[:-4], refs[-4:]
    span, local = d_query.shape[1:]
    half = span // 2
    block = targets[0].shape[1] - STAT_ROWS
    put_slots(turned, slots, [lane_part(part, half) for part in (tok_a, tok_b)], owners, block)
    first = dot_nn(slots[...], both_rows(d_query, half)).astype(low)
    put_slots(turned_second, slots_second, [lane_part(part, half) for part in (d_attn_a, d_attn_b)], owners, block)
    mixed = jnp.concatenate([half_rows(part, half) for part in (mixed_a, mixed_b)], axis=0)
    second = dot_nn(slots_second[...], mixed).astype(low)
    for slot, (ref, index) in enumerate(places_of(targets)):
        start = slot * padded(block)
        for which, product in enumerate((first, second)):
            columns = slice(which * local, (which + 1) * local)
            ref[index, STAT_ROWS:, columns] = product[start : start + block]
        ref[index, :STAT_ROWS, :local] = jnp.zeros((STAT_ROWS, local), low)
        ref[index, :STAT_ROWS, local:] = small[owners[slot]].astype(low)


def key_value_grad_kernel(owners, tok_a, tok_b, d_kv, *refs):
    targets, (turned, slots) = refs[:-2], refs[-2:]
    half = d_kv.shape[1] // 2
    block = targets[0].shape[1]
    put_slots(turned, slots, [lane_part(part, half) for part in (tok_a, tok_b)], owners, block)
    put_blocks(dot_nn(slots[...], both_rows(d_kv, half)), targets, block, 0)


def norm_of(residual):
    center = residual - jnp.mean(residual, axis=-1, keepdims=True)
    inverse = lax.rsqrt(jnp.mean(center * center, axis=-1, keepdims=True) + 1e-06)
    return center * inverse, inverse


def norm_back(d_normal, normal, inverse):
    return inverse * (
        d_normal
        - jnp.mean(d_normal, axis=-1, keepdims=True)
        - normal * jnp.mean(d_normal * normal, axis=-1, keepdims=True)
    )


def middle_kernel(
    chunk,
    turn_ref,
    tok,
    mixed_keep,
    mixed_recv,
    lse_keep,
    w_out_own,
    w_out_oth,
    w_up_own,
    w_up_oth,
    w_down_own,
    w_down_oth,
    gain,
    shift,
    grad_out,
    out,
    d_resid,
    payload,
    active_own,
    active_oth,
    d_up_own,
    d_up_oth,
    d_ffn_out,
    normed_out,
    small,
    slope,
):
    seqs, half, width = out.shape
    rows = seqs * half
    heads = mixed_keep.shape[2] // HEAD_DIM
    keep = mixed_keep[...].reshape(rows, -1)
    recv = mixed_recv[:, :half, :].reshape(rows, -1)
    attn = dot_nn(keep, w_out_own[...]) + dot_nn(recv, w_out_oth[...])
    resid_one = tok[:, :half, :].reshape(rows, width).astype(full) + attn
    normal_one, inverse_one = norm_of(resid_one)
    gain_one, gain_two = gain[0:1, :], gain[1:2, :]
    normed = normal_one * gain_one + shift[0:1, :]
    normed_low = normed.astype(low)
    normed_out[...] = normed_low
    units = w_up_own.shape[0]
    sides = ((w_up_own, w_down_own, active_own, d_up_own), (w_up_oth, w_down_oth, active_oth, d_up_oth))
    ffn = jnp.zeros((rows, width), full)
    for which, (w_up, w_down, active_ref, _) in enumerate(sides):
        for start in range(0, units, chunk):
            part = slice(start, start + chunk)
            upward = dot_nt(normed_low, w_up[part, :])
            spread = 0.5 * (1.0 + lax.erf(upward * 0.7071067811865476))
            active = (upward * spread).astype(low)
            slope[:, which * units + start : which * units + start + chunk] = (
                spread + upward * (jnp.exp(upward * upward * -0.5) * 0.3989422804014327)
            )
            active_ref[:, part] = active
            ffn = ffn + dot_nn(active, w_down[part, :])
    normal_two, inverse_two = norm_of(normed + ffn)
    out[...] = (normal_two * gain_two + shift[1:2, :]).astype(low).reshape(seqs, half, width)
    grad = grad_out[...].reshape(rows, width).astype(full)
    small[1:2, :] = jnp.sum(grad * normal_two, axis=0, keepdims=True)
    small[3:4, :] = jnp.sum(grad, axis=0, keepdims=True)
    d_resid_two = norm_back(grad * gain_two, normal_two, inverse_two)
    d_ffn = d_resid_two.astype(low)
    d_ffn_out[...] = d_ffn
    d_normed = d_resid_two
    for which, (w_up, w_down, _, d_up_ref) in enumerate(sides):
        for start in range(0, units, chunk):
            part = slice(start, start + chunk)
            d_active = dot_nt(d_ffn, w_down[part, :])
            d_up = (d_active * slope[:, which * units + start : which * units + start + chunk]).astype(low)
            d_up_ref[:, part] = d_up
            d_normed = d_normed + dot_nn(d_up, w_up[part, :])
    small[0:1, :] = jnp.sum(d_normed * normal_one, axis=0, keepdims=True)
    small[2:3, :] = jnp.sum(d_normed, axis=0, keepdims=True)
    small[4:8, :] = jnp.zeros((4, width), full)
    d_resid_one = norm_back(d_normed * gain_one, normal_one, inverse_one)
    d_resid[...] = d_resid_one.reshape(seqs, half, width)
    d_attn = d_resid_one.astype(low)
    payload[:, :half, :] = d_attn.reshape(seqs, half, width)
    column_of = lax.broadcasted_iota(jnp.int32, (8, heads * HEAD_DIM), 1) // HEAD_DIM
    chosen = jnp.where(column_of == lax.broadcasted_iota(jnp.int32, (8, heads * HEAD_DIM), 0), 1.0, 0.0)
    deltas = []
    for mixed, w_out in ((keep, w_out_own), (recv, w_out_oth)):
        d_mixed = dot_nt(d_attn, w_out[...]).astype(low).astype(full)
        deltas.append(
            lax.dot_general(
                chosen,
                d_mixed * mixed.astype(full),
                (((1,), (1,)), ((), ())),
                precision=lax.Precision.HIGHEST,
                preferred_element_type=full,
            )
        )
    row_of = lax.broadcasted_iota(jnp.int32, (STAT_ROWS, half), 0)
    pairs = heads // 2
    for seq in range(seqs):
        for head in range(heads):
            lse_high, lse_low = two_parts(lse_keep[seq, head : head + 1, :half])
            tile = slice((head % pairs) * LANES, (head % pairs + 1) * LANES)
            row = half + 2 * (head // pairs)
            parts = [lse_high.astype(full), lse_low.astype(full)]
            for which in range(2):
                piece = deltas[which][head : head + 1, seq * half : (seq + 1) * half]
                if which == 1:
                    parts.append(mixed_recv[seq, row : row + 1, tile].astype(full))
                    parts.append(mixed_recv[seq, row + 1 : row + 2, tile].astype(full))
                parts.extend(part.astype(full) for part in two_parts(piece))
            stat = jnp.zeros((STAT_ROWS, half), full)
            for index, part in enumerate(parts):
                stat = jnp.where(row_of == index, part, stat)
            payload[seq, half:, head * LANES : (head + 1) * LANES] = stat.astype(low)


def slot_order(count):
    if count == 1:
        return [0]
    inner = slot_order(count // 2)
    return [2 * slot + 1 for slot in inner] + [2 * slot for slot in inner]


def reversed_bits(value, bits):
    return sum(((value >> bit) & 1) << (bits - 1 - bit) for bit in range(bits))


def lasting(microseconds):
    return pl.CostEstimate(flops=int(microseconds * 1.15e+09), transcendentals=0, bytes_accessed=0)


def far(value):
    return pltpu.with_memory_space_constraint(value, pltpu.HBM)


def whole(shape):
    return pl.BlockSpec(shape, lambda *_: (0,) * len(shape), pipeline_mode=pl.Buffered(1))


def kernel_params(megabytes):
    return pltpu.CompilerParams(vmem_limit_bytes=megabytes << 20)


def on_device(
    ctx_size,
    dp_size,
    tokens,
    segment_ids,
    w_qkv,
    w_out,
    w_up,
    w_down,
    norm_gain,
    norm_bias,
    grad_out,
):
    seqs, span, width = tokens.shape
    half = span // 2
    local_width = w_out.shape[0]
    heads = local_width // HEAD_DIM
    units_local = w_up.shape[0]
    rows = seqs * half
    long_half = half + STAT_ROWS
    ctx_bits = ctx_size.bit_length() - 1
    turn = lax.axis_index("tensor")
    place = lax.axis_index("ctx")
    row_place = lax.axis_index("dp")
    turn_array = turn.reshape(1)

    def room(megabytes):
        return kernel_params(megabytes if ctx_size <= 4 else 60)

    def swap(value):
        return lax.ppermute(value, "tensor", [(0, 1), (1, 0)])

    def hop(value, stage):
        moves = []
        for spot in range(ctx_size):
            for core in range(2):
                bit = stage if core == 0 else ctx_bits - 1 - stage
                moves.append((spot * 2 + core, (spot ^ (1 << bit)) * 2 + core))
        return lax.ppermute(value, ("ctx", "tensor"), moves)

    def tie(*values):
        return lax.optimization_barrier(values)

    def gather_near(own):
        own = own[:, None]
        return [hop(own, stage) for stage in range(min(ctx_bits, 2))]

    def gather_far(own, near_groups):
        groups = list(near_groups)
        if ctx_bits >= 2:
            groups.append(hop(groups[0], 1))
        for stage in range(2, ctx_bits):
            groups.append(hop(jnp.concatenate([own[:, None]] + groups, axis=1), stage))
        return groups

    def half_of(value, which):
        return lax.dynamic_slice_in_dim(value, which * half, half, 1)

    def with_ids(which):
        ids = half_of(segment_ids, which).astype(low)
        row = jnp.pad(ids[:, None, :], ((0, 0), (0, STAT_ROWS - 1), (0, width - half)))
        return jnp.concatenate([half_of(tokens, which), row], axis=1)

    def units_of(groups):
        direct, swapped = groups[: len(groups) // 2], groups[len(groups) // 2 :]
        if ctx_size == 4:
            return [(direct[0], swapped[1]), (direct[1], swapped[0]), (direct[2], swapped[2])]
        mirror = [reversed_bits(slot, ctx_bits) - 1 for slot in range(1, ctx_size)]
        first, second = jnp.concatenate(direct, axis=1), jnp.concatenate(swapped, axis=1)
        return [(first, jnp.stack([second[:, slot] for slot in mirror], axis=1))]

    block_width = 3 * local_width + LANES
    part_spec = pl.BlockSpec((1, 1, long_half, width), lambda g, s: (s, g, 0, 0))

    def project(part_a, part_b):
        count = part_a.shape[1]
        return pl.pallas_call(
            project_kernel,
            grid=(count, seqs),
            in_specs=[whole(w_qkv.shape), part_spec, part_spec],
            out_specs=pl.BlockSpec((1, 1, span, block_width), lambda g, s: (s, g, 0, 0)),
            out_shape=jax.ShapeDtypeStruct((seqs, count, span, block_width), low),
            compiler_params=room(16),
            cost_estimate=lasting(2),
            name="project",
        )(w_qkv, part_a, part_b)

    tok_a, tok_b = with_ids(turn), with_ids(1 - turn)
    tok_near = gather_near(tok_a)
    w_out_oth, w_up_oth, w_down_oth = swap(w_out), swap(w_up), swap(w_down)
    own = project(tok_a[:, None], tok_b[:, None])

    def seq_spec(shape):
        return pl.BlockSpec((1,) + shape, lambda s, *_: (s,) + (0,) * len(shape))

    def unit_specs(chosen):
        return [
            pl.BlockSpec(
                (1,) + value.shape[1:],
                lambda s, *_: (s, 0, 0, 0),
                pipeline_mode=pl.Buffered(2 if value.shape[1] == 1 else 1),
            )
            for value in chosen
        ]

    head_square = pltpu.VMEM((heads, span, span), full)
    head_square_low = pltpu.VMEM((heads, span, span), low)
    q_scratch = pltpu.VMEM((heads, span, 2 * LANES), low)
    head_rows = pltpu.VMEM((heads, span, LANES), low)

    def attend(chosen, state, finish):
        begin = state is None
        state_shapes = [((local_width, span), full), ((16, span), full)]
        shapes = (
            [((half, local_width), low), ((long_half, local_width), low), ((8, span), full)]
            if finish
            else state_shapes
        )
        state = [] if begin else list(state)
        return pl.pallas_call(
            functools.partial(attend_kernel, [value.shape[1] for value in chosen], heads, begin, finish),
            grid=(seqs,),
            in_specs=unit_specs([own] + chosen) + [seq_spec(value.shape[1:]) for value in state],
            out_specs=[seq_spec(shape) for shape, _ in shapes],
            out_shape=[
                (pltpu.HBM if finish else jax.ShapeDtypeStruct)((seqs,) + shape, kind) for shape, kind in shapes
            ],
            scratch_shapes=[
                q_scratch,
                head_square,
                head_square_low,
                pltpu.VMEM((16, span), full),
                pltpu.VMEM((local_width, span), full),
            ],
            compiler_params=room(14),
            cost_estimate=lasting(3),
            name="attend",
        )(own, *chosen, *state)

    state = attend([], None, False)
    *tok_near, first_state = tie(*tok_near, state[0])
    state = (first_state, state[1])
    tok_groups = gather_far(tok_a, tok_near)
    if ctx_size == 4:
        swapped = [swap(group) for group in tok_groups[:2]]
        near_units = [project(tok_groups[0], swapped[1]), project(tok_groups[1], swapped[0])]
        state = attend(near_units, state, False)
        last, first_state = tie(tok_groups[2], state[0])
        far_units = [project(last, swap(last))]
        units = near_units + far_units
        mixed_keep, mixed_send, lse = attend(far_units, (first_state, state[1]), True)
    else:
        units = [project(*pair) for pair in units_of(tok_groups + [swap(group) for group in tok_groups])]
        mixed_keep, mixed_send, lse = attend(units, state, True)
    mixed_recv = swap(mixed_send)

    middle_in = [
        tok_a,
        mixed_keep,
        mixed_recv,
        lse,
        w_out,
        w_out_oth,
        w_up,
        w_up_oth,
        w_down,
        w_down_oth,
        norm_gain,
        norm_bias,
    ]
    middle_shapes = [
        ((seqs, half, width), low),
        ((seqs, half, width), full),
        ((seqs, long_half, width), low),
        ((rows, units_local), low),
        ((rows, units_local), low),
        ((rows, units_local), low),
        ((rows, units_local), low),
        ((rows, width), low),
        ((rows, width), low),
        ((8, width), full),
    ]
    (
        out_half,
        d_resid,
        payload,
        active_own,
        active_oth,
        d_up_own,
        d_up_oth,
        d_ffn,
        normed_low,
        small,
    ) = pl.pallas_call(
        functools.partial(middle_kernel, min(512, units_local)),
        grid_spec=pltpu.PrefetchScalarGridSpec(
            num_scalar_prefetch=1,
            grid=(1,),
            in_specs=[whole(value.shape) for value in middle_in]
            + [pl.BlockSpec((seqs, half, width), lambda s, turn_ref: (0, turn_ref[0], 0))],
            out_specs=[whole(shape) for shape, _ in middle_shapes],
            scratch_shapes=[pltpu.VMEM((rows, 2 * units_local), full)],
        ),
        out_shape=[
            (jax.ShapeDtypeStruct if number == 2 else pltpu.HBM)(shape, kind)
            for number, (shape, kind) in enumerate(middle_shapes)
        ],
        compiler_params=room(36),
        cost_estimate=lasting(16),
        name="middle",
    )(turn_array, *middle_in, grad_out)

    order = slot_order(ctx_size)
    mirrored = [reversed_bits(slot, ctx_bits) for slot in order]
    owners = place ^ jnp.where(turn == 0, jnp.array(order, jnp.int32), jnp.array(mirrored, jnp.int32))
    quarter = width // ctx_size
    stages = [ctx_size >> (stage + 1) for stage in range(ctx_bits)] + [1]
    turned_kind = low if quarter % 16 == 0 else full
    chunk = min(512, units_local)

    def slot_scratch(count):
        return [pltpu.VMEM((width, count), turned_kind), pltpu.VMEM((ctx_size * padded(quarter), count), low)]

    def pair_grad(left_a, left_b, right_a, right_b, name):
        right_spec = pl.BlockSpec((rows, chunk), lambda n, *_: (0, n))
        return pl.pallas_call(
            pair_grad_kernel,
            grid_spec=pltpu.PrefetchScalarGridSpec(
                num_scalar_prefetch=1,
                grid=(units_local // chunk,),
                in_specs=[whole(left_a.shape), whole(left_b.shape), right_spec, right_spec],
                out_specs=[pl.BlockSpec((count, quarter, chunk), lambda n, *_: (0, 0, n)) for count in stages],
                scratch_shapes=slot_scratch(2 * rows),
            ),
            out_shape=[pltpu.HBM((count, quarter, units_local), low) for count in stages],
            compiler_params=room(16),
            cost_estimate=lasting(5.5),
            name=name,
        )(owners, *map(far, (left_a, left_b, right_a, right_b)))

    parity = row_place & 1

    def add_up(values):
        return sum(value.astype(full) for value in values)

    def send_stage(parts, gots, stage):
        count, start = parts[stage].shape[0], 0
        values = [parts[stage]]
        for got in gots:
            start = got.shape[0] - sum(part.shape[0] for part in parts[stage:])
            values.append(got[start : start + count])
        return add_up(values).astype(low)

    def own_half(parts, gots, which):
        values = [parts[-1]] + gots
        split = parts[-1].shape[1] // 2
        return add_up(
            [
                lax.dynamic_slice(value, (value.shape[0] - 1, which * split, 0), (1, split, value.shape[2]))
                for value in values
            ]
        )[0]

    class Blocks:
        def __init__(self, parts):
            self.parts, self.gots, self.stage, self.sent = list(parts), [], 0, None
            self.dp_stage, self.got = 0, None

        @property
        def arrived(self):
            return self.gots[-1] if self.dp_stage == 0 else self.got

        @arrived.setter
        def arrived(self, value):
            if self.dp_stage == 0:
                self.gots[-1] = value
            else:
                self.got = value

        def ready(self):
            if self.stage < ctx_bits:
                self.sent = send_stage(self.parts, self.gots, self.stage) if self.stage else self.parts[0]
            elif self.dp_stage == 0:
                self.sent = own_half(self.parts, self.gots, 1 - parity).astype(low)
            else:
                mine = own_half(self.parts, self.gots, parity) if self.dp_stage == 1 else self.sent.astype(full)
                self.sent = (mine + self.got.astype(full)).astype(low)

        def send(self):
            if self.stage < ctx_bits:
                self.gots.append(hop(self.sent, self.stage))
                self.stage += 1
                return
            last = self.dp_stage == dp_size.bit_length() - 1
            bit = 0 if last else self.dp_stage
            moves = [(spot, spot ^ (1 << bit)) for spot in range(dp_size)]
            self.got = lax.ppermute(self.sent, "dp", moves)
            self.dp_stage += 1

        def advance(self, *after):
            if self.gots:
                self.arrived = tie(self.arrived, *after)[0]
            elif after:
                self.parts[0] = tie(self.parts[0], *after)[0]
            self.ready()
            self.send()
            return self.sent

        def total(self):
            while self.dp_stage < dp_size.bit_length():
                self.advance()
            mine, other = self.sent, self.got
            return jnp.where(
                parity == 0, jnp.concatenate([mine, other], axis=0), jnp.concatenate([other, mine], axis=0)
            ).astype(full)

    grad_near = gather_near(payload)
    payload_b = swap(payload)
    d_ffn_b, active_b = swap(d_ffn), swap(active_oth)
    normed_b, d_up_b = swap(normed_low), swap(d_up_oth)
    down = Blocks(pair_grad(d_ffn, d_ffn_b, active_own, active_b, "grad_down"))
    latest = down.advance()
    normed_low, latest = tie(normed_low, latest)
    up = Blocks(pair_grad(normed_low, normed_b, d_up_own, d_up_b, "grad_up"))
    *grad_near, up.parts[0] = tie(*grad_near, up.parts[0])
    latest = up.advance()
    own_back, latest = tie(own, latest)
    grad_far = gather_far(payload, grad_near)
    grad_groups = grad_far + [swap(group) for group in grad_far]

    sum_shape = pltpu.HBM((seqs, span, local_width), full)
    row_shape = pltpu.HBM((seqs, span, local_width), low)
    grad_spec = seq_spec((long_half, width))
    span_spec = seq_spec((span, local_width))
    counts = [value.shape[1] for value in units]
    d_query, dk_sum, dv_sum = pl.pallas_call(
        functools.partial(query_grad_kernel, counts, heads),
        grid=(seqs,),
        in_specs=unit_specs([own]) + [grad_spec, grad_spec, whole(w_out.shape)] + unit_specs(units),
        out_specs=[span_spec] * 3,
        out_shape=[row_shape, sum_shape, sum_shape],
        scratch_shapes=[
            q_scratch,
            head_rows,
            pltpu.VMEM((16, span), full),
            head_square,
            head_square_low,
            head_square_low,
            pltpu.VMEM((local_width, span), full),
        ],
        compiler_params=room(20),
        cost_estimate=lasting(11),
        name="query_grad",
    )(own_back, payload, payload_b, far(w_out), *units)

    def sequence_grad(kernel, values, lefts, extra, columns, name):
        return Blocks(
            pl.pallas_call(
                kernel,
                grid_spec=pltpu.PrefetchScalarGridSpec(
                    num_scalar_prefetch=1,
                    grid=(1,),
                    in_specs=[whole(value.shape) for value in values],
                    out_specs=[whole((count, extra + quarter, columns)) for count in stages],
                    scratch_shapes=slot_scratch(seqs * span) * lefts,
                ),
                out_shape=[pltpu.HBM((count, extra + quarter, columns), low) for count in stages],
                compiler_params=room(20),
                cost_estimate=lasting(5.5),
                name=name,
            )(owners, *map(far, values))
        )

    small_rows = (small[:4] + swap(small)[:4]).reshape(4, ctx_size, quarter).transpose(1, 0, 2)
    small_rows = jnp.pad(small_rows, ((0, 0), (0, STAT_ROWS - 4), (0, local_width - quarter)))
    latest = down.advance(d_query)
    d_query, latest = tie(d_query, latest)
    query_out = sequence_grad(
        query_out_grad_kernel,
        (tok_a, tok_b, d_query, payload, payload_b, mixed_keep, mixed_send, small_rows),
        2,
        STAT_ROWS,
        2 * local_width,
        "query_out_grad",
    )
    latest = query_out.advance()
    latest = down.advance(latest)
    d_query, latest = tie(d_query, latest)
    grad_units = units_of(grad_groups)
    grad_a, grad_b = [pair[0] for pair in grad_units], [pair[1] for pair in grad_units]
    d_kv, d_input = pl.pallas_call(
        functools.partial(key_grad_kernel, counts, heads),
        grid_spec=pltpu.PrefetchScalarGridSpec(
            num_scalar_prefetch=1,
            grid=(seqs,),
            in_specs=unit_specs([own])
            + [span_spec] * 3
            + [whole(w_out.shape), whole(w_qkv.shape)]
            + unit_specs(units + grad_a + grad_b),
            out_specs=[seq_spec((span, 2 * local_width)), seq_spec((span, width))],
            scratch_shapes=[
                pltpu.VMEM((heads // 2, span, 2 * LANES), low),
                head_rows,
                head_rows,
                head_square,
                head_square_low,
                head_square_low,
                pltpu.VMEM((span, local_width), full),
                pltpu.VMEM((span, local_width), full),
            ],
        ),
        out_shape=[
            jax.ShapeDtypeStruct((seqs, span, 2 * local_width), low),
            jax.ShapeDtypeStruct((seqs, span, width), low),
        ],
        compiler_params=room(26),
        cost_estimate=lasting(12.5),
        name="key_grad",
    )(turn_array, own, *map(far, (d_query, dk_sum, dv_sum, w_out, w_qkv, *units)), *grad_a, *grad_b)

    latest = up.advance(d_kv)
    latest = down.advance(latest)
    latest = query_out.advance(latest)
    d_kv, latest = tie(d_kv, latest)
    key_value = sequence_grad(key_value_grad_kernel, (tok_a, tok_b, d_kv), 1, 0, 2 * local_width, "key_value_grad")
    latest = key_value.advance()
    out_half, d_resid, d_input, latest = tie(out_half, d_resid, d_input, latest)
    swapped = [swap(out_half), swap(d_resid), swap(d_input)]
    for blocks in (up, down, key_value, query_out):
        latest = blocks.advance(latest)

    def both_halves(mine, other):
        return jnp.where(
            turn == 0, jnp.concatenate([mine, other], axis=1), jnp.concatenate([other, mine], axis=1)
        )

    *swapped, latest = tie(*swapped, latest)
    outputs = both_halves(out_half, swapped[0])
    grad_tokens = d_input.astype(full) + swapped[2].astype(full) + both_halves(d_resid, swapped[1])
    outputs, grad_tokens, latest = tie(outputs, grad_tokens, latest)
    for blocks in (up, key_value, query_out, up, key_value, query_out, key_value):
        latest = blocks.advance(latest)
    down_total, up_total = down.total(), up.total()
    query_out_total, key_value_total = query_out.total(), key_value.total()
    small_total = query_out_total[:4, local_width : local_width + quarter]
    query_out_total = query_out_total[STAT_ROWS:]
    return (
        outputs,
        grad_tokens,
        jnp.stack(
            [query_out_total[:, :local_width], key_value_total[:, :local_width], key_value_total[:, local_width:]]
        ),
        query_out_total[:, local_width:].T,
        up_total.T,
        down_total.T,
        small_total[0:2],
        small_total[2:4],
    )


def solution(mesh):
    return jax.shard_map(
        functools.partial(on_device, mesh.shape["ctx"], mesh.shape["dp"]),
        mesh=mesh,
        in_specs=(
            P("dp", "ctx", None),
            P("dp", "ctx"),
            P(None, None, "tensor"),
            P("tensor", None),
            P("tensor", None),
            P("tensor", None),
            P(),
            P(),
            P("dp", "ctx", None),
        ),
        out_specs=(
            P("dp", "ctx", None),
            P("dp", "ctx", None),
            P(None, "ctx", "tensor"),
            P("tensor", "ctx"),
            P("tensor", "ctx"),
            P("tensor", "ctx"),
            P(None, "ctx"),
            P(None, "ctx"),
        ),
        check_vma=False,
    )
```

```python
import functools
import jax
import jax.numpy as jnp
from jax import lax
from jax.experimental import pallas as pl
from jax.experimental.pallas import tpu as pltpu
from jax.sharding import PartitionSpec as P

HEAD_DIM = 64
LANES = 128
STAT_ROWS = 16
BIG = 2.0**30
low, full = jnp.bfloat16, jnp.float32


def dot_nn(left, right):
    return lax.dot_general(left, right, (((1,), (0,)), ((), ())), preferred_element_type=full)


def dot_nt(left, right):
    return lax.dot_general(left, right, (((1,), (1,)), ((), ())), preferred_element_type=full)


def dot_tn(left, right):
    return lax.dot_general(left, right, (((0,), (0,)), ((), ())), preferred_element_type=full)


def two_parts(values):
    high = values.astype(low)
    return high, (values - high.astype(full)).astype(low)


def project_kernel(w_qkv, part_a, part_b, out):
    half = part_a.shape[2] - STAT_ROWS
    local = w_qkv.shape[2]
    rows = jnp.concatenate([part[0, 0, :half, :] for part in (part_a, part_b)], axis=0)
    for kind in range(3):
        product = dot_nn(rows, w_qkv[kind])
        if kind == 0:
            product = product * 0.125
        out[0, 0, :, kind * local : (kind + 1) * local] = product.astype(low)
    ids = lax.broadcasted_iota(jnp.int32, (LANES, half), 0).astype(full)
    for which, part in enumerate((part_a, part_b)):
        row = part[0, 0, half : half + 1, :half].astype(full)
        out[0, 0, which * half : (which + 1) * half, 3 * local :] = jnp.where(ids == row, 1.0, 0.0).T.astype(low)


class Lanes:
    def __init__(self, heads):
        self.local = heads * HEAD_DIM

    def of(self, kind, pair):
        start = kind * self.local + pair * LANES
        return slice(start, start + LANES)

    @property
    def hot(self):
        return slice(3 * self.local, 3 * self.local + LANES)


def split_heads(value):
    left = lax.broadcasted_iota(jnp.int32, value.shape, 1) < HEAD_DIM
    zero = jnp.zeros_like(value)
    return jnp.where(left, value, zero), jnp.where(left, zero, value)


def present(hot):
    return jnp.max(hot.astype(full), axis=0, keepdims=True)


def over_units(counts, unit_refs, lanes, own_ids, body):
    flags = [
        jnp.max(own_ids * present(ref[0, 0, :, lanes.hot])) > 0.0 if count == 1 else None
        for count, ref in zip(counts, unit_refs)
    ]
    for number, (count, ref) in enumerate(zip(counts, unit_refs)):
        if count == 1:
            pl.when(flags[number])(functools.partial(body, number, 0))
        else:

            def step(index, carry, number=number, ref=ref):
                shared = jnp.max(own_ids * present(ref[0, index, :, lanes.hot])) > 0.0
                pl.when(shared)(functools.partial(body, number, index))
                return carry

            lax.fori_loop(0, count, step, 0)


def attend_kernel(counts, heads, begin, finish, *refs):
    lanes, pairs, units = Lanes(heads), heads // 2, len(counts)
    own, unit_refs = refs[0], refs[1 : 1 + units]
    refs = refs[1 + units :]
    if not begin:
        acc_in, stat_in = refs[:2]
        refs = refs[2:]
    if finish:
        mixed_keep, mixed_send, lse_out = refs[:3]
        refs = refs[3:]
    else:
        acc_out, stat_out = refs[:2]
        refs = refs[2:]
    q_aug, scores, weights, stat, acc = refs
    span = own.shape[2]
    half = span // 2
    hot_own = own[0, 0, :, lanes.hot]
    penalty = ((hot_own.astype(full) - 1.0) * BIG).astype(low)
    for pair in range(pairs):
        for side, masked in enumerate(split_heads(own[0, 0, :, lanes.of(0, pair)])):
            q_aug[2 * pair + side] = jnp.concatenate([masked, penalty], axis=1)
    if not begin:
        acc[...] = acc_in[0]
        stat[...] = stat_in[0]

    def block(ref, index, first):
        hot = ref[0, index, :, lanes.hot]
        peaks = []
        for pair in range(pairs):
            k_aug = jnp.concatenate([ref[0, index, :, lanes.of(1, pair)], hot], axis=1)
            for side in range(2):
                head = 2 * pair + side
                product = dot_nt(k_aug, q_aug[head])
                scores[head] = product
                peak = jnp.max(product, axis=0, keepdims=True)
                peaks.append(peak if first else jnp.maximum(peak, stat[head : head + 1, :]))
        sums = []
        for head in range(heads):
            weight = jnp.exp(scores[head] - peaks[head])
            sums.append(jnp.sum(weight, axis=0, keepdims=True))
            weights[head] = weight.astype(low)
        for pair in range(pairs):
            turned = ref[0, index, :, lanes.of(2, pair)].T
            for side in range(2):
                head = 2 * pair + side
                rows = slice(head * HEAD_DIM, (head + 1) * HEAD_DIM)
                mix = dot_nn(turned[side * HEAD_DIM : (side + 1) * HEAD_DIM], weights[head])
                total = sums[head]
                if not first:
                    shrink = jnp.exp(stat[head : head + 1, :] - peaks[head])
                    total = total + stat[8 + head : 9 + head, :] * shrink
                    mix = mix + acc[rows, :] * shrink
                acc[rows, :] = mix
                stat[head : head + 1, :] = peaks[head]
                stat[8 + head : 9 + head, :] = total

    if begin:
        block(own, 0, True)
    over_units(
        counts, unit_refs, lanes, present(hot_own), lambda number, index: block(unit_refs[number], index, False)
    )
    if not finish:
        acc_out[0] = acc[...]
        stat_out[0] = stat[...]
        return
    totals = stat[8 : 8 + heads, :]
    lse = stat[0:heads, :] + jnp.log(totals)
    lse_out[0, 0:heads, :] = lse
    lse_out[0, heads:8, :] = jnp.zeros((8 - heads, span), full)
    scale = 1.0 / totals
    for pair in range(pairs):
        chosen = slice(pair * LANES, (pair + 1) * LANES)
        mixed = jnp.concatenate(
            [
                acc[head * HEAD_DIM : (head + 1) * HEAD_DIM, :] * scale[head : head + 1, :]
                for head in (2 * pair, 2 * pair + 1)
            ],
            axis=0,
        ).T.astype(low)
        mixed_keep[0, :, chosen] = mixed[:half]
        mixed_send[0, :half, chosen] = mixed[half:]
    row_of = lax.broadcasted_iota(jnp.int32, (STAT_ROWS, half), 0)
    for column in range(pairs):
        tile = jnp.zeros((STAT_ROWS, half), full)
        for which in range(2):
            row = lse[which * pairs + column : which * pairs + column + 1, half:]
            for kind, part in enumerate(two_parts(row)):
                tile = jnp.where(row_of == kind + 2 * which, part.astype(full), tile)
        mixed_send[0, half:, column * LANES : (column + 1) * LANES] = tile.astype(low)


def stat_row(grad_a, grad_b, at, kind, head, half):
    tile = slice(head * LANES, (head + 1) * LANES)
    parts = []
    for other, ref in enumerate((grad_a, grad_b)):
        row = half + 2 * kind + 4 * other
        parts.append(
            ref[at + (slice(row, row + 1), tile)].astype(full)
            + ref[at + (slice(row + 1, row + 2), tile)].astype(full)
        )
    return jnp.concatenate(parts, axis=1)


def query_grad_kernel(counts, heads, *refs):
    lanes, pairs, units = Lanes(heads), heads // 2, len(counts)
    own, grad_a, grad_b, w_out = refs[:4]
    unit_refs = refs[4 : 4 + units]
    dq_out, dk_out, dv_out, q_aug, d_mix, rows_of, scores, weights, d_scores, acc = refs[4 + units :]
    span = own.shape[2]
    half = span // 2
    hot_own = own[0, 0, :, lanes.hot]
    penalty = ((hot_own.astype(full) - 1.0) * BIG).astype(low)
    d_attn = jnp.concatenate([grad_a[0, :half, :], grad_b[0, :half, :]], axis=0)
    d_mixed = dot_nt(d_attn, w_out[...]).astype(low)
    for pair in range(pairs):
        q_parts = split_heads(own[0, 0, :, lanes.of(0, pair)])
        d_parts = split_heads(d_mixed[:, pair * LANES : (pair + 1) * LANES])
        for side in range(2):
            head = 2 * pair + side
            q_aug[head] = jnp.concatenate([q_parts[side], penalty], axis=1)
            d_mix[head] = d_parts[side]
            rows_of[head : head + 1, :] = stat_row(grad_a, grad_b, (0,), 0, head, half)
            rows_of[8 + head : 9 + head, :] = stat_row(grad_a, grad_b, (0,), 1, head, half)

    def block(ref, index, first):
        hot = ref[0, index, :, lanes.hot]
        for pair in range(pairs):
            k_aug = jnp.concatenate([ref[0, index, :, lanes.of(1, pair)], hot], axis=1)
            for side in range(2):
                head = 2 * pair + side
                scores[head] = dot_nt(k_aug, q_aug[head])
        for pair in range(pairs):
            values = ref[0, index, :, lanes.of(2, pair)]
            for side in range(2):
                head = 2 * pair + side
                weight = jnp.exp(scores[head] - rows_of[head : head + 1, :])
                d_weight = dot_nt(values, d_mix[head])
                d_scores[head] = (weight * (d_weight - rows_of[8 + head : 9 + head, :])).astype(low)
                if first:
                    weights[head] = weight.astype(low)
        for pair in range(pairs):
            turned = ref[0, index, :, lanes.of(1, pair)].T
            for side in range(2):
                head = 2 * pair + side
                rows = slice(head * HEAD_DIM, (head + 1) * HEAD_DIM)
                product = dot_nn(turned[side * HEAD_DIM : (side + 1) * HEAD_DIM], d_scores[head])
                acc[rows, :] = product if first else acc[rows, :] + product
            if first:
                chosen = slice(pair * LANES, (pair + 1) * LANES)
                one, two = 2 * pair, 2 * pair + 1
                dv_out[0, :, chosen] = dot_nn(weights[one], d_mix[one]) + dot_nn(weights[two], d_mix[two])
                dk_out[0, :, chosen] = dot_nn(d_scores[one], q_aug[one, :, :LANES]) + dot_nn(
                    d_scores[two], q_aug[two, :, :LANES]
                )

    block(own, 0, True)
    over_units(
        counts, unit_refs, lanes, present(hot_own), lambda number, index: block(unit_refs[number], index, False)
    )
    for pair in range(pairs):
        chosen = slice(pair * LANES, (pair + 1) * LANES)
        dq_out[0, :, chosen] = (acc[chosen, :] * 0.125).T.astype(low)


def key_grad_kernel(counts, heads, turn_ref, *refs):
    lanes, pairs, units = Lanes(heads), heads // 2, len(counts)
    own, dq_in, dk_in, dv_in, w_out, w_qkv = refs[:6]
    unit_refs = refs[6 : 6 + units]
    a_refs = refs[6 + units : 6 + 2 * units]
    b_refs = refs[6 + 2 * units : 6 + 3 * units]
    d_kv, d_input, k_aug, q_mask, d_mix, scores, weights, d_scores, dk_acc, dv_acc = refs[6 + 3 * units :]
    span = own.shape[2]
    half = span // 2
    local = lanes.local
    turn = turn_ref[0]
    hot_own = own[0, 0, :, lanes.hot]
    for pair in range(pairs):
        k_aug[pair] = jnp.concatenate([own[0, 0, :, lanes.of(1, pair)], hot_own], axis=1)
    dk_acc[...] = dk_in[0]
    dv_acc[...] = dv_in[0]

    def block(number, index):
        ref, grad_a, grad_b = unit_refs[number], a_refs[number], b_refs[number]
        penalty = ((ref[0, index, :, lanes.hot].astype(full) - 1.0) * BIG).astype(low)
        d_attn = jnp.concatenate([grad_a[0, index, :half, :], grad_b[0, index, :half, :]], axis=0)
        d_mixed = dot_nt(d_attn, w_out[...]).astype(low)
        for pair in range(pairs):
            q_parts = split_heads(ref[0, index, :, lanes.of(0, pair)])
            d_parts = split_heads(d_mixed[:, pair * LANES : (pair + 1) * LANES])
            for side in range(2):
                head = 2 * pair + side
                q_mask[head] = q_parts[side]
                d_mix[head] = d_parts[side]
                scores[head] = dot_nt(k_aug[pair], jnp.concatenate([q_parts[side], penalty], axis=1))
        for pair in range(pairs):
            values = own[0, 0, :, lanes.of(2, pair)]
            for side in range(2):
                head = 2 * pair + side
                lse = stat_row(grad_a, grad_b, (0, index), 0, head, half)
                delta = stat_row(grad_a, grad_b, (0, index), 1, head, half)
                weight = jnp.exp(scores[head] - lse)
                d_weight = dot_nt(values, d_mix[head])
                d_scores[head] = (weight * (d_weight - delta)).astype(low)
                weights[head] = weight.astype(low)
        for pair in range(pairs):
            chosen = slice(pair * LANES, (pair + 1) * LANES)
            one, two = 2 * pair, 2 * pair + 1
            dv_acc[:, chosen] += dot_nn(weights[one], d_mix[one]) + dot_nn(weights[two], d_mix[two])
            dk_acc[:, chosen] += dot_nn(d_scores[one], q_mask[one]) + dot_nn(d_scores[two], q_mask[two])

    over_units(counts, unit_refs, lanes, present(hot_own), block)
    half_a = pl.ds(pl.multiple_of(turn * half, half), half)
    half_b = pl.ds(pl.multiple_of((1 - turn) * half, half), half)
    for kind, value in enumerate((dq_in[0], dk_acc[...].astype(low), dv_acc[...].astype(low))):
        chosen = slice(kind * local, (kind + 1) * local)
        product = dot_nt(value, w_qkv[kind])
        total = product if kind == 0 else total + product
        if kind > 0:
            d_kv[0, :, (kind - 1) * local : kind * local] = value
    total = total.astype(low)
    d_input[0, half_a, :] = total[:half]
    d_input[0, half_b, :] = total[half:]


def padded(block):
    return -(-block // 16) * 16


def lane_part(ref, half=None):
    if half is None:
        return lambda lanes: ref[:, lanes]
    return lambda lanes: ref[:, :half, lanes].reshape(ref.shape[0] * half, LANES)


def put_slots(turned, slots, values, owners, block):
    def turn_lanes(step, carry):
        lanes = pl.ds(pl.multiple_of(step * LANES, LANES), LANES)
        start = 0
        for load in values:
            value = load(lanes)
            turned[lanes, start : start + value.shape[0]] = value.astype(turned.dtype).T
            start += value.shape[0]
        return carry

    lax.fori_loop(0, turned.shape[0] // LANES, turn_lanes, 0)
    room = padded(block)
    for slot in range(slots.shape[0] // room):
        source = pl.ds(pl.multiple_of(owners[slot] * block, 16 if block % 16 == 0 else 8), block)
        slots[slot * room : slot * room + block, :] = turned[source, :].astype(low)


def places_of(targets):
    return [(ref, index) for ref in targets for index in range(ref.shape[0])]


def put_blocks(product, targets, block, skip):
    for slot, (ref, index) in enumerate(places_of(targets)):
        start = slot * padded(block)
        ref[index, skip : skip + block, :] = product[start : start + block].astype(low)


def pair_grad_kernel(owners, left_a, left_b, right_a, right_b, *refs):
    targets, (turned, slots) = refs[:-2], refs[-2:]
    block = targets[0].shape[1]

    @pl.when(pl.program_id(0) == 0)
    def _():
        put_slots(turned, slots, [lane_part(part) for part in (left_a, left_b)], owners, block)

    right = jnp.concatenate([right_a[...], right_b[...]], axis=0)
    put_blocks(dot_nn(slots[...], right), targets, block, 0)


def half_rows(part, half):
    return part[:, :half, :].reshape(part.shape[0] * half, -1)


def both_rows(value, half):
    return jnp.concatenate([half_rows(value[:, :half], half), half_rows(value[:, half:], half)], axis=0)


def query_out_grad_kernel(owners, tok_a, tok_b, d_query, d_attn_a, d_attn_b, mixed_a, mixed_b, small, *refs):
    targets, (turned, slots, turned_second, slots_second) = refs[:-4], refs[-4:]
    span, local = d_query.shape[1:]
    half = span // 2
    block = targets[0].shape[1] - STAT_ROWS
    put_slots(turned, slots, [lane_part(part, half) for part in (tok_a, tok_b)], owners, block)
    first = dot_nn(slots[...], both_rows(d_query, half)).astype(low)
    put_slots(turned_second, slots_second, [lane_part(part, half) for part in (d_attn_a, d_attn_b)], owners, block)
    mixed = jnp.concatenate([half_rows(part, half) for part in (mixed_a, mixed_b)], axis=0)
    second = dot_nn(slots_second[...], mixed).astype(low)
    for slot, (ref, index) in enumerate(places_of(targets)):
        start = slot * padded(block)
        for which, product in enumerate((first, second)):
            columns = slice(which * local, (which + 1) * local)
            ref[index, STAT_ROWS:, columns] = product[start : start + block]
        ref[index, :STAT_ROWS, :local] = jnp.zeros((STAT_ROWS, local), low)
        ref[index, :STAT_ROWS, local:] = small[owners[slot]].astype(low)


def key_value_grad_kernel(owners, tok_a, tok_b, d_kv, *refs):
    targets, (turned, slots) = refs[:-2], refs[-2:]
    half = d_kv.shape[1] // 2
    block = targets[0].shape[1]
    put_slots(turned, slots, [lane_part(part, half) for part in (tok_a, tok_b)], owners, block)
    put_blocks(dot_nn(slots[...], both_rows(d_kv, half)), targets, block, 0)


def norm_of(residual):
    center = residual - jnp.mean(residual, axis=-1, keepdims=True)
    inverse = lax.rsqrt(jnp.mean(center * center, axis=-1, keepdims=True) + 1e-06)
    return center * inverse, inverse


def norm_back(d_normal, normal, inverse):
    return inverse * (
        d_normal
        - jnp.mean(d_normal, axis=-1, keepdims=True)
        - normal * jnp.mean(d_normal * normal, axis=-1, keepdims=True)
    )


def middle_kernel(
    chunk,
    turn_ref,
    tok,
    mixed_keep,
    mixed_recv,
    lse_keep,
    w_out_own,
    w_out_oth,
    w_up_own,
    w_up_oth,
    w_down_own,
    w_down_oth,
    gain,
    shift,
    grad_out,
    out,
    d_resid,
    payload,
    active_own,
    active_oth,
    d_up_own,
    d_up_oth,
    d_ffn_out,
    normed_out,
    small,
    slope,
):
    seqs, half, width = out.shape
    rows = seqs * half
    heads = mixed_keep.shape[2] // HEAD_DIM
    keep = mixed_keep[...].reshape(rows, -1)
    recv = mixed_recv[:, :half, :].reshape(rows, -1)
    attn = dot_nn(keep, w_out_own[...]) + dot_nn(recv, w_out_oth[...])
    resid_one = tok[:, :half, :].reshape(rows, width).astype(full) + attn
    normal_one, inverse_one = norm_of(resid_one)
    gain_one, gain_two = gain[0:1, :], gain[1:2, :]
    normed = normal_one * gain_one + shift[0:1, :]
    normed_low = normed.astype(low)
    normed_out[...] = normed_low
    units = w_up_own.shape[0]
    sides = ((w_up_own, w_down_own, active_own, d_up_own), (w_up_oth, w_down_oth, active_oth, d_up_oth))
    ffn = jnp.zeros((rows, width), full)
    for which, (w_up, w_down, active_ref, _) in enumerate(sides):
        for start in range(0, units, chunk):
            part = slice(start, start + chunk)
            upward = dot_nt(normed_low, w_up[part, :])
            spread = 0.5 * (1.0 + lax.erf(upward * 0.7071067811865476))
            active = (upward * spread).astype(low)
            slope[:, which * units + start : which * units + start + chunk] = (
                spread + upward * (jnp.exp(upward * upward * -0.5) * 0.3989422804014327)
            )
            active_ref[:, part] = active
            ffn = ffn + dot_nn(active, w_down[part, :])
    normal_two, inverse_two = norm_of(normed + ffn)
    out[...] = (normal_two * gain_two + shift[1:2, :]).astype(low).reshape(seqs, half, width)
    grad = grad_out[...].reshape(rows, width).astype(full)
    small[1:2, :] = jnp.sum(grad * normal_two, axis=0, keepdims=True)
    small[3:4, :] = jnp.sum(grad, axis=0, keepdims=True)
    d_resid_two = norm_back(grad * gain_two, normal_two, inverse_two)
    d_ffn = d_resid_two.astype(low)
    d_ffn_out[...] = d_ffn
    d_normed = d_resid_two
    for which, (w_up, w_down, _, d_up_ref) in enumerate(sides):
        for start in range(0, units, chunk):
            part = slice(start, start + chunk)
            d_active = dot_nt(d_ffn, w_down[part, :])
            d_up = (d_active * slope[:, which * units + start : which * units + start + chunk]).astype(low)
            d_up_ref[:, part] = d_up
            d_normed = d_normed + dot_nn(d_up, w_up[part, :])
    small[0:1, :] = jnp.sum(d_normed * normal_one, axis=0, keepdims=True)
    small[2:3, :] = jnp.sum(d_normed, axis=0, keepdims=True)
    small[4:8, :] = jnp.zeros((4, width), full)
    d_resid_one = norm_back(d_normed * gain_one, normal_one, inverse_one)
    d_resid[...] = d_resid_one.reshape(seqs, half, width)
    d_attn = d_resid_one.astype(low)
    payload[:, :half, :] = d_attn.reshape(seqs, half, width)
    column_of = lax.broadcasted_iota(jnp.int32, (8, heads * HEAD_DIM), 1) // HEAD_DIM
    chosen = jnp.where(column_of == lax.broadcasted_iota(jnp.int32, (8, heads * HEAD_DIM), 0), 1.0, 0.0)
    deltas = []
    for mixed, w_out in ((keep, w_out_own), (recv, w_out_oth)):
        d_mixed = dot_nt(d_attn, w_out[...]).astype(low).astype(full)
        deltas.append(
            lax.dot_general(
                chosen,
                d_mixed * mixed.astype(full),
                (((1,), (1,)), ((), ())),
                precision=lax.Precision.HIGHEST,
                preferred_element_type=full,
            )
        )
    row_of = lax.broadcasted_iota(jnp.int32, (STAT_ROWS, half), 0)
    pairs = heads // 2
    for seq in range(seqs):
        for head in range(heads):
            lse_high, lse_low = two_parts(lse_keep[seq, head : head + 1, :half])
            tile = slice((head % pairs) * LANES, (head % pairs + 1) * LANES)
            row = half + 2 * (head // pairs)
            parts = [lse_high.astype(full), lse_low.astype(full)]
            for which in range(2):
                piece = deltas[which][head : head + 1, seq * half : (seq + 1) * half]
                if which == 1:
                    parts.append(mixed_recv[seq, row : row + 1, tile].astype(full))
                    parts.append(mixed_recv[seq, row + 1 : row + 2, tile].astype(full))
                parts.extend(part.astype(full) for part in two_parts(piece))
            stat = jnp.zeros((STAT_ROWS, half), full)
            for index, part in enumerate(parts):
                stat = jnp.where(row_of == index, part, stat)
            payload[seq, half:, head * LANES : (head + 1) * LANES] = stat.astype(low)


def slot_order(count):
    if count == 1:
        return [0]
    inner = slot_order(count // 2)
    return [2 * slot + 1 for slot in inner] + [2 * slot for slot in inner]


def reversed_bits(value, bits):
    return sum(((value >> bit) & 1) << (bits - 1 - bit) for bit in range(bits))


def lasting(microseconds):
    return pl.CostEstimate(flops=int(microseconds * 1.15e+09), transcendentals=0, bytes_accessed=0)


def far(value):
    return pltpu.with_memory_space_constraint(value, pltpu.HBM)


def whole(shape):
    return pl.BlockSpec(shape, lambda *_: (0,) * len(shape), pipeline_mode=pl.Buffered(1))


def kernel_params(megabytes):
    return pltpu.CompilerParams(vmem_limit_bytes=megabytes << 20)


def on_device(
    ctx_size,
    dp_size,
    tokens,
    segment_ids,
    w_qkv,
    w_out,
    w_up,
    w_down,
    norm_gain,
    norm_bias,
    grad_out,
):
    seqs, span, width = tokens.shape
    half = span // 2
    local_width = w_out.shape[0]
    heads = local_width // HEAD_DIM
    units_local = w_up.shape[0]
    rows = seqs * half
    long_half = half + STAT_ROWS
    ctx_bits = ctx_size.bit_length() - 1
    turn = lax.axis_index("tensor")
    place = lax.axis_index("ctx")
    row_place = lax.axis_index("dp")
    turn_array = turn.reshape(1)

    def room(megabytes):
        return kernel_params(megabytes if ctx_size <= 4 else 60)

    def swap(value):
        return lax.ppermute(value, "tensor", [(0, 1), (1, 0)])

    def hop(value, stage):
        moves = []
        for spot in range(ctx_size):
            for core in range(2):
                bit = stage if core == 0 else ctx_bits - 1 - stage
                moves.append((spot * 2 + core, (spot ^ (1 << bit)) * 2 + core))
        return lax.ppermute(value, ("ctx", "tensor"), moves)

    def tie(*values):
        return lax.optimization_barrier(values)

    def gather_near(own):
        own = own[:, None]
        return [hop(own, stage) for stage in range(min(ctx_bits, 2))]

    def gather_far(own, near_groups):
        groups = list(near_groups)
        if ctx_bits >= 2:
            groups.append(hop(groups[0], 1))
        for stage in range(2, ctx_bits):
            groups.append(hop(jnp.concatenate([own[:, None]] + groups, axis=1), stage))
        return groups

    def half_of(value, which):
        return lax.dynamic_slice_in_dim(value, which * half, half, 1)

    def with_ids(which):
        ids = half_of(segment_ids, which).astype(low)
        row = jnp.pad(ids[:, None, :], ((0, 0), (0, STAT_ROWS - 1), (0, width - half)))
        return jnp.concatenate([half_of(tokens, which), row], axis=1)

    def units_of(groups):
        direct, swapped = groups[: len(groups) // 2], groups[len(groups) // 2 :]
        if ctx_size == 4:
            return [(direct[0], swapped[1]), (direct[1], swapped[0]), (direct[2], swapped[2])]
        mirror = [reversed_bits(slot, ctx_bits) - 1 for slot in range(1, ctx_size)]
        first, second = jnp.concatenate(direct, axis=1), jnp.concatenate(swapped, axis=1)
        return [(first, jnp.stack([second[:, slot] for slot in mirror], axis=1))]

    block_width = 3 * local_width + LANES
    part_spec = pl.BlockSpec((1, 1, long_half, width), lambda g, s: (s, g, 0, 0))

    def project(part_a, part_b):
        count = part_a.shape[1]
        return pl.pallas_call(
            project_kernel,
            grid=(count, seqs),
            in_specs=[whole(w_qkv.shape), part_spec, part_spec],
            out_specs=pl.BlockSpec((1, 1, span, block_width), lambda g, s: (s, g, 0, 0)),
            out_shape=jax.ShapeDtypeStruct((seqs, count, span, block_width), low),
            compiler_params=room(16),
            cost_estimate=lasting(2),
            name="project",
        )(w_qkv, part_a, part_b)

    tok_a, tok_b = with_ids(turn), with_ids(1 - turn)
    tok_near = gather_near(tok_a)
    w_out_oth, w_up_oth, w_down_oth = swap(w_out), swap(w_up), swap(w_down)
    own = project(tok_a[:, None], tok_b[:, None])

    def seq_spec(shape):
        return pl.BlockSpec((1,) + shape, lambda s, *_: (s,) + (0,) * len(shape))

    def unit_specs(chosen):
        return [
            pl.BlockSpec(
                (1,) + value.shape[1:],
                lambda s, *_: (s, 0, 0, 0),
                pipeline_mode=pl.Buffered(2 if value.shape[1] == 1 else 1),
            )
            for value in chosen
        ]

    head_square = pltpu.VMEM((heads, span, span), full)
    head_square_low = pltpu.VMEM((heads, span, span), low)
    q_scratch = pltpu.VMEM((heads, span, 2 * LANES), low)
    head_rows = pltpu.VMEM((heads, span, LANES), low)

    def attend(chosen, state, finish):
        begin = state is None
        state_shapes = [((local_width, span), full), ((16, span), full)]
        shapes = (
            [((half, local_width), low), ((long_half, local_width), low), ((8, span), full)]
            if finish
            else state_shapes
        )
        state = [] if begin else list(state)
        return pl.pallas_call(
            functools.partial(attend_kernel, [value.shape[1] for value in chosen], heads, begin, finish),
            grid=(seqs,),
            in_specs=unit_specs([own] + chosen) + [seq_spec(value.shape[1:]) for value in state],
            out_specs=[seq_spec(shape) for shape, _ in shapes],
            out_shape=[
                (pltpu.HBM if finish else jax.ShapeDtypeStruct)((seqs,) + shape, kind) for shape, kind in shapes
            ],
            scratch_shapes=[
                q_scratch,
                head_square,
                head_square_low,
                pltpu.VMEM((16, span), full),
                pltpu.VMEM((local_width, span), full),
            ],
            compiler_params=room(14),
            cost_estimate=lasting(3),
            name="attend",
        )(own, *chosen, *state)

    state = attend([], None, False)
    *tok_near, first_state = tie(*tok_near, state[0])
    state = (first_state, state[1])
    tok_groups = gather_far(tok_a, tok_near)
    if ctx_size == 4:
        swapped = [swap(group) for group in tok_groups[:2]]
        near_units = [project(tok_groups[0], swapped[1]), project(tok_groups[1], swapped[0])]
        state = attend(near_units, state, False)
        last, first_state = tie(tok_groups[2], state[0])
        far_units = [project(last, swap(last))]
        units = near_units + far_units
        mixed_keep, mixed_send, lse = attend(far_units, (first_state, state[1]), True)
    else:
        units = [project(*pair) for pair in units_of(tok_groups + [swap(group) for group in tok_groups])]
        mixed_keep, mixed_send, lse = attend(units, state, True)
    mixed_recv = swap(mixed_send)

    middle_in = [
        tok_a,
        mixed_keep,
        mixed_recv,
        lse,
        w_out,
        w_out_oth,
        w_up,
        w_up_oth,
        w_down,
        w_down_oth,
        norm_gain,
        norm_bias,
    ]
    middle_shapes = [
        ((seqs, half, width), low),
        ((seqs, half, width), full),
        ((seqs, long_half, width), low),
        ((rows, units_local), low),
        ((rows, units_local), low),
        ((rows, units_local), low),
        ((rows, units_local), low),
        ((rows, width), low),
        ((rows, width), low),
        ((8, width), full),
    ]
    (
        out_half,
        d_resid,
        payload,
        active_own,
        active_oth,
        d_up_own,
        d_up_oth,
        d_ffn,
        normed_low,
        small,
    ) = pl.pallas_call(
        functools.partial(middle_kernel, min(512, units_local)),
        grid_spec=pltpu.PrefetchScalarGridSpec(
            num_scalar_prefetch=1,
            grid=(1,),
            in_specs=[whole(value.shape) for value in middle_in]
            + [pl.BlockSpec((seqs, half, width), lambda s, turn_ref: (0, turn_ref[0], 0))],
            out_specs=[whole(shape) for shape, _ in middle_shapes],
            scratch_shapes=[pltpu.VMEM((rows, 2 * units_local), full)],
        ),
        out_shape=[
            (jax.ShapeDtypeStruct if number == 2 else pltpu.HBM)(shape, kind)
            for number, (shape, kind) in enumerate(middle_shapes)
        ],
        compiler_params=room(36),
        cost_estimate=lasting(16),
        name="middle",
    )(turn_array, *middle_in, grad_out)

    order = slot_order(ctx_size)
    mirrored = [reversed_bits(slot, ctx_bits) for slot in order]
    owners = place ^ jnp.where(turn == 0, jnp.array(order, jnp.int32), jnp.array(mirrored, jnp.int32))
    quarter = width // ctx_size
    stages = [ctx_size >> (stage + 1) for stage in range(ctx_bits)] + [1]
    turned_kind = low if quarter % 16 == 0 else full
    chunk = min(512, units_local)

    def slot_scratch(count):
        return [pltpu.VMEM((width, count), turned_kind), pltpu.VMEM((ctx_size * padded(quarter), count), low)]

    def pair_grad(left_a, left_b, right_a, right_b, name):
        right_spec = pl.BlockSpec((rows, chunk), lambda n, *_: (0, n))
        return pl.pallas_call(
            pair_grad_kernel,
            grid_spec=pltpu.PrefetchScalarGridSpec(
                num_scalar_prefetch=1,
                grid=(units_local // chunk,),
                in_specs=[whole(left_a.shape), whole(left_b.shape), right_spec, right_spec],
                out_specs=[pl.BlockSpec((count, quarter, chunk), lambda n, *_: (0, 0, n)) for count in stages],
                scratch_shapes=slot_scratch(2 * rows),
            ),
            out_shape=[pltpu.HBM((count, quarter, units_local), low) for count in stages],
            compiler_params=room(16),
            cost_estimate=lasting(5.5),
            name=name,
        )(owners, *map(far, (left_a, left_b, right_a, right_b)))

    parity = row_place & 1

    def add_up(values):
        return sum(value.astype(full) for value in values)

    def send_stage(parts, gots, stage):
        count, start = parts[stage].shape[0], 0
        values = [parts[stage]]
        for got in gots:
            start = got.shape[0] - sum(part.shape[0] for part in parts[stage:])
            values.append(got[start : start + count])
        return add_up(values).astype(low)

    def own_half(parts, gots, which):
        values = [parts[-1]] + gots
        split = parts[-1].shape[1] // 2
        return add_up(
            [
                lax.dynamic_slice(value, (value.shape[0] - 1, which * split, 0), (1, split, value.shape[2]))
                for value in values
            ]
        )[0]

    class Blocks:
        def __init__(self, parts):
            self.parts, self.gots, self.stage, self.sent = list(parts), [], 0, None
            self.dp_stage, self.got = 0, None

        @property
        def arrived(self):
            return self.gots[-1] if self.dp_stage == 0 else self.got

        @arrived.setter
        def arrived(self, value):
            if self.dp_stage == 0:
                self.gots[-1] = value
            else:
                self.got = value

        def ready(self):
            if self.stage < ctx_bits:
                self.sent = send_stage(self.parts, self.gots, self.stage) if self.stage else self.parts[0]
            elif self.dp_stage == 0:
                self.sent = own_half(self.parts, self.gots, 1 - parity).astype(low)
            else:
                mine = own_half(self.parts, self.gots, parity) if self.dp_stage == 1 else self.sent.astype(full)
                self.sent = (mine + self.got.astype(full)).astype(low)

        def send(self):
            if self.stage < ctx_bits:
                self.gots.append(hop(self.sent, self.stage))
                self.stage += 1
                return
            last = self.dp_stage == dp_size.bit_length() - 1
            bit = 0 if last else self.dp_stage
            moves = [(spot, spot ^ (1 << bit)) for spot in range(dp_size)]
            self.got = lax.ppermute(self.sent, "dp", moves)
            self.dp_stage += 1

        def advance(self, *after):
            if self.gots:
                self.arrived = tie(self.arrived, *after)[0]
            elif after:
                self.parts[0] = tie(self.parts[0], *after)[0]
            self.ready()
            self.send()
            return self.sent

        def total(self):
            while self.dp_stage < dp_size.bit_length():
                self.advance()
            mine, other = self.sent, self.got
            return jnp.where(
                parity == 0, jnp.concatenate([mine, other], axis=0), jnp.concatenate([other, mine], axis=0)
            ).astype(full)

    grad_near = gather_near(payload)
    payload_b = swap(payload)
    d_ffn_b, active_b = swap(d_ffn), swap(active_oth)
    normed_b, d_up_b = swap(normed_low), swap(d_up_oth)
    down = Blocks(pair_grad(d_ffn, d_ffn_b, active_own, active_b, "grad_down"))
    latest = down.advance()
    normed_low, latest = tie(normed_low, latest)
    up = Blocks(pair_grad(normed_low, normed_b, d_up_own, d_up_b, "grad_up"))
    *grad_near, up.parts[0] = tie(*grad_near, up.parts[0])
    latest = up.advance()
    own_back, latest = tie(own, latest)
    grad_far = gather_far(payload, grad_near)
    crossed = [swap(group) for group in grad_far[:-1]]

    sum_shape = pltpu.HBM((seqs, span, local_width), full)
    row_shape = pltpu.HBM((seqs, span, local_width), low)
    grad_spec = seq_spec((long_half, width))
    span_spec = seq_spec((span, local_width))
    counts = [value.shape[1] for value in units]
    d_query, dk_sum, dv_sum = pl.pallas_call(
        functools.partial(query_grad_kernel, counts, heads),
        grid=(seqs,),
        in_specs=unit_specs([own]) + [grad_spec, grad_spec, whole(w_out.shape)] + unit_specs(units),
        out_specs=[span_spec] * 3,
        out_shape=[row_shape, sum_shape, sum_shape],
        scratch_shapes=[
            q_scratch,
            head_rows,
            pltpu.VMEM((16, span), full),
            head_square,
            head_square_low,
            head_square_low,
            pltpu.VMEM((local_width, span), full),
        ],
        compiler_params=room(20),
        cost_estimate=lasting(11),
        name="query_grad",
    )(own_back, payload, payload_b, far(w_out), *units)

    def sequence_grad(kernel, values, lefts, extra, columns, name):
        return Blocks(
            pl.pallas_call(
                kernel,
                grid_spec=pltpu.PrefetchScalarGridSpec(
                    num_scalar_prefetch=1,
                    grid=(1,),
                    in_specs=[whole(value.shape) for value in values],
                    out_specs=[whole((count, extra + quarter, columns)) for count in stages],
                    scratch_shapes=slot_scratch(seqs * span) * lefts,
                ),
                out_shape=[pltpu.HBM((count, extra + quarter, columns), low) for count in stages],
                compiler_params=room(20),
                cost_estimate=lasting(5.5),
                name=name,
            )(owners, *map(far, values))
        )

    small_rows = (small[:4] + swap(small)[:4]).reshape(4, ctx_size, quarter).transpose(1, 0, 2)
    small_rows = jnp.pad(small_rows, ((0, 0), (0, STAT_ROWS - 4), (0, local_width - quarter)))
    latest = down.advance(d_query)
    d_query, latest = tie(d_query, latest)
    query_out = sequence_grad(
        query_out_grad_kernel,
        (tok_a, tok_b, d_query, payload, payload_b, mixed_keep, mixed_send, small_rows),
        2,
        STAT_ROWS,
        2 * local_width,
        "query_out_grad",
    )
    grad_far[-1], query_out.parts[1] = tie(grad_far[-1], query_out.parts[1])
    crossed.append(swap(grad_far[-1]))
    latest = query_out.advance()
    latest = down.advance(latest)
    d_query, latest = tie(d_query, latest)
    grad_units = units_of(grad_far + crossed)
    grad_a, grad_b = [pair[0] for pair in grad_units], [pair[1] for pair in grad_units]
    d_kv, d_input = pl.pallas_call(
        functools.partial(key_grad_kernel, counts, heads),
        grid_spec=pltpu.PrefetchScalarGridSpec(
            num_scalar_prefetch=1,
            grid=(seqs,),
            in_specs=unit_specs([own])
            + [span_spec] * 3
            + [whole(w_out.shape), whole(w_qkv.shape)]
            + unit_specs(units + grad_a + grad_b),
            out_specs=[seq_spec((span, 2 * local_width)), seq_spec((span, width))],
            scratch_shapes=[
                pltpu.VMEM((heads // 2, span, 2 * LANES), low),
                head_rows,
                head_rows,
                head_square,
                head_square_low,
                head_square_low,
                pltpu.VMEM((span, local_width), full),
                pltpu.VMEM((span, local_width), full),
            ],
        ),
        out_shape=[
            jax.ShapeDtypeStruct((seqs, span, 2 * local_width), low),
            jax.ShapeDtypeStruct((seqs, span, width), low),
        ],
        compiler_params=room(26),
        cost_estimate=lasting(12.5),
        name="key_grad",
    )(turn_array, own, *map(far, (d_query, dk_sum, dv_sum, w_out, w_qkv, *units, *grad_a, *grad_b)))

    latest = up.advance(d_kv)
    latest = down.advance(latest)
    latest = query_out.advance(latest)
    d_kv, latest = tie(d_kv, latest)
    key_value = sequence_grad(key_value_grad_kernel, (tok_a, tok_b, d_kv), 1, 0, 2 * local_width, "key_value_grad")
    latest = key_value.advance()
    out_half, d_resid, d_input, latest = tie(out_half, d_resid, d_input, latest)
    swapped = [swap(out_half), swap(d_resid), swap(d_input)]
    for blocks in (up, down, key_value, query_out):
        latest = blocks.advance(latest)

    def both_halves(mine, other):
        return jnp.where(
            turn == 0, jnp.concatenate([mine, other], axis=1), jnp.concatenate([other, mine], axis=1)
        )

    *swapped, latest = tie(*swapped, latest)
    outputs = both_halves(out_half, swapped[0])
    grad_tokens = d_input.astype(full) + swapped[2].astype(full) + both_halves(d_resid, swapped[1])
    outputs, grad_tokens, latest = tie(outputs, grad_tokens, latest)
    for blocks in (up, key_value, query_out, up, key_value, query_out, key_value):
        latest = blocks.advance(latest)
    down_total, up_total = down.total(), up.total()
    query_out_total, key_value_total = query_out.total(), key_value.total()
    small_total = query_out_total[:4, local_width : local_width + quarter]
    query_out_total = query_out_total[STAT_ROWS:]
    return (
        outputs,
        grad_tokens,
        jnp.stack(
            [query_out_total[:, :local_width], key_value_total[:, :local_width], key_value_total[:, local_width:]]
        ),
        query_out_total[:, local_width:].T,
        up_total.T,
        down_total.T,
        small_total[0:2],
        small_total[2:4],
    )


def solution(mesh):
    return jax.shard_map(
        functools.partial(on_device, mesh.shape["ctx"], mesh.shape["dp"]),
        mesh=mesh,
        in_specs=(
            P("dp", "ctx", None),
            P("dp", "ctx"),
            P(None, None, "tensor"),
            P("tensor", None),
            P("tensor", None),
            P("tensor", None),
            P(),
            P(),
            P("dp", "ctx", None),
        ),
        out_specs=(
            P("dp", "ctx", None),
            P("dp", "ctx", None),
            P(None, "ctx", "tensor"),
            P("tensor", "ctx"),
            P("tensor", "ctx"),
            P("tensor", "ctx"),
            P(None, "ctx"),
            P(None, "ctx"),
        ),
        check_vma=False,
    )
```

```python
import functools
import jax
import jax.numpy as jnp
from jax import lax
from jax.experimental import pallas as pl
from jax.experimental.pallas import tpu as pltpu
from jax.sharding import PartitionSpec as P

HEAD_DIM = 64
LANES = 128
STAT_ROWS = 8
SMALL_ROWS = 16
BIG = 2.0**30
low, full = jnp.bfloat16, jnp.float32


def dot_nn(left, right):
    return lax.dot_general(left, right, (((1,), (0,)), ((), ())), preferred_element_type=full)


def dot_nt(left, right):
    return lax.dot_general(left, right, (((1,), (1,)), ((), ())), preferred_element_type=full)


def dot_tn(left, right):
    return lax.dot_general(left, right, (((0,), (0,)), ((), ())), preferred_element_type=full)


def two_parts(values):
    high = values.astype(low)
    return high, (values - high.astype(full)).astype(low)


def project_kernel(w_qkv, part_a, part_b, out):
    half = part_a.shape[2] - STAT_ROWS
    local = w_qkv.shape[2]
    rows = jnp.concatenate([part[0, 0, :half, :] for part in (part_a, part_b)], axis=0)
    for kind in range(3):
        product = dot_nn(rows, w_qkv[kind])
        if kind == 0:
            product = product * 0.125
        out[0, 0, :, kind * local : (kind + 1) * local] = product.astype(low)
    ids = lax.broadcasted_iota(jnp.int32, (LANES, half), 0).astype(full)
    for which, part in enumerate((part_a, part_b)):
        row = part[0, 0, half : half + 1, :half].astype(full)
        out[0, 0, which * half : (which + 1) * half, 3 * local :] = jnp.where(ids == row, 1.0, 0.0).T.astype(low)


class Lanes:
    def __init__(self, heads):
        self.local = heads * HEAD_DIM

    def of(self, kind, pair):
        start = kind * self.local + pair * LANES
        return slice(start, start + LANES)

    @property
    def hot(self):
        return slice(3 * self.local, 3 * self.local + LANES)


def split_heads(value):
    left = lax.broadcasted_iota(jnp.int32, value.shape, 1) < HEAD_DIM
    zero = jnp.zeros_like(value)
    return jnp.where(left, value, zero), jnp.where(left, zero, value)


def present(hot):
    return jnp.max(hot.astype(full), axis=0, keepdims=True)


def over_units(counts, unit_refs, lanes, own_ids, body):
    flags = [
        jnp.max(own_ids * present(ref[0, 0, :, lanes.hot])) > 0.0 if count == 1 else None
        for count, ref in zip(counts, unit_refs)
    ]
    for number, (count, ref) in enumerate(zip(counts, unit_refs)):
        if count == 1:
            pl.when(flags[number])(functools.partial(body, number, 0))
        else:

            def step(index, carry, number=number, ref=ref):
                shared = jnp.max(own_ids * present(ref[0, index, :, lanes.hot])) > 0.0
                pl.when(shared)(functools.partial(body, number, index))
                return carry

            lax.fori_loop(0, count, step, 0)


def attend_kernel(counts, heads, begin, finish, *refs):
    lanes, pairs, units = Lanes(heads), heads // 2, len(counts)
    own, unit_refs = refs[0], refs[1 : 1 + units]
    refs = refs[1 + units :]
    if not begin:
        acc_in, stat_in = refs[:2]
        refs = refs[2:]
    if finish:
        mixed_keep, mixed_send, lse_out = refs[:3]
        refs = refs[3:]
    else:
        acc_out, stat_out = refs[:2]
        refs = refs[2:]
    q_aug, scores, weights, stat, acc = refs
    span = own.shape[2]
    half = span // 2
    hot_own = own[0, 0, :, lanes.hot]
    penalty = ((hot_own.astype(full) - 1.0) * BIG).astype(low)
    for pair in range(pairs):
        for side, masked in enumerate(split_heads(own[0, 0, :, lanes.of(0, pair)])):
            q_aug[2 * pair + side] = jnp.concatenate([masked, penalty], axis=1)
    if not begin:
        acc[...] = acc_in[0]
        stat[...] = stat_in[0]

    def block(ref, index, first):
        hot = ref[0, index, :, lanes.hot]
        peaks = []
        for pair in range(pairs):
            k_aug = jnp.concatenate([ref[0, index, :, lanes.of(1, pair)], hot], axis=1)
            for side in range(2):
                head = 2 * pair + side
                product = dot_nt(k_aug, q_aug[head])
                scores[head] = product
                peak = jnp.max(product, axis=0, keepdims=True)
                peaks.append(peak if first else jnp.maximum(peak, stat[head : head + 1, :]))
        sums = []
        for head in range(heads):
            weight = jnp.exp(scores[head] - peaks[head])
            sums.append(jnp.sum(weight, axis=0, keepdims=True))
            weights[head] = weight.astype(low)
        for pair in range(pairs):
            turned = ref[0, index, :, lanes.of(2, pair)].T
            for side in range(2):
                head = 2 * pair + side
                rows = slice(head * HEAD_DIM, (head + 1) * HEAD_DIM)
                mix = dot_nn(turned[side * HEAD_DIM : (side + 1) * HEAD_DIM], weights[head])
                total = sums[head]
                if not first:
                    shrink = jnp.exp(stat[head : head + 1, :] - peaks[head])
                    total = total + stat[8 + head : 9 + head, :] * shrink
                    mix = mix + acc[rows, :] * shrink
                acc[rows, :] = mix
                stat[head : head + 1, :] = peaks[head]
                stat[8 + head : 9 + head, :] = total

    if begin:
        block(own, 0, True)
    over_units(
        counts, unit_refs, lanes, present(hot_own), lambda number, index: block(unit_refs[number], index, False)
    )
    if not finish:
        acc_out[0] = acc[...]
        stat_out[0] = stat[...]
        return
    totals = stat[8 : 8 + heads, :]
    lse = stat[0:heads, :] + jnp.log(totals)
    lse_out[0, 0:heads, :] = lse
    lse_out[0, heads:8, :] = jnp.zeros((8 - heads, span), full)
    scale = 1.0 / totals
    for pair in range(pairs):
        chosen = slice(pair * LANES, (pair + 1) * LANES)
        mixed = jnp.concatenate(
            [
                acc[head * HEAD_DIM : (head + 1) * HEAD_DIM, :] * scale[head : head + 1, :]
                for head in (2 * pair, 2 * pair + 1)
            ],
            axis=0,
        ).T.astype(low)
        mixed_keep[0, :, chosen] = mixed[:half]
        mixed_send[0, :half, chosen] = mixed[half:]
    row_of = lax.broadcasted_iota(jnp.int32, (STAT_ROWS, half), 0)
    for column in range(pairs):
        tile = jnp.zeros((STAT_ROWS, half), full)
        for which in range(2):
            row = lse[which * pairs + column : which * pairs + column + 1, half:]
            for kind, part in enumerate(two_parts(row)):
                tile = jnp.where(row_of == kind + 2 * which, part.astype(full), tile)
        mixed_send[0, half:, column * LANES : (column + 1) * LANES] = tile.astype(low)


def stat_row(grad_a, grad_b, at, kind, head, half):
    tile = slice(head * LANES, (head + 1) * LANES)
    parts = []
    for other, ref in enumerate((grad_a, grad_b)):
        row = half + 2 * kind + 4 * other
        parts.append(
            ref[at + (slice(row, row + 1), tile)].astype(full)
            + ref[at + (slice(row + 1, row + 2), tile)].astype(full)
        )
    return jnp.concatenate(parts, axis=1)


def query_grad_kernel(counts, heads, *refs):
    lanes, pairs, units = Lanes(heads), heads // 2, len(counts)
    own, grad_a, grad_b, w_out = refs[:4]
    unit_refs = refs[4 : 4 + units]
    dq_out, dk_out, dv_out, q_aug, d_mix, rows_of, scores, weights, d_scores, acc = refs[4 + units :]
    span = own.shape[2]
    half = span // 2
    hot_own = own[0, 0, :, lanes.hot]
    penalty = ((hot_own.astype(full) - 1.0) * BIG).astype(low)
    d_attn = jnp.concatenate([grad_a[0, :half, :], grad_b[0, :half, :]], axis=0)
    d_mixed = dot_nt(d_attn, w_out[...]).astype(low)
    for pair in range(pairs):
        q_parts = split_heads(own[0, 0, :, lanes.of(0, pair)])
        d_parts = split_heads(d_mixed[:, pair * LANES : (pair + 1) * LANES])
        for side in range(2):
            head = 2 * pair + side
            q_aug[head] = jnp.concatenate([q_parts[side], penalty], axis=1)
            d_mix[head] = d_parts[side]
            rows_of[head : head + 1, :] = stat_row(grad_a, grad_b, (0,), 0, head, half)
            rows_of[8 + head : 9 + head, :] = stat_row(grad_a, grad_b, (0,), 1, head, half)

    def block(ref, index, first):
        hot = ref[0, index, :, lanes.hot]
        for pair in range(pairs):
            k_aug = jnp.concatenate([ref[0, index, :, lanes.of(1, pair)], hot], axis=1)
            for side in range(2):
                head = 2 * pair + side
                scores[head] = dot_nt(k_aug, q_aug[head])
        for pair in range(pairs):
            values = ref[0, index, :, lanes.of(2, pair)]
            for side in range(2):
                head = 2 * pair + side
                weight = jnp.exp(scores[head] - rows_of[head : head + 1, :])
                d_weight = dot_nt(values, d_mix[head])
                d_scores[head] = (weight * (d_weight - rows_of[8 + head : 9 + head, :])).astype(low)
                if first:
                    weights[head] = weight.astype(low)
        for pair in range(pairs):
            turned = ref[0, index, :, lanes.of(1, pair)].T
            for side in range(2):
                head = 2 * pair + side
                rows = slice(head * HEAD_DIM, (head + 1) * HEAD_DIM)
                product = dot_nn(turned[side * HEAD_DIM : (side + 1) * HEAD_DIM], d_scores[head])
                acc[rows, :] = product if first else acc[rows, :] + product
            if first:
                chosen = slice(pair * LANES, (pair + 1) * LANES)
                one, two = 2 * pair, 2 * pair + 1
                dv_out[0, :, chosen] = dot_nn(weights[one], d_mix[one]) + dot_nn(weights[two], d_mix[two])
                dk_out[0, :, chosen] = dot_nn(d_scores[one], q_aug[one, :, :LANES]) + dot_nn(
                    d_scores[two], q_aug[two, :, :LANES]
                )

    block(own, 0, True)
    over_units(
        counts, unit_refs, lanes, present(hot_own), lambda number, index: block(unit_refs[number], index, False)
    )
    for pair in range(pairs):
        chosen = slice(pair * LANES, (pair + 1) * LANES)
        dq_out[0, :, chosen] = (acc[chosen, :] * 0.125).T.astype(low)


def key_grad_kernel(counts, heads, turn_ref, *refs):
    lanes, pairs, units = Lanes(heads), heads // 2, len(counts)
    own, dq_in, dk_in, dv_in, w_out, w_qkv = refs[:6]
    unit_refs = refs[6 : 6 + units]
    a_refs = refs[6 + units : 6 + 2 * units]
    b_refs = refs[6 + 2 * units : 6 + 3 * units]
    d_kv, d_input, k_aug, q_mask, d_mix, scores, weights, d_scores, dk_acc, dv_acc = refs[6 + 3 * units :]
    span = own.shape[2]
    half = span // 2
    local = lanes.local
    turn = turn_ref[0]
    hot_own = own[0, 0, :, lanes.hot]
    for pair in range(pairs):
        k_aug[pair] = jnp.concatenate([own[0, 0, :, lanes.of(1, pair)], hot_own], axis=1)
    dk_acc[...] = dk_in[0]
    dv_acc[...] = dv_in[0]

    def block(number, index):
        ref, grad_a, grad_b = unit_refs[number], a_refs[number], b_refs[number]
        penalty = ((ref[0, index, :, lanes.hot].astype(full) - 1.0) * BIG).astype(low)
        d_attn = jnp.concatenate([grad_a[0, index, :half, :], grad_b[0, index, :half, :]], axis=0)
        d_mixed = dot_nt(d_attn, w_out[...]).astype(low)
        for pair in range(pairs):
            q_parts = split_heads(ref[0, index, :, lanes.of(0, pair)])
            d_parts = split_heads(d_mixed[:, pair * LANES : (pair + 1) * LANES])
            for side in range(2):
                head = 2 * pair + side
                q_mask[head] = q_parts[side]
                d_mix[head] = d_parts[side]
                scores[head] = dot_nt(k_aug[pair], jnp.concatenate([q_parts[side], penalty], axis=1))
        for pair in range(pairs):
            values = own[0, 0, :, lanes.of(2, pair)]
            for side in range(2):
                head = 2 * pair + side
                lse = stat_row(grad_a, grad_b, (0, index), 0, head, half)
                delta = stat_row(grad_a, grad_b, (0, index), 1, head, half)
                weight = jnp.exp(scores[head] - lse)
                d_weight = dot_nt(values, d_mix[head])
                d_scores[head] = (weight * (d_weight - delta)).astype(low)
                weights[head] = weight.astype(low)
        for pair in range(pairs):
            chosen = slice(pair * LANES, (pair + 1) * LANES)
            one, two = 2 * pair, 2 * pair + 1
            dv_acc[:, chosen] += dot_nn(weights[one], d_mix[one]) + dot_nn(weights[two], d_mix[two])
            dk_acc[:, chosen] += dot_nn(d_scores[one], q_mask[one]) + dot_nn(d_scores[two], q_mask[two])

    over_units(counts, unit_refs, lanes, present(hot_own), block)
    half_a = pl.ds(pl.multiple_of(turn * half, half), half)
    half_b = pl.ds(pl.multiple_of((1 - turn) * half, half), half)
    for kind, value in enumerate((dq_in[0], dk_acc[...].astype(low), dv_acc[...].astype(low))):
        chosen = slice(kind * local, (kind + 1) * local)
        product = dot_nt(value, w_qkv[kind])
        total = product if kind == 0 else total + product
        if kind > 0:
            d_kv[0, :, (kind - 1) * local : kind * local] = value
    total = total.astype(low)
    d_input[0, half_a, :] = total[:half]
    d_input[0, half_b, :] = total[half:]


def padded(block):
    return -(-block // 16) * 16


def lane_part(ref, half=None):
    if half is None:
        return lambda lanes: ref[:, lanes]
    return lambda lanes: ref[:, :half, lanes].reshape(ref.shape[0] * half, LANES)


def put_slots(turned, slots, values, owners, block):
    def turn_lanes(step, carry):
        lanes = pl.ds(pl.multiple_of(step * LANES, LANES), LANES)
        start = 0
        for load in values:
            value = load(lanes)
            turned[lanes, start : start + value.shape[0]] = value.astype(turned.dtype).T
            start += value.shape[0]
        return carry

    lax.fori_loop(0, turned.shape[0] // LANES, turn_lanes, 0)
    room = padded(block)
    for slot in range(slots.shape[0] // room):
        source = pl.ds(pl.multiple_of(owners[slot] * block, 16 if block % 16 == 0 else 8), block)
        slots[slot * room : slot * room + block, :] = turned[source, :].astype(low)


def places_of(targets):
    return [(ref, index) for ref in targets for index in range(ref.shape[0])]


def put_blocks(product, targets, block, skip):
    for slot, (ref, index) in enumerate(places_of(targets)):
        start = slot * padded(block)
        ref[index, skip : skip + block, :] = product[start : start + block].astype(low)


def pair_grad_kernel(owners, left_a, left_b, right_a, right_b, *refs):
    targets, (turned, slots) = refs[:-2], refs[-2:]
    block = targets[0].shape[1]

    @pl.when(pl.program_id(0) == 0)
    def _():
        put_slots(turned, slots, [lane_part(part) for part in (left_a, left_b)], owners, block)

    right = jnp.concatenate([right_a[...], right_b[...]], axis=0)
    put_blocks(dot_nn(slots[...], right), targets, block, 0)


def half_rows(part, half):
    return part[:, :half, :].reshape(part.shape[0] * half, -1)


def both_rows(value, half):
    return jnp.concatenate([half_rows(value[:, :half], half), half_rows(value[:, half:], half)], axis=0)


def query_out_grad_kernel(owners, tok_a, tok_b, d_query, d_attn_a, d_attn_b, mixed_a, mixed_b, small, *refs):
    targets, (turned, slots, turned_second, slots_second) = refs[:-4], refs[-4:]
    span, local = d_query.shape[1:]
    half = span // 2
    block = targets[0].shape[1] - SMALL_ROWS
    put_slots(turned, slots, [lane_part(part, half) for part in (tok_a, tok_b)], owners, block)
    first = dot_nn(slots[...], both_rows(d_query, half)).astype(low)
    put_slots(turned_second, slots_second, [lane_part(part, half) for part in (d_attn_a, d_attn_b)], owners, block)
    mixed = jnp.concatenate([half_rows(part, half) for part in (mixed_a, mixed_b)], axis=0)
    second = dot_nn(slots_second[...], mixed).astype(low)
    for slot, (ref, index) in enumerate(places_of(targets)):
        start = slot * padded(block)
        for which, product in enumerate((first, second)):
            columns = slice(which * local, (which + 1) * local)
            ref[index, SMALL_ROWS:, columns] = product[start : start + block]
        ref[index, :SMALL_ROWS, :local] = jnp.zeros((SMALL_ROWS, local), low)
        ref[index, :SMALL_ROWS, local:] = small[owners[slot]].astype(low)


def key_value_grad_kernel(owners, tok_a, tok_b, d_kv, *refs):
    targets, (turned, slots) = refs[:-2], refs[-2:]
    half = d_kv.shape[1] // 2
    block = targets[0].shape[1]
    put_slots(turned, slots, [lane_part(part, half) for part in (tok_a, tok_b)], owners, block)
    put_blocks(dot_nn(slots[...], both_rows(d_kv, half)), targets, block, 0)


def norm_of(residual):
    center = residual - jnp.mean(residual, axis=-1, keepdims=True)
    inverse = lax.rsqrt(jnp.mean(center * center, axis=-1, keepdims=True) + 1e-06)
    return center * inverse, inverse


def norm_back(d_normal, normal, inverse):
    return inverse * (
        d_normal
        - jnp.mean(d_normal, axis=-1, keepdims=True)
        - normal * jnp.mean(d_normal * normal, axis=-1, keepdims=True)
    )


def middle_kernel(
    chunk,
    turn_ref,
    tok,
    mixed_keep,
    mixed_recv,
    lse_keep,
    w_out_own,
    w_out_oth,
    w_up_own,
    w_up_oth,
    w_down_own,
    w_down_oth,
    gain,
    shift,
    grad_out,
    out,
    d_resid,
    payload,
    active_own,
    active_oth,
    d_up_own,
    d_up_oth,
    d_ffn_out,
    normed_out,
    small,
    slope,
):
    seqs, half, width = out.shape
    rows = seqs * half
    heads = mixed_keep.shape[2] // HEAD_DIM
    keep = mixed_keep[...].reshape(rows, -1)
    recv = mixed_recv[:, :half, :].reshape(rows, -1)
    attn = dot_nn(keep, w_out_own[...]) + dot_nn(recv, w_out_oth[...])
    resid_one = tok[:, :half, :].reshape(rows, width).astype(full) + attn
    normal_one, inverse_one = norm_of(resid_one)
    gain_one, gain_two = gain[0:1, :], gain[1:2, :]
    normed = normal_one * gain_one + shift[0:1, :]
    normed_low = normed.astype(low)
    normed_out[...] = normed_low
    units = w_up_own.shape[0]
    sides = ((w_up_own, w_down_own, active_own, d_up_own), (w_up_oth, w_down_oth, active_oth, d_up_oth))
    ffn = jnp.zeros((rows, width), full)
    for which, (w_up, w_down, active_ref, _) in enumerate(sides):
        for start in range(0, units, chunk):
            part = slice(start, start + chunk)
            upward = dot_nt(normed_low, w_up[part, :])
            spread = 0.5 * (1.0 + lax.erf(upward * 0.7071067811865476))
            active = (upward * spread).astype(low)
            slope[:, which * units + start : which * units + start + chunk] = (
                spread + upward * (jnp.exp(upward * upward * -0.5) * 0.3989422804014327)
            )
            active_ref[:, part] = active
            ffn = ffn + dot_nn(active, w_down[part, :])
    normal_two, inverse_two = norm_of(normed + ffn)
    out[...] = (normal_two * gain_two + shift[1:2, :]).astype(low).reshape(seqs, half, width)
    grad = grad_out[...].reshape(rows, width).astype(full)
    small[1:2, :] = jnp.sum(grad * normal_two, axis=0, keepdims=True)
    small[3:4, :] = jnp.sum(grad, axis=0, keepdims=True)
    d_resid_two = norm_back(grad * gain_two, normal_two, inverse_two)
    d_ffn = d_resid_two.astype(low)
    d_ffn_out[...] = d_ffn
    d_normed = d_resid_two
    for which, (w_up, w_down, _, d_up_ref) in enumerate(sides):
        for start in range(0, units, chunk):
            part = slice(start, start + chunk)
            d_active = dot_nt(d_ffn, w_down[part, :])
            d_up = (d_active * slope[:, which * units + start : which * units + start + chunk]).astype(low)
            d_up_ref[:, part] = d_up
            d_normed = d_normed + dot_nn(d_up, w_up[part, :])
    small[0:1, :] = jnp.sum(d_normed * normal_one, axis=0, keepdims=True)
    small[2:3, :] = jnp.sum(d_normed, axis=0, keepdims=True)
    small[4:8, :] = jnp.zeros((4, width), full)
    d_resid_one = norm_back(d_normed * gain_one, normal_one, inverse_one)
    d_resid[...] = d_resid_one.reshape(seqs, half, width)
    d_attn = d_resid_one.astype(low)
    payload[:, :half, :] = d_attn.reshape(seqs, half, width)
    column_of = lax.broadcasted_iota(jnp.int32, (8, heads * HEAD_DIM), 1) // HEAD_DIM
    chosen = jnp.where(column_of == lax.broadcasted_iota(jnp.int32, (8, heads * HEAD_DIM), 0), 1.0, 0.0)
    deltas = []
    for mixed, w_out in ((keep, w_out_own), (recv, w_out_oth)):
        d_mixed = dot_nt(d_attn, w_out[...]).astype(low).astype(full)
        deltas.append(
            lax.dot_general(
                chosen,
                d_mixed * mixed.astype(full),
                (((1,), (1,)), ((), ())),
                precision=lax.Precision.HIGHEST,
                preferred_element_type=full,
            )
        )
    row_of = lax.broadcasted_iota(jnp.int32, (STAT_ROWS, half), 0)
    pairs = heads // 2
    for seq in range(seqs):
        for head in range(heads):
            lse_high, lse_low = two_parts(lse_keep[seq, head : head + 1, :half])
            tile = slice((head % pairs) * LANES, (head % pairs + 1) * LANES)
            row = half + 2 * (head // pairs)
            parts = [lse_high.astype(full), lse_low.astype(full)]
            for which in range(2):
                piece = deltas[which][head : head + 1, seq * half : (seq + 1) * half]
                if which == 1:
                    parts.append(mixed_recv[seq, row : row + 1, tile].astype(full))
                    parts.append(mixed_recv[seq, row + 1 : row + 2, tile].astype(full))
                parts.extend(part.astype(full) for part in two_parts(piece))
            stat = jnp.zeros((STAT_ROWS, half), full)
            for index, part in enumerate(parts):
                stat = jnp.where(row_of == index, part, stat)
            payload[seq, half:, head * LANES : (head + 1) * LANES] = stat.astype(low)


def slot_order(count):
    if count == 1:
        return [0]
    inner = slot_order(count // 2)
    return [2 * slot + 1 for slot in inner] + [2 * slot for slot in inner]


def reversed_bits(value, bits):
    return sum(((value >> bit) & 1) << (bits - 1 - bit) for bit in range(bits))


def lasting(microseconds):
    return pl.CostEstimate(flops=int(microseconds * 1.15e+09), transcendentals=0, bytes_accessed=0)


def far(value):
    return pltpu.with_memory_space_constraint(value, pltpu.HBM)


def whole(shape):
    return pl.BlockSpec(shape, lambda *_: (0,) * len(shape), pipeline_mode=pl.Buffered(1))


def kernel_params(megabytes):
    return pltpu.CompilerParams(vmem_limit_bytes=megabytes << 20)


def on_device(
    ctx_size,
    dp_size,
    tokens,
    segment_ids,
    w_qkv,
    w_out,
    w_up,
    w_down,
    norm_gain,
    norm_bias,
    grad_out,
):
    seqs, span, width = tokens.shape
    half = span // 2
    local_width = w_out.shape[0]
    heads = local_width // HEAD_DIM
    units_local = w_up.shape[0]
    rows = seqs * half
    long_half = half + STAT_ROWS
    ctx_bits = ctx_size.bit_length() - 1
    turn = lax.axis_index("tensor")
    place = lax.axis_index("ctx")
    row_place = lax.axis_index("dp")
    turn_array = turn.reshape(1)

    def room(megabytes):
        return kernel_params(megabytes if ctx_size <= 4 else 60)

    def swap(value):
        return lax.ppermute(value, "tensor", [(0, 1), (1, 0)])

    def hop(value, stage):
        moves = []
        for spot in range(ctx_size):
            for core in range(2):
                bit = stage if core == 0 else ctx_bits - 1 - stage
                moves.append((spot * 2 + core, (spot ^ (1 << bit)) * 2 + core))
        return lax.ppermute(value, ("ctx", "tensor"), moves)

    def tie(*values):
        return lax.optimization_barrier(values)

    def gather_near(own):
        own = own[:, None]
        return [hop(own, stage) for stage in range(min(ctx_bits, 2))]

    def gather_far(own, near_groups):
        groups = list(near_groups)
        if ctx_bits >= 2:
            groups.append(hop(groups[0], 1))
        for stage in range(2, ctx_bits):
            groups.append(hop(jnp.concatenate([own[:, None]] + groups, axis=1), stage))
        return groups

    def half_of(value, which):
        return lax.dynamic_slice_in_dim(value, which * half, half, 1)

    def with_ids(which):
        ids = half_of(segment_ids, which).astype(low)
        row = jnp.pad(ids[:, None, :], ((0, 0), (0, STAT_ROWS - 1), (0, width - half)))
        return jnp.concatenate([half_of(tokens, which), row], axis=1)

    def units_of(groups):
        direct, swapped = groups[: len(groups) // 2], groups[len(groups) // 2 :]
        if ctx_size == 4:
            return [(direct[0], swapped[1]), (direct[1], swapped[0]), (direct[2], swapped[2])]
        mirror = [reversed_bits(slot, ctx_bits) - 1 for slot in range(1, ctx_size)]
        first, second = jnp.concatenate(direct, axis=1), jnp.concatenate(swapped, axis=1)
        return [(first, jnp.stack([second[:, slot] for slot in mirror], axis=1))]

    block_width = 3 * local_width + LANES
    part_spec = pl.BlockSpec((1, 1, long_half, width), lambda g, s: (s, g, 0, 0))

    def project(part_a, part_b):
        count = part_a.shape[1]
        return pl.pallas_call(
            project_kernel,
            grid=(count, seqs),
            in_specs=[whole(w_qkv.shape), part_spec, part_spec],
            out_specs=pl.BlockSpec((1, 1, span, block_width), lambda g, s: (s, g, 0, 0)),
            out_shape=jax.ShapeDtypeStruct((seqs, count, span, block_width), low),
            compiler_params=room(16),
            cost_estimate=lasting(2),
            name="project",
        )(w_qkv, part_a, part_b)

    tok_a, tok_b = with_ids(turn), with_ids(1 - turn)
    tok_near = gather_near(tok_a)
    w_out_oth, w_up_oth, w_down_oth = swap(w_out), swap(w_up), swap(w_down)
    own = project(tok_a[:, None], tok_b[:, None])

    def seq_spec(shape):
        return pl.BlockSpec((1,) + shape, lambda s, *_: (s,) + (0,) * len(shape))

    def unit_specs(chosen):
        return [
            pl.BlockSpec(
                (1,) + value.shape[1:],
                lambda s, *_: (s, 0, 0, 0),
                pipeline_mode=pl.Buffered(2 if value.shape[1] == 1 else 1),
            )
            for value in chosen
        ]

    head_square = pltpu.VMEM((heads, span, span), full)
    head_square_low = pltpu.VMEM((heads, span, span), low)
    q_scratch = pltpu.VMEM((heads, span, 2 * LANES), low)
    head_rows = pltpu.VMEM((heads, span, LANES), low)

    def attend(chosen, state, finish):
        begin = state is None
        state_shapes = [((local_width, span), full), ((16, span), full)]
        shapes = (
            [((half, local_width), low), ((long_half, local_width), low), ((8, span), full)]
            if finish
            else state_shapes
        )
        state = [] if begin else list(state)
        return pl.pallas_call(
            functools.partial(attend_kernel, [value.shape[1] for value in chosen], heads, begin, finish),
            grid=(seqs,),
            in_specs=unit_specs([own] + chosen) + [seq_spec(value.shape[1:]) for value in state],
            out_specs=[seq_spec(shape) for shape, _ in shapes],
            out_shape=[
                (pltpu.HBM if finish else jax.ShapeDtypeStruct)((seqs,) + shape, kind) for shape, kind in shapes
            ],
            scratch_shapes=[
                q_scratch,
                head_square,
                head_square_low,
                pltpu.VMEM((16, span), full),
                pltpu.VMEM((local_width, span), full),
            ],
            compiler_params=room(14),
            cost_estimate=lasting(3),
            name="attend",
        )(own, *chosen, *state)

    state = attend([], None, False)
    *tok_near, first_state = tie(*tok_near, state[0])
    state = (first_state, state[1])
    tok_groups = gather_far(tok_a, tok_near)
    if ctx_size == 4:
        swapped = [swap(group) for group in tok_groups[:2]]
        near_units = [project(tok_groups[0], swapped[1]), project(tok_groups[1], swapped[0])]
        state = attend(near_units, state, False)
        last, first_state = tie(tok_groups[2], state[0])
        far_units = [project(last, swap(last))]
        units = near_units + far_units
        mixed_keep, mixed_send, lse = attend(far_units, (first_state, state[1]), True)
    else:
        units = [project(*pair) for pair in units_of(tok_groups + [swap(group) for group in tok_groups])]
        mixed_keep, mixed_send, lse = attend(units, state, True)
    mixed_recv = swap(mixed_send)

    middle_in = [
        tok_a,
        mixed_keep,
        mixed_recv,
        lse,
        w_out,
        w_out_oth,
        w_up,
        w_up_oth,
        w_down,
        w_down_oth,
        norm_gain,
        norm_bias,
    ]
    middle_shapes = [
        ((seqs, half, width), low),
        ((seqs, half, width), full),
        ((seqs, long_half, width), low),
        ((rows, units_local), low),
        ((rows, units_local), low),
        ((rows, units_local), low),
        ((rows, units_local), low),
        ((rows, width), low),
        ((rows, width), low),
        ((8, width), full),
    ]
    (
        out_half,
        d_resid,
        payload,
        active_own,
        active_oth,
        d_up_own,
        d_up_oth,
        d_ffn,
        normed_low,
        small,
    ) = pl.pallas_call(
        functools.partial(middle_kernel, min(512, units_local)),
        grid_spec=pltpu.PrefetchScalarGridSpec(
            num_scalar_prefetch=1,
            grid=(1,),
            in_specs=[whole(value.shape) for value in middle_in]
            + [pl.BlockSpec((seqs, half, width), lambda s, turn_ref: (0, turn_ref[0], 0))],
            out_specs=[whole(shape) for shape, _ in middle_shapes],
            scratch_shapes=[pltpu.VMEM((rows, 2 * units_local), full)],
        ),
        out_shape=[
            (jax.ShapeDtypeStruct if number == 2 else pltpu.HBM)(shape, kind)
            for number, (shape, kind) in enumerate(middle_shapes)
        ],
        compiler_params=room(36),
        cost_estimate=lasting(16),
        name="middle",
    )(turn_array, *middle_in, grad_out)

    order = slot_order(ctx_size)
    mirrored = [reversed_bits(slot, ctx_bits) for slot in order]
    owners = place ^ jnp.where(turn == 0, jnp.array(order, jnp.int32), jnp.array(mirrored, jnp.int32))
    quarter = width // ctx_size
    stages = [ctx_size >> (stage + 1) for stage in range(ctx_bits)] + [1]
    turned_kind = low if quarter % 16 == 0 else full
    chunk = min(512, units_local)

    def slot_scratch(count):
        return [pltpu.VMEM((width, count), turned_kind), pltpu.VMEM((ctx_size * padded(quarter), count), low)]

    def pair_grad(left_a, left_b, right_a, right_b, name):
        right_spec = pl.BlockSpec((rows, chunk), lambda n, *_: (0, n))
        return pl.pallas_call(
            pair_grad_kernel,
            grid_spec=pltpu.PrefetchScalarGridSpec(
                num_scalar_prefetch=1,
                grid=(units_local // chunk,),
                in_specs=[whole(left_a.shape), whole(left_b.shape), right_spec, right_spec],
                out_specs=[pl.BlockSpec((count, quarter, chunk), lambda n, *_: (0, 0, n)) for count in stages],
                scratch_shapes=slot_scratch(2 * rows),
            ),
            out_shape=[pltpu.HBM((count, quarter, units_local), low) for count in stages],
            compiler_params=room(16),
            cost_estimate=lasting(5.5),
            name=name,
        )(owners, *map(far, (left_a, left_b, right_a, right_b)))

    parity = row_place & 1

    def add_up(values):
        return sum(value.astype(full) for value in values)

    def send_stage(parts, gots, stage):
        count, start = parts[stage].shape[0], 0
        values = [parts[stage]]
        for got in gots:
            start = got.shape[0] - sum(part.shape[0] for part in parts[stage:])
            values.append(got[start : start + count])
        return add_up(values).astype(low)

    def own_half(parts, gots, which):
        values = [parts[-1]] + gots
        split = parts[-1].shape[1] // 2
        return add_up(
            [
                lax.dynamic_slice(value, (value.shape[0] - 1, which * split, 0), (1, split, value.shape[2]))
                for value in values
            ]
        )[0]

    class Blocks:
        def __init__(self, parts):
            self.parts, self.gots, self.stage, self.sent = list(parts), [], 0, None
            self.dp_stage, self.got = 0, None

        @property
        def arrived(self):
            return self.gots[-1] if self.dp_stage == 0 else self.got

        @arrived.setter
        def arrived(self, value):
            if self.dp_stage == 0:
                self.gots[-1] = value
            else:
                self.got = value

        def ready(self):
            if self.stage < ctx_bits:
                self.sent = send_stage(self.parts, self.gots, self.stage) if self.stage else self.parts[0]
            elif self.dp_stage == 0:
                self.sent = own_half(self.parts, self.gots, 1 - parity).astype(low)
            else:
                mine = own_half(self.parts, self.gots, parity) if self.dp_stage == 1 else self.sent.astype(full)
                self.sent = (mine + self.got.astype(full)).astype(low)

        def send(self):
            if self.stage < ctx_bits:
                self.gots.append(hop(self.sent, self.stage))
                self.stage += 1
                return
            last = self.dp_stage == dp_size.bit_length() - 1
            bit = 0 if last else self.dp_stage
            moves = [(spot, spot ^ (1 << bit)) for spot in range(dp_size)]
            self.got = lax.ppermute(self.sent, "dp", moves)
            self.dp_stage += 1

        def advance(self, *after):
            if self.gots:
                self.arrived = tie(self.arrived, *after)[0]
            elif after:
                self.parts[0] = tie(self.parts[0], *after)[0]
            self.ready()
            self.send()
            return self.sent

        def total(self):
            while self.dp_stage < dp_size.bit_length():
                self.advance()
            mine, other = self.sent, self.got
            return jnp.where(
                parity == 0, jnp.concatenate([mine, other], axis=0), jnp.concatenate([other, mine], axis=0)
            ).astype(full)

    grad_near = gather_near(payload)
    payload_b = swap(payload)
    d_ffn_b, active_b = swap(d_ffn), swap(active_oth)
    normed_b, d_up_b = swap(normed_low), swap(d_up_oth)
    down = Blocks(pair_grad(d_ffn, d_ffn_b, active_own, active_b, "grad_down"))
    latest = down.advance()
    normed_low, latest = tie(normed_low, latest)
    up = Blocks(pair_grad(normed_low, normed_b, d_up_own, d_up_b, "grad_up"))
    *grad_near, up.parts[0] = tie(*grad_near, up.parts[0])
    latest = up.advance()
    own_back, latest = tie(own, latest)
    grad_far = gather_far(payload, grad_near)
    crossed = [swap(group) for group in grad_far[:-1]]

    sum_shape = pltpu.HBM((seqs, span, local_width), full)
    row_shape = pltpu.HBM((seqs, span, local_width), low)
    grad_spec = seq_spec((long_half, width))
    span_spec = seq_spec((span, local_width))
    counts = [value.shape[1] for value in units]
    d_query, dk_sum, dv_sum = pl.pallas_call(
        functools.partial(query_grad_kernel, counts, heads),
        grid=(seqs,),
        in_specs=unit_specs([own]) + [grad_spec, grad_spec, whole(w_out.shape)] + unit_specs(units),
        out_specs=[span_spec] * 3,
        out_shape=[row_shape, sum_shape, sum_shape],
        scratch_shapes=[
            q_scratch,
            head_rows,
            pltpu.VMEM((16, span), full),
            head_square,
            head_square_low,
            head_square_low,
            pltpu.VMEM((local_width, span), full),
        ],
        compiler_params=room(20),
        cost_estimate=lasting(11),
        name="query_grad",
    )(own_back, payload, payload_b, far(w_out), *units)

    def sequence_grad(kernel, values, lefts, extra, columns, name):
        return Blocks(
            pl.pallas_call(
                kernel,
                grid_spec=pltpu.PrefetchScalarGridSpec(
                    num_scalar_prefetch=1,
                    grid=(1,),
                    in_specs=[whole(value.shape) for value in values],
                    out_specs=[whole((count, extra + quarter, columns)) for count in stages],
                    scratch_shapes=slot_scratch(seqs * span) * lefts,
                ),
                out_shape=[pltpu.HBM((count, extra + quarter, columns), low) for count in stages],
                compiler_params=room(20),
                cost_estimate=lasting(5.5),
                name=name,
            )(owners, *map(far, values))
        )

    small_rows = (small[:4] + swap(small)[:4]).reshape(4, ctx_size, quarter).transpose(1, 0, 2)
    small_rows = jnp.pad(small_rows, ((0, 0), (0, SMALL_ROWS - 4), (0, local_width - quarter)))
    latest = down.advance(d_query)
    d_query, latest = tie(d_query, latest)
    query_out = sequence_grad(
        query_out_grad_kernel,
        (tok_a, tok_b, d_query, payload, payload_b, mixed_keep, mixed_send, small_rows),
        2,
        SMALL_ROWS,
        2 * local_width,
        "query_out_grad",
    )
    grad_far[-1], query_out.parts[1] = tie(grad_far[-1], query_out.parts[1])
    crossed.append(swap(grad_far[-1]))
    latest = query_out.advance()
    latest = down.advance(latest)
    d_query, latest = tie(d_query, latest)
    grad_units = units_of(grad_far + crossed)
    grad_a, grad_b = [pair[0] for pair in grad_units], [pair[1] for pair in grad_units]
    d_kv, d_input = pl.pallas_call(
        functools.partial(key_grad_kernel, counts, heads),
        grid_spec=pltpu.PrefetchScalarGridSpec(
            num_scalar_prefetch=1,
            grid=(seqs,),
            in_specs=unit_specs([own])
            + [span_spec] * 3
            + [whole(w_out.shape), whole(w_qkv.shape)]
            + unit_specs(units + grad_a + grad_b),
            out_specs=[seq_spec((span, 2 * local_width)), seq_spec((span, width))],
            scratch_shapes=[
                pltpu.VMEM((heads // 2, span, 2 * LANES), low),
                head_rows,
                head_rows,
                head_square,
                head_square_low,
                head_square_low,
                pltpu.VMEM((span, local_width), full),
                pltpu.VMEM((span, local_width), full),
            ],
        ),
        out_shape=[
            jax.ShapeDtypeStruct((seqs, span, 2 * local_width), low),
            jax.ShapeDtypeStruct((seqs, span, width), low),
        ],
        compiler_params=room(26),
        cost_estimate=lasting(12.5),
        name="key_grad",
    )(turn_array, own, *map(far, (d_query, dk_sum, dv_sum, w_out, w_qkv, *units, *grad_a, *grad_b)))

    latest = up.advance(d_kv)
    latest = down.advance(latest)
    latest = query_out.advance(latest)
    d_kv, latest = tie(d_kv, latest)
    key_value = sequence_grad(key_value_grad_kernel, (tok_a, tok_b, d_kv), 1, 0, 2 * local_width, "key_value_grad")
    latest = key_value.advance()
    out_half, d_resid, d_input, latest = tie(out_half, d_resid, d_input, latest)
    swapped = [swap(out_half), swap(d_resid), swap(d_input)]
    for blocks in (up, down, key_value, query_out):
        latest = blocks.advance(latest)

    def both_halves(mine, other):
        return jnp.where(
            turn == 0, jnp.concatenate([mine, other], axis=1), jnp.concatenate([other, mine], axis=1)
        )

    *swapped, latest = tie(*swapped, latest)
    outputs = both_halves(out_half, swapped[0])
    grad_tokens = d_input.astype(full) + swapped[2].astype(full) + both_halves(d_resid, swapped[1])
    outputs, grad_tokens, latest = tie(outputs, grad_tokens, latest)
    for blocks in (up, key_value, query_out, up, key_value, query_out, key_value):
        latest = blocks.advance(latest)
    down_total, up_total = down.total(), up.total()
    query_out_total, key_value_total = query_out.total(), key_value.total()
    small_total = query_out_total[:4, local_width : local_width + quarter]
    query_out_total = query_out_total[SMALL_ROWS:]
    return (
        outputs,
        grad_tokens,
        jnp.stack(
            [query_out_total[:, :local_width], key_value_total[:, :local_width], key_value_total[:, local_width:]]
        ),
        query_out_total[:, local_width:].T,
        up_total.T,
        down_total.T,
        small_total[0:2],
        small_total[2:4],
    )


def solution(mesh):
    return jax.shard_map(
        functools.partial(on_device, mesh.shape["ctx"], mesh.shape["dp"]),
        mesh=mesh,
        in_specs=(
            P("dp", "ctx", None),
            P("dp", "ctx"),
            P(None, None, "tensor"),
            P("tensor", None),
            P("tensor", None),
            P("tensor", None),
            P(),
            P(),
            P("dp", "ctx", None),
        ),
        out_specs=(
            P("dp", "ctx", None),
            P("dp", "ctx", None),
            P(None, "ctx", "tensor"),
            P("tensor", "ctx"),
            P("tensor", "ctx"),
            P("tensor", "ctx"),
            P(None, "ctx"),
            P(None, "ctx"),
        ),
        check_vma=False,
    )
```

```python
import functools
import jax
import jax.numpy as jnp
from jax import lax
from jax.experimental import pallas as pl
from jax.experimental.pallas import tpu as pltpu
from jax.sharding import PartitionSpec as P

HEAD_DIM = 64
LANES = 128
STAT_ROWS = 8
SMALL_ROWS = 16
BIG = 2.0**30
low, full = jnp.bfloat16, jnp.float32


def dot_nn(left, right):
    return lax.dot_general(left, right, (((1,), (0,)), ((), ())), preferred_element_type=full)


def dot_nt(left, right):
    return lax.dot_general(left, right, (((1,), (1,)), ((), ())), preferred_element_type=full)


def dot_tn(left, right):
    return lax.dot_general(left, right, (((0,), (0,)), ((), ())), preferred_element_type=full)


def two_parts(values):
    high = values.astype(low)
    return high, (values - high.astype(full)).astype(low)


def project_kernel(w_qkv, part_a, part_b, out):
    half = part_a.shape[2] - STAT_ROWS
    local = w_qkv.shape[2]
    rows = jnp.concatenate([part[0, 0, :half, :] for part in (part_a, part_b)], axis=0)
    for kind in range(3):
        product = dot_nn(rows, w_qkv[kind])
        if kind == 0:
            product = product * 0.125
        out[0, 0, :, kind * local : (kind + 1) * local] = product.astype(low)
    ids = lax.broadcasted_iota(jnp.int32, (LANES, half), 0).astype(full)
    for which, part in enumerate((part_a, part_b)):
        row = part[0, 0, half : half + 1, :half].astype(full)
        out[0, 0, which * half : (which + 1) * half, 3 * local :] = jnp.where(ids == row, 1.0, 0.0).T.astype(low)


class Lanes:
    def __init__(self, heads):
        self.local = heads * HEAD_DIM

    def of(self, kind, pair):
        start = kind * self.local + pair * LANES
        return slice(start, start + LANES)

    @property
    def hot(self):
        return slice(3 * self.local, 3 * self.local + LANES)


def split_heads(value):
    left = lax.broadcasted_iota(jnp.int32, value.shape, 1) < HEAD_DIM
    zero = jnp.zeros_like(value)
    return jnp.where(left, value, zero), jnp.where(left, zero, value)


def present(hot):
    return jnp.max(hot.astype(full), axis=0, keepdims=True)


def over_units(counts, unit_refs, lanes, own_ids, body):
    flags = [
        jnp.max(own_ids * present(ref[0, 0, :, lanes.hot])) > 0.0 if count == 1 else None
        for count, ref in zip(counts, unit_refs)
    ]
    for number, (count, ref) in enumerate(zip(counts, unit_refs)):
        if count == 1:
            pl.when(flags[number])(functools.partial(body, number, 0))
        else:

            def step(index, carry, number=number, ref=ref):
                shared = jnp.max(own_ids * present(ref[0, index, :, lanes.hot])) > 0.0
                pl.when(shared)(functools.partial(body, number, index))
                return carry

            lax.fori_loop(0, count, step, 0)


def attend_kernel(counts, heads, begin, finish, *refs):
    lanes, pairs, units = Lanes(heads), heads // 2, len(counts)
    own, unit_refs = refs[0], refs[1 : 1 + units]
    refs = refs[1 + units :]
    if not begin:
        acc_in, stat_in = refs[:2]
        refs = refs[2:]
    if finish:
        mixed_keep, mixed_send, lse_out = refs[:3]
        refs = refs[3:]
    else:
        acc_out, stat_out = refs[:2]
        refs = refs[2:]
    q_aug, scores, weights, stat, acc = refs
    span = own.shape[2]
    half = span // 2
    hot_own = own[0, 0, :, lanes.hot]
    penalty = ((hot_own.astype(full) - 1.0) * BIG).astype(low)
    for pair in range(pairs):
        for side, masked in enumerate(split_heads(own[0, 0, :, lanes.of(0, pair)])):
            q_aug[2 * pair + side] = jnp.concatenate([masked, penalty], axis=1)
    if not begin:
        acc[...] = acc_in[0]
        stat[...] = stat_in[0]

    def block(ref, index, first):
        hot = ref[0, index, :, lanes.hot]
        peaks = []
        for pair in range(pairs):
            k_aug = jnp.concatenate([ref[0, index, :, lanes.of(1, pair)], hot], axis=1)
            for side in range(2):
                head = 2 * pair + side
                product = dot_nt(k_aug, q_aug[head])
                scores[head] = product
                peak = jnp.max(product, axis=0, keepdims=True)
                peaks.append(peak if first else jnp.maximum(peak, stat[head : head + 1, :]))
        sums = []
        for head in range(heads):
            weight = jnp.exp(scores[head] - peaks[head])
            sums.append(jnp.sum(weight, axis=0, keepdims=True))
            weights[head] = weight.astype(low)
        for pair in range(pairs):
            turned = ref[0, index, :, lanes.of(2, pair)].T
            for side in range(2):
                head = 2 * pair + side
                rows = slice(head * HEAD_DIM, (head + 1) * HEAD_DIM)
                mix = dot_nn(turned[side * HEAD_DIM : (side + 1) * HEAD_DIM], weights[head])
                total = sums[head]
                if not first:
                    shrink = jnp.exp(stat[head : head + 1, :] - peaks[head])
                    total = total + stat[8 + head : 9 + head, :] * shrink
                    mix = mix + acc[rows, :] * shrink
                acc[rows, :] = mix
                stat[head : head + 1, :] = peaks[head]
                stat[8 + head : 9 + head, :] = total

    if begin:
        block(own, 0, True)
    over_units(
        counts, unit_refs, lanes, present(hot_own), lambda number, index: block(unit_refs[number], index, False)
    )
    if not finish:
        acc_out[0] = acc[...]
        stat_out[0] = stat[...]
        return
    totals = stat[8 : 8 + heads, :]
    lse = stat[0:heads, :] + jnp.log(totals)
    lse_out[0, 0:heads, :] = lse
    lse_out[0, heads:8, :] = jnp.zeros((8 - heads, span), full)
    scale = 1.0 / totals
    for pair in range(pairs):
        chosen = slice(pair * LANES, (pair + 1) * LANES)
        mixed = jnp.concatenate(
            [
                acc[head * HEAD_DIM : (head + 1) * HEAD_DIM, :] * scale[head : head + 1, :]
                for head in (2 * pair, 2 * pair + 1)
            ],
            axis=0,
        ).T.astype(low)
        mixed_keep[0, :, chosen] = mixed[:half]
        mixed_send[0, :half, chosen] = mixed[half:]
    row_of = lax.broadcasted_iota(jnp.int32, (STAT_ROWS, half), 0)
    for column in range(pairs):
        tile = jnp.zeros((STAT_ROWS, half), full)
        for which in range(2):
            row = lse[which * pairs + column : which * pairs + column + 1, half:]
            for kind, part in enumerate(two_parts(row)):
                tile = jnp.where(row_of == kind + 2 * which, part.astype(full), tile)
        mixed_send[0, half:, column * LANES : (column + 1) * LANES] = tile.astype(low)


def stat_row(grad_a, grad_b, at, kind, head, half):
    tile = slice(head * LANES, (head + 1) * LANES)
    parts = []
    for other, ref in enumerate((grad_a, grad_b)):
        row = half + 2 * kind + 4 * other
        parts.append(
            ref[at + (slice(row, row + 1), tile)].astype(full)
            + ref[at + (slice(row + 1, row + 2), tile)].astype(full)
        )
    return jnp.concatenate(parts, axis=1)


def query_grad_kernel(counts, heads, *refs):
    lanes, pairs, units = Lanes(heads), heads // 2, len(counts)
    own, grad_a, grad_b, w_out = refs[:4]
    unit_refs = refs[4 : 4 + units]
    dq_out, dk_out, dv_out, q_aug, d_mix, rows_of, scores, weights, d_scores, acc = refs[4 + units :]
    span = own.shape[2]
    half = span // 2
    hot_own = own[0, 0, :, lanes.hot]
    penalty = ((hot_own.astype(full) - 1.0) * BIG).astype(low)
    d_attn = jnp.concatenate([grad_a[0, :half, :], grad_b[0, :half, :]], axis=0)
    d_mixed = dot_nt(d_attn, w_out[...]).astype(low)
    for pair in range(pairs):
        q_parts = split_heads(own[0, 0, :, lanes.of(0, pair)])
        d_parts = split_heads(d_mixed[:, pair * LANES : (pair + 1) * LANES])
        for side in range(2):
            head = 2 * pair + side
            q_aug[head] = jnp.concatenate([q_parts[side], penalty], axis=1)
            d_mix[head] = d_parts[side]
            rows_of[head : head + 1, :] = stat_row(grad_a, grad_b, (0,), 0, head, half)
            rows_of[8 + head : 9 + head, :] = stat_row(grad_a, grad_b, (0,), 1, head, half)

    def block(ref, index, first):
        hot = ref[0, index, :, lanes.hot]
        for pair in range(pairs):
            k_aug = jnp.concatenate([ref[0, index, :, lanes.of(1, pair)], hot], axis=1)
            for side in range(2):
                head = 2 * pair + side
                scores[head] = dot_nt(k_aug, q_aug[head])
        for pair in range(pairs):
            values = ref[0, index, :, lanes.of(2, pair)]
            for side in range(2):
                head = 2 * pair + side
                weight = jnp.exp(scores[head] - rows_of[head : head + 1, :])
                d_weight = dot_nt(values, d_mix[head])
                d_scores[head] = (weight * (d_weight - rows_of[8 + head : 9 + head, :])).astype(low)
                if first:
                    weights[head] = weight.astype(low)
        for pair in range(pairs):
            turned = ref[0, index, :, lanes.of(1, pair)].T
            for side in range(2):
                head = 2 * pair + side
                rows = slice(head * HEAD_DIM, (head + 1) * HEAD_DIM)
                product = dot_nn(turned[side * HEAD_DIM : (side + 1) * HEAD_DIM], d_scores[head])
                acc[rows, :] = product if first else acc[rows, :] + product
            if first:
                chosen = slice(pair * LANES, (pair + 1) * LANES)
                one, two = 2 * pair, 2 * pair + 1
                dv_out[0, :, chosen] = dot_nn(weights[one], d_mix[one]) + dot_nn(weights[two], d_mix[two])
                dk_out[0, :, chosen] = dot_nn(d_scores[one], q_aug[one, :, :LANES]) + dot_nn(
                    d_scores[two], q_aug[two, :, :LANES]
                )

    block(own, 0, True)
    over_units(
        counts, unit_refs, lanes, present(hot_own), lambda number, index: block(unit_refs[number], index, False)
    )
    for pair in range(pairs):
        chosen = slice(pair * LANES, (pair + 1) * LANES)
        dq_out[0, :, chosen] = (acc[chosen, :] * 0.125).T.astype(low)


def key_grad_kernel(counts, heads, turn_ref, *refs):
    lanes, pairs, units = Lanes(heads), heads // 2, len(counts)
    own, dq_in, dk_in, dv_in, w_out, w_qkv = refs[:6]
    unit_refs = refs[6 : 6 + units]
    a_refs = refs[6 + units : 6 + 2 * units]
    b_refs = refs[6 + 2 * units : 6 + 3 * units]
    d_kv, d_input, k_aug, q_mask, d_mix, scores, weights, d_scores, dk_acc, dv_acc = refs[6 + 3 * units :]
    span = own.shape[2]
    half = span // 2
    local = lanes.local
    turn = turn_ref[0]
    hot_own = own[0, 0, :, lanes.hot]
    for pair in range(pairs):
        k_aug[pair] = jnp.concatenate([own[0, 0, :, lanes.of(1, pair)], hot_own], axis=1)
    dk_acc[...] = dk_in[0]
    dv_acc[...] = dv_in[0]

    def block(number, index):
        ref, grad_a, grad_b = unit_refs[number], a_refs[number], b_refs[number]
        penalty = ((ref[0, index, :, lanes.hot].astype(full) - 1.0) * BIG).astype(low)
        d_attn = jnp.concatenate([grad_a[0, index, :half, :], grad_b[0, index, :half, :]], axis=0)
        d_mixed = dot_nt(d_attn, w_out[...]).astype(low)
        for pair in range(pairs):
            q_parts = split_heads(ref[0, index, :, lanes.of(0, pair)])
            d_parts = split_heads(d_mixed[:, pair * LANES : (pair + 1) * LANES])
            for side in range(2):
                head = 2 * pair + side
                q_mask[head] = q_parts[side]
                d_mix[head] = d_parts[side]
                scores[head] = dot_nt(k_aug[pair], jnp.concatenate([q_parts[side], penalty], axis=1))
        for pair in range(pairs):
            values = own[0, 0, :, lanes.of(2, pair)]
            for side in range(2):
                head = 2 * pair + side
                lse = stat_row(grad_a, grad_b, (0, index), 0, head, half)
                delta = stat_row(grad_a, grad_b, (0, index), 1, head, half)
                weight = jnp.exp(scores[head] - lse)
                d_weight = dot_nt(values, d_mix[head])
                d_scores[head] = (weight * (d_weight - delta)).astype(low)
                weights[head] = weight.astype(low)
        for pair in range(pairs):
            chosen = slice(pair * LANES, (pair + 1) * LANES)
            one, two = 2 * pair, 2 * pair + 1
            dv_acc[:, chosen] += dot_nn(weights[one], d_mix[one]) + dot_nn(weights[two], d_mix[two])
            dk_acc[:, chosen] += dot_nn(d_scores[one], q_mask[one]) + dot_nn(d_scores[two], q_mask[two])

    over_units(counts, unit_refs, lanes, present(hot_own), block)
    half_a = pl.ds(pl.multiple_of(turn * half, half), half)
    half_b = pl.ds(pl.multiple_of((1 - turn) * half, half), half)
    for kind, value in enumerate((dq_in[0], dk_acc[...].astype(low), dv_acc[...].astype(low))):
        chosen = slice(kind * local, (kind + 1) * local)
        product = dot_nt(value, w_qkv[kind])
        total = product if kind == 0 else total + product
        if kind > 0:
            d_kv[0, :, (kind - 1) * local : kind * local] = value
    total = total.astype(low)
    d_input[0, half_a, :] = total[:half]
    d_input[0, half_b, :] = total[half:]


def padded(block):
    return -(-block // 16) * 16


def lane_part(ref, half=None):
    if half is None:
        return lambda lanes: ref[:, lanes]
    return lambda lanes: ref[:, :half, lanes].reshape(ref.shape[0] * half, LANES)


def put_slots(turned, slots, values, owners, block):
    def turn_lanes(step, carry):
        lanes = pl.ds(pl.multiple_of(step * LANES, LANES), LANES)
        start = 0
        for load in values:
            value = load(lanes)
            turned[lanes, start : start + value.shape[0]] = value.astype(turned.dtype).T
            start += value.shape[0]
        return carry

    lax.fori_loop(0, turned.shape[0] // LANES, turn_lanes, 0)
    room = padded(block)
    for slot in range(slots.shape[0] // room):
        source = pl.ds(pl.multiple_of(owners[slot] * block, 16 if block % 16 == 0 else 8), block)
        slots[slot * room : slot * room + block, :] = turned[source, :].astype(low)


def places_of(targets):
    return [(ref, index) for ref in targets for index in range(ref.shape[0])]


def put_blocks(product, targets, block, skip):
    for slot, (ref, index) in enumerate(places_of(targets)):
        start = slot * padded(block)
        ref[index, skip : skip + block, :] = product[start : start + block].astype(low)


def pair_grad_kernel(owners, left_a, left_b, right_a, right_b, *refs):
    targets, (turned, slots) = refs[:-2], refs[-2:]
    block = targets[0].shape[1]

    @pl.when(pl.program_id(0) == 0)
    def _():
        put_slots(turned, slots, [lane_part(part) for part in (left_a, left_b)], owners, block)

    right = jnp.concatenate([right_a[...], right_b[...]], axis=0)
    put_blocks(dot_nn(slots[...], right), targets, block, 0)


def half_rows(part, half):
    return part[:, :half, :].reshape(part.shape[0] * half, -1)


def both_rows(value, half):
    return jnp.concatenate([half_rows(value[:, :half], half), half_rows(value[:, half:], half)], axis=0)


def query_out_grad_kernel(owners, tok_a, tok_b, d_query, d_attn_a, d_attn_b, mixed_a, mixed_b, small, *refs):
    targets, (turned, slots, turned_second, slots_second) = refs[:-4], refs[-4:]
    span, local = d_query.shape[1:]
    half = span // 2
    block = targets[0].shape[1] - SMALL_ROWS
    put_slots(turned, slots, [lane_part(part, half) for part in (tok_a, tok_b)], owners, block)
    first = dot_nn(slots[...], both_rows(d_query, half)).astype(low)
    put_slots(turned_second, slots_second, [lane_part(part, half) for part in (d_attn_a, d_attn_b)], owners, block)
    mixed = jnp.concatenate([half_rows(part, half) for part in (mixed_a, mixed_b)], axis=0)
    second = dot_nn(slots_second[...], mixed).astype(low)
    for slot, (ref, index) in enumerate(places_of(targets)):
        start = slot * padded(block)
        for which, product in enumerate((first, second)):
            columns = slice(which * local, (which + 1) * local)
            ref[index, SMALL_ROWS:, columns] = product[start : start + block]
        ref[index, :SMALL_ROWS, :local] = jnp.zeros((SMALL_ROWS, local), low)
        ref[index, :SMALL_ROWS, local:] = small[owners[slot]].astype(low)


def key_value_grad_kernel(owners, tok_a, tok_b, d_kv, *refs):
    targets, (turned, slots) = refs[:-2], refs[-2:]
    half = d_kv.shape[1] // 2
    block = targets[0].shape[1]
    put_slots(turned, slots, [lane_part(part, half) for part in (tok_a, tok_b)], owners, block)
    put_blocks(dot_nn(slots[...], both_rows(d_kv, half)), targets, block, 0)


def norm_of(residual):
    center = residual - jnp.mean(residual, axis=-1, keepdims=True)
    inverse = lax.rsqrt(jnp.mean(center * center, axis=-1, keepdims=True) + 1e-06)
    return center * inverse, inverse


def norm_back(d_normal, normal, inverse):
    return inverse * (
        d_normal
        - jnp.mean(d_normal, axis=-1, keepdims=True)
        - normal * jnp.mean(d_normal * normal, axis=-1, keepdims=True)
    )


def middle_kernel(
    chunk,
    turn_ref,
    tok,
    mixed_keep,
    mixed_recv,
    lse_keep,
    w_out_own,
    w_out_oth,
    w_up_own,
    w_up_oth,
    w_down_own,
    w_down_oth,
    gain,
    shift,
    grad_out,
    out,
    d_resid,
    payload,
    active_own,
    active_oth,
    d_up_own,
    d_up_oth,
    d_ffn_out,
    normed_out,
    small,
    slope,
):
    seqs, half, width = out.shape
    rows = seqs * half
    heads = mixed_keep.shape[2] // HEAD_DIM
    keep = mixed_keep[...].reshape(rows, -1)
    recv = mixed_recv[:, :half, :].reshape(rows, -1)
    attn = dot_nn(keep, w_out_own[...]) + dot_nn(recv, w_out_oth[...])
    resid_one = tok[:, :half, :].reshape(rows, width).astype(full) + attn
    normal_one, inverse_one = norm_of(resid_one)
    gain_one, gain_two = gain[0:1, :], gain[1:2, :]
    normed = normal_one * gain_one + shift[0:1, :]
    normed_low = normed.astype(low)
    normed_out[...] = normed_low
    units = w_up_own.shape[0]
    sides = ((w_up_own, w_down_own, active_own, d_up_own), (w_up_oth, w_down_oth, active_oth, d_up_oth))
    ffn = jnp.zeros((rows, width), full)
    for which, (w_up, w_down, active_ref, _) in enumerate(sides):
        for start in range(0, units, chunk):
            part = slice(start, start + chunk)
            upward = dot_nt(normed_low, w_up[part, :])
            spread = 0.5 * (1.0 + lax.erf(upward * 0.7071067811865476))
            active = (upward * spread).astype(low)
            slope[:, which * units + start : which * units + start + chunk] = (
                spread + upward * (jnp.exp(upward * upward * -0.5) * 0.3989422804014327)
            )
            active_ref[:, part] = active
            ffn = ffn + dot_nn(active, w_down[part, :])
    normal_two, inverse_two = norm_of(normed + ffn)
    out[...] = (normal_two * gain_two + shift[1:2, :]).astype(low).reshape(seqs, half, width)
    grad = grad_out[...].reshape(rows, width).astype(full)
    small[1:2, :] = jnp.sum(grad * normal_two, axis=0, keepdims=True)
    small[3:4, :] = jnp.sum(grad, axis=0, keepdims=True)
    d_resid_two = norm_back(grad * gain_two, normal_two, inverse_two)
    d_ffn = d_resid_two.astype(low)
    d_ffn_out[...] = d_ffn
    d_normed = d_resid_two
    for which, (w_up, w_down, _, d_up_ref) in enumerate(sides):
        for start in range(0, units, chunk):
            part = slice(start, start + chunk)
            d_active = dot_nt(d_ffn, w_down[part, :])
            d_up = (d_active * slope[:, which * units + start : which * units + start + chunk]).astype(low)
            d_up_ref[:, part] = d_up
            d_normed = d_normed + dot_nn(d_up, w_up[part, :])
    small[0:1, :] = jnp.sum(d_normed * normal_one, axis=0, keepdims=True)
    small[2:3, :] = jnp.sum(d_normed, axis=0, keepdims=True)
    small[4:8, :] = jnp.zeros((4, width), full)
    d_resid_one = norm_back(d_normed * gain_one, normal_one, inverse_one)
    d_resid[...] = d_resid_one.reshape(seqs, half, width)
    d_attn = d_resid_one.astype(low)
    payload[:, :half, :] = d_attn.reshape(seqs, half, width)
    column_of = lax.broadcasted_iota(jnp.int32, (8, heads * HEAD_DIM), 1) // HEAD_DIM
    chosen = jnp.where(column_of == lax.broadcasted_iota(jnp.int32, (8, heads * HEAD_DIM), 0), 1.0, 0.0)
    deltas = []
    for mixed, w_out in ((keep, w_out_own), (recv, w_out_oth)):
        d_mixed = dot_nt(d_attn, w_out[...]).astype(low).astype(full)
        deltas.append(
            lax.dot_general(
                chosen,
                d_mixed * mixed.astype(full),
                (((1,), (1,)), ((), ())),
                precision=lax.Precision.HIGHEST,
                preferred_element_type=full,
            )
        )
    row_of = lax.broadcasted_iota(jnp.int32, (STAT_ROWS, half), 0)
    pairs = heads // 2
    for seq in range(seqs):
        for head in range(heads):
            lse_high, lse_low = two_parts(lse_keep[seq, head : head + 1, :half])
            tile = slice((head % pairs) * LANES, (head % pairs + 1) * LANES)
            row = half + 2 * (head // pairs)
            parts = [lse_high.astype(full), lse_low.astype(full)]
            for which in range(2):
                piece = deltas[which][head : head + 1, seq * half : (seq + 1) * half]
                if which == 1:
                    parts.append(mixed_recv[seq, row : row + 1, tile].astype(full))
                    parts.append(mixed_recv[seq, row + 1 : row + 2, tile].astype(full))
                parts.extend(part.astype(full) for part in two_parts(piece))
            stat = jnp.zeros((STAT_ROWS, half), full)
            for index, part in enumerate(parts):
                stat = jnp.where(row_of == index, part, stat)
            payload[seq, half:, head * LANES : (head + 1) * LANES] = stat.astype(low)


def slot_order(count):
    if count == 1:
        return [0]
    inner = slot_order(count // 2)
    return [2 * slot + 1 for slot in inner] + [2 * slot for slot in inner]


def reversed_bits(value, bits):
    return sum(((value >> bit) & 1) << (bits - 1 - bit) for bit in range(bits))


def lasting(microseconds):
    return pl.CostEstimate(flops=int(microseconds * 1.15e+09), transcendentals=0, bytes_accessed=0)


def far(value):
    return pltpu.with_memory_space_constraint(value, pltpu.HBM)


def whole(shape):
    return pl.BlockSpec(shape, lambda *_: (0,) * len(shape), pipeline_mode=pl.Buffered(1))


def kernel_params(megabytes):
    return pltpu.CompilerParams(vmem_limit_bytes=megabytes << 20)


def on_device(
    ctx_size,
    dp_size,
    tokens,
    segment_ids,
    w_qkv,
    w_out,
    w_up,
    w_down,
    norm_gain,
    norm_bias,
    grad_out,
):
    seqs, span, width = tokens.shape
    half = span // 2
    local_width = w_out.shape[0]
    heads = local_width // HEAD_DIM
    units_local = w_up.shape[0]
    rows = seqs * half
    long_half = half + STAT_ROWS
    ctx_bits = ctx_size.bit_length() - 1
    turn = lax.axis_index("tensor")
    place = lax.axis_index("ctx")
    row_place = lax.axis_index("dp")
    turn_array = turn.reshape(1)

    def room(megabytes):
        return kernel_params(megabytes if ctx_size <= 4 else 60)

    def swap(value):
        return lax.ppermute(value, "tensor", [(0, 1), (1, 0)])

    def hop(value, stage):
        moves = []
        for spot in range(ctx_size):
            for core in range(2):
                bit = stage if core == 0 else ctx_bits - 1 - stage
                moves.append((spot * 2 + core, (spot ^ (1 << bit)) * 2 + core))
        return lax.ppermute(value, ("ctx", "tensor"), moves)

    def tie(*values):
        return lax.optimization_barrier(values)

    def gather_near(own):
        own = own[:, None]
        return [hop(own, stage) for stage in range(min(ctx_bits, 2))]

    def gather_far(own, near_groups):
        groups = list(near_groups)
        if ctx_bits >= 2:
            groups.append(hop(groups[0], 1))
        for stage in range(2, ctx_bits):
            groups.append(hop(jnp.concatenate([own[:, None]] + groups, axis=1), stage))
        return groups

    def half_of(value, which):
        return lax.dynamic_slice_in_dim(value, which * half, half, 1)

    def with_ids(which):
        ids = half_of(segment_ids, which).astype(low)
        row = jnp.pad(ids[:, None, :], ((0, 0), (0, STAT_ROWS - 1), (0, width - half)))
        return jnp.concatenate([half_of(tokens, which), row], axis=1)

    def units_of(groups):
        direct, swapped = groups[: len(groups) // 2], groups[len(groups) // 2 :]
        if ctx_size == 4:
            return [(direct[0], swapped[1]), (direct[1], swapped[0]), (direct[2], swapped[2])]
        mirror = [reversed_bits(slot, ctx_bits) - 1 for slot in range(1, ctx_size)]
        first, second = jnp.concatenate(direct, axis=1), jnp.concatenate(swapped, axis=1)
        return [(first, jnp.stack([second[:, slot] for slot in mirror], axis=1))]

    block_width = 3 * local_width + LANES
    part_spec = pl.BlockSpec((1, 1, long_half, width), lambda g, s: (s, g, 0, 0))

    def project(part_a, part_b):
        count = part_a.shape[1]
        return pl.pallas_call(
            project_kernel,
            grid=(count, seqs),
            in_specs=[whole(w_qkv.shape), part_spec, part_spec],
            out_specs=pl.BlockSpec((1, 1, span, block_width), lambda g, s: (s, g, 0, 0)),
            out_shape=jax.ShapeDtypeStruct((seqs, count, span, block_width), low),
            compiler_params=room(16),
            cost_estimate=lasting(2),
            name="project",
        )(w_qkv, part_a, part_b)

    tok_a, tok_b = with_ids(turn), with_ids(1 - turn)
    tok_near = gather_near(tok_a)
    w_out_oth, w_up_oth, w_down_oth = swap(w_out), swap(w_up), swap(w_down)
    own = project(tok_a[:, None], tok_b[:, None])

    def seq_spec(shape):
        return pl.BlockSpec((1,) + shape, lambda s, *_: (s,) + (0,) * len(shape))

    def unit_specs(chosen):
        return [
            pl.BlockSpec(
                (1,) + value.shape[1:],
                lambda s, *_: (s, 0, 0, 0),
                pipeline_mode=pl.Buffered(2 if value.shape[1] == 1 else 1),
            )
            for value in chosen
        ]

    head_square = pltpu.VMEM((heads, span, span), full)
    head_square_low = pltpu.VMEM((heads, span, span), low)
    q_scratch = pltpu.VMEM((heads, span, 2 * LANES), low)
    head_rows = pltpu.VMEM((heads, span, LANES), low)

    def attend(chosen, state, finish):
        begin = state is None
        state_shapes = [((local_width, span), full), ((16, span), full)]
        shapes = (
            [((half, local_width), low), ((long_half, local_width), low), ((8, span), full)]
            if finish
            else state_shapes
        )
        state = [] if begin else list(state)
        return pl.pallas_call(
            functools.partial(attend_kernel, [value.shape[1] for value in chosen], heads, begin, finish),
            grid=(seqs,),
            in_specs=unit_specs([own] + chosen) + [seq_spec(value.shape[1:]) for value in state],
            out_specs=[seq_spec(shape) for shape, _ in shapes],
            out_shape=[
                (pltpu.HBM if finish else jax.ShapeDtypeStruct)((seqs,) + shape, kind) for shape, kind in shapes
            ],
            scratch_shapes=[
                q_scratch,
                head_square,
                head_square_low,
                pltpu.VMEM((16, span), full),
                pltpu.VMEM((local_width, span), full),
            ],
            compiler_params=room(14),
            cost_estimate=lasting(3),
            name="attend",
        )(own, *chosen, *state)

    state = attend([], None, False)
    *tok_near, first_state = tie(*tok_near, state[0])
    state = (first_state, state[1])
    tok_groups = gather_far(tok_a, tok_near)
    if ctx_size == 4:
        swapped = [swap(group) for group in tok_groups[:2]]
        near_units = [project(tok_groups[0], swapped[1]), project(tok_groups[1], swapped[0])]
        state = attend(near_units, state, False)
        last, first_state = tie(tok_groups[2], state[0])
        far_units = [project(last, swap(last))]
        units = near_units + far_units
        mixed_keep, mixed_send, lse = attend(far_units, (first_state, state[1]), True)
    else:
        units = [project(*pair) for pair in units_of(tok_groups + [swap(group) for group in tok_groups])]
        mixed_keep, mixed_send, lse = attend(units, state, True)
    mixed_recv = swap(mixed_send)

    middle_in = [
        tok_a,
        mixed_keep,
        mixed_recv,
        lse,
        w_out,
        w_out_oth,
        w_up,
        w_up_oth,
        w_down,
        w_down_oth,
        norm_gain,
        norm_bias,
    ]
    middle_shapes = [
        ((seqs, half, width), low),
        ((seqs, half, width), full),
        ((seqs, long_half, width), low),
        ((rows, units_local), low),
        ((rows, units_local), low),
        ((rows, units_local), low),
        ((rows, units_local), low),
        ((rows, width), low),
        ((rows, width), low),
        ((8, width), full),
    ]
    (
        out_half,
        d_resid,
        payload,
        active_own,
        active_oth,
        d_up_own,
        d_up_oth,
        d_ffn,
        normed_low,
        small,
    ) = pl.pallas_call(
        functools.partial(middle_kernel, min(512, units_local)),
        grid_spec=pltpu.PrefetchScalarGridSpec(
            num_scalar_prefetch=1,
            grid=(1,),
            in_specs=[whole(value.shape) for value in middle_in]
            + [pl.BlockSpec((seqs, half, width), lambda s, turn_ref: (0, turn_ref[0], 0))],
            out_specs=[whole(shape) for shape, _ in middle_shapes],
            scratch_shapes=[pltpu.VMEM((rows, 2 * units_local), full)],
        ),
        out_shape=[
            (jax.ShapeDtypeStruct if number == 2 else pltpu.HBM)(shape, kind)
            for number, (shape, kind) in enumerate(middle_shapes)
        ],
        compiler_params=room(36),
        cost_estimate=lasting(16),
        name="middle",
    )(turn_array, *middle_in, grad_out)

    order = slot_order(ctx_size)
    mirrored = [reversed_bits(slot, ctx_bits) for slot in order]
    owners = place ^ jnp.where(turn == 0, jnp.array(order, jnp.int32), jnp.array(mirrored, jnp.int32))
    quarter = width // ctx_size
    stages = [ctx_size >> (stage + 1) for stage in range(ctx_bits)] + [1]
    turned_kind = low if quarter % 16 == 0 else full
    chunk = min(768, units_local)

    def slot_scratch(count):
        return [pltpu.VMEM((width, count), turned_kind), pltpu.VMEM((ctx_size * padded(quarter), count), low)]

    def pair_grad(left_a, left_b, right_a, right_b, name):
        right_spec = pl.BlockSpec((rows, chunk), lambda n, *_: (0, n))
        return pl.pallas_call(
            pair_grad_kernel,
            grid_spec=pltpu.PrefetchScalarGridSpec(
                num_scalar_prefetch=1,
                grid=(units_local // chunk,),
                in_specs=[whole(left_a.shape), whole(left_b.shape), right_spec, right_spec],
                out_specs=[pl.BlockSpec((count, quarter, chunk), lambda n, *_: (0, 0, n)) for count in stages],
                scratch_shapes=slot_scratch(2 * rows),
            ),
            out_shape=[pltpu.HBM((count, quarter, units_local), low) for count in stages],
            compiler_params=room(16),
            cost_estimate=lasting(5.5),
            name=name,
        )(owners, *map(far, (left_a, left_b, right_a, right_b)))

    parity = row_place & 1

    def add_up(values):
        return sum(value.astype(full) for value in values)

    def send_stage(parts, gots, stage):
        count, start = parts[stage].shape[0], 0
        values = [parts[stage]]
        for got in gots:
            start = got.shape[0] - sum(part.shape[0] for part in parts[stage:])
            values.append(got[start : start + count])
        return add_up(values).astype(low)

    def own_half(parts, gots, which):
        values = [parts[-1]] + gots
        split = parts[-1].shape[1] // 2
        return add_up(
            [
                lax.dynamic_slice(value, (value.shape[0] - 1, which * split, 0), (1, split, value.shape[2]))
                for value in values
            ]
        )[0]

    class Blocks:
        def __init__(self, parts):
            self.parts, self.gots, self.stage, self.sent = list(parts), [], 0, None
            self.dp_stage, self.got = 0, None

        @property
        def arrived(self):
            return self.gots[-1] if self.dp_stage == 0 else self.got

        @arrived.setter
        def arrived(self, value):
            if self.dp_stage == 0:
                self.gots[-1] = value
            else:
                self.got = value

        def ready(self):
            if self.stage < ctx_bits:
                self.sent = send_stage(self.parts, self.gots, self.stage) if self.stage else self.parts[0]
            elif self.dp_stage == 0:
                self.sent = own_half(self.parts, self.gots, 1 - parity).astype(low)
            else:
                mine = own_half(self.parts, self.gots, parity) if self.dp_stage == 1 else self.sent.astype(full)
                self.sent = (mine + self.got.astype(full)).astype(low)

        def send(self):
            if self.stage < ctx_bits:
                self.gots.append(hop(self.sent, self.stage))
                self.stage += 1
                return
            last = self.dp_stage == dp_size.bit_length() - 1
            bit = 0 if last else self.dp_stage
            moves = [(spot, spot ^ (1 << bit)) for spot in range(dp_size)]
            self.got = lax.ppermute(self.sent, "dp", moves)
            self.dp_stage += 1

        def advance(self, *after):
            if self.gots:
                self.arrived = tie(self.arrived, *after)[0]
            elif after:
                self.parts[0] = tie(self.parts[0], *after)[0]
            self.ready()
            self.send()
            return self.sent

        def total(self):
            while self.dp_stage < dp_size.bit_length():
                self.advance()
            mine, other = self.sent, self.got
            return jnp.where(
                parity == 0, jnp.concatenate([mine, other], axis=0), jnp.concatenate([other, mine], axis=0)
            ).astype(full)

    grad_near = gather_near(payload)
    payload_b = swap(payload)
    d_ffn_b, active_b = swap(d_ffn), swap(active_oth)
    normed_b, d_up_b = swap(normed_low), swap(d_up_oth)
    down = Blocks(pair_grad(d_ffn, d_ffn_b, active_own, active_b, "grad_down"))
    latest = down.advance()
    normed_low, latest = tie(normed_low, latest)
    up = Blocks(pair_grad(normed_low, normed_b, d_up_own, d_up_b, "grad_up"))
    *grad_near, up.parts[0] = tie(*grad_near, up.parts[0])
    latest = up.advance()
    own_back, latest = tie(own, latest)
    grad_far = gather_far(payload, grad_near)
    crossed = [swap(group) for group in grad_far[:-1]]

    sum_shape = pltpu.HBM((seqs, span, local_width), full)
    row_shape = pltpu.HBM((seqs, span, local_width), low)
    grad_spec = seq_spec((long_half, width))
    span_spec = seq_spec((span, local_width))
    counts = [value.shape[1] for value in units]
    d_query, dk_sum, dv_sum = pl.pallas_call(
        functools.partial(query_grad_kernel, counts, heads),
        grid=(seqs,),
        in_specs=unit_specs([own]) + [grad_spec, grad_spec, whole(w_out.shape)] + unit_specs(units),
        out_specs=[span_spec] * 3,
        out_shape=[row_shape, sum_shape, sum_shape],
        scratch_shapes=[
            q_scratch,
            head_rows,
            pltpu.VMEM((16, span), full),
            head_square,
            head_square_low,
            head_square_low,
            pltpu.VMEM((local_width, span), full),
        ],
        compiler_params=room(20),
        cost_estimate=lasting(11),
        name="query_grad",
    )(own_back, payload, payload_b, far(w_out), *units)

    def sequence_grad(kernel, values, lefts, extra, columns, name):
        return Blocks(
            pl.pallas_call(
                kernel,
                grid_spec=pltpu.PrefetchScalarGridSpec(
                    num_scalar_prefetch=1,
                    grid=(1,),
                    in_specs=[whole(value.shape) for value in values],
                    out_specs=[whole((count, extra + quarter, columns)) for count in stages],
                    scratch_shapes=slot_scratch(seqs * span) * lefts,
                ),
                out_shape=[pltpu.HBM((count, extra + quarter, columns), low) for count in stages],
                compiler_params=room(20),
                cost_estimate=lasting(5.5),
                name=name,
            )(owners, *map(far, values))
        )

    small_rows = (small[:4] + swap(small)[:4]).reshape(4, ctx_size, quarter).transpose(1, 0, 2)
    small_rows = jnp.pad(small_rows, ((0, 0), (0, SMALL_ROWS - 4), (0, local_width - quarter)))
    latest = down.advance(d_query)
    d_query, latest = tie(d_query, latest)
    query_out = sequence_grad(
        query_out_grad_kernel,
        (tok_a, tok_b, d_query, payload, payload_b, mixed_keep, mixed_send, small_rows),
        2,
        SMALL_ROWS,
        2 * local_width,
        "query_out_grad",
    )
    grad_far[-1], query_out.parts[1] = tie(grad_far[-1], query_out.parts[1])
    crossed.append(swap(grad_far[-1]))
    latest = query_out.advance()
    latest = down.advance(latest)
    d_query, latest = tie(d_query, latest)
    grad_units = units_of(grad_far + crossed)
    grad_a, grad_b = [pair[0] for pair in grad_units], [pair[1] for pair in grad_units]
    d_kv, d_input = pl.pallas_call(
        functools.partial(key_grad_kernel, counts, heads),
        grid_spec=pltpu.PrefetchScalarGridSpec(
            num_scalar_prefetch=1,
            grid=(seqs,),
            in_specs=unit_specs([own])
            + [span_spec] * 3
            + [whole(w_out.shape), whole(w_qkv.shape)]
            + unit_specs(units + grad_a + grad_b),
            out_specs=[seq_spec((span, 2 * local_width)), seq_spec((span, width))],
            scratch_shapes=[
                pltpu.VMEM((heads // 2, span, 2 * LANES), low),
                head_rows,
                head_rows,
                head_square,
                head_square_low,
                head_square_low,
                pltpu.VMEM((span, local_width), full),
                pltpu.VMEM((span, local_width), full),
            ],
        ),
        out_shape=[
            jax.ShapeDtypeStruct((seqs, span, 2 * local_width), low),
            jax.ShapeDtypeStruct((seqs, span, width), low),
        ],
        compiler_params=room(26),
        cost_estimate=lasting(12.5),
        name="key_grad",
    )(turn_array, own, *map(far, (d_query, dk_sum, dv_sum, w_out, w_qkv, *units, *grad_a, *grad_b)))

    latest = up.advance(d_kv)
    latest = down.advance(latest)
    latest = query_out.advance(latest)
    d_kv, latest = tie(d_kv, latest)
    key_value = sequence_grad(key_value_grad_kernel, (tok_a, tok_b, d_kv), 1, 0, 2 * local_width, "key_value_grad")
    latest = key_value.advance()
    out_half, d_resid, d_input, latest = tie(out_half, d_resid, d_input, latest)
    swapped = [swap(out_half), swap(d_resid), swap(d_input)]
    for blocks in (up, down, key_value, query_out):
        latest = blocks.advance(latest)

    def both_halves(mine, other):
        return jnp.where(
            turn == 0, jnp.concatenate([mine, other], axis=1), jnp.concatenate([other, mine], axis=1)
        )

    *swapped, latest = tie(*swapped, latest)
    outputs = both_halves(out_half, swapped[0])
    grad_tokens = d_input.astype(full) + swapped[2].astype(full) + both_halves(d_resid, swapped[1])
    outputs, grad_tokens, latest = tie(outputs, grad_tokens, latest)
    for blocks in (up, key_value, query_out, up, key_value, query_out, key_value):
        latest = blocks.advance(latest)
    down_total, up_total = down.total(), up.total()
    query_out_total, key_value_total = query_out.total(), key_value.total()
    small_total = query_out_total[:4, local_width : local_width + quarter]
    query_out_total = query_out_total[SMALL_ROWS:]
    return (
        outputs,
        grad_tokens,
        jnp.stack(
            [query_out_total[:, :local_width], key_value_total[:, :local_width], key_value_total[:, local_width:]]
        ),
        query_out_total[:, local_width:].T,
        up_total.T,
        down_total.T,
        small_total[0:2],
        small_total[2:4],
    )


def solution(mesh):
    return jax.shard_map(
        functools.partial(on_device, mesh.shape["ctx"], mesh.shape["dp"]),
        mesh=mesh,
        in_specs=(
            P("dp", "ctx", None),
            P("dp", "ctx"),
            P(None, None, "tensor"),
            P("tensor", None),
            P("tensor", None),
            P("tensor", None),
            P(),
            P(),
            P("dp", "ctx", None),
        ),
        out_specs=(
            P("dp", "ctx", None),
            P("dp", "ctx", None),
            P(None, "ctx", "tensor"),
            P("tensor", "ctx"),
            P("tensor", "ctx"),
            P("tensor", "ctx"),
            P(None, "ctx"),
            P(None, "ctx"),
        ),
        check_vma=False,
    )
```
